768 devices in a mesh: region: 64 (over x, y, core), dom: 12 (over z).
Axes of the slice: x: 4, y: 8, z: 12, core: 2. Of those that a mesh axis runs over, the one named last changes fastest.
Arguments:
- water_state: float32 [3, 10, 393216], P(None, None, ('region', 'dom')), may hold values from -6 to 6
- water_depth: float32 [393216], P(('region', 'dom')), may hold values from 0.3 to 3
- metric: float32 [4, 393216], P(None, ('region', 'dom'))
- diff_ops: float32 [2, 10, 10], replicated, may hold values from -2 to 2
- stiff_ops: float32 [2, 10, 10], replicated, may hold values from -2 to 2
- trace_ops: float32 [3, 4, 10], replicated, may hold values from -2 to 2
- lift_ops: float32 [3, 10, 4], replicated, may hold values from -3 to 3
- cluster: int32 [393216], P(('region', 'dom')), may hold values from 0 to 1, as said below
- face_code: int32 [3, 393216], P(None, ('region', 'dom')), may hold values from 0 to 2304, as said below
- send_region: int32 [2, 196608], P(None, ('region', 'dom')), may hold values from 0 to 1535, as said below
- send_dom: int32 [2, 98304], P(None, ('region', 'dom')), may hold values from 0 to 1535, as said below
- move_dom: int32 [393216], P(('region', 'dom')), may hold values from 0 to 11, as said below
- move_slot: int32 [393216], P(('region', 'dom')), may hold values from 0 to 511, as said below
Outputs:
- new_state: float32 [3, 10, 393216], P(None, None, ('region', 'dom'))
The draws below stay inside these ranges and needn't reach their ends.
Inputs may be any that keep to these rules, and one draw needn't show every extreme that they name: Each device holds at most 128 triangles of cluster 0, some device exactly 128, the others 128 or 32. `face_code`: codes below 1536 name a face f * 512 + e of the own device; the next 768 codes name received slots, each named by exactly one face of the device; the largest code marks a wall, named by 64 faces of each device. `send_region`: each list names faces f * 512 + e of its own device, none twice; its first 8 slots hold faces of cluster-0 triangles, the others faces of cluster-1 triangles. `send_dom`: each list names faces f * 512 + e of its own device, none twice; its first 4 slots hold faces of cluster-0 triangles, the others faces of cluster-1 triangles. `move_dom`: with move_slot, a permutation of each region's triangles; every device hands exactly 32 triangles to each other dom index of its region and keeps the rest at their own positions. `move_slot`: see move_dom; staying triangles keep their position.
All inputs are finite; a program needn't handle non-finite values.
Results may differ from the reference program's by a relative error of at most 0.0003.
Values sent between devices are 32-bit elements; how exact they have to be, the bound alone decides.
A program may use at most 32 MiB of HBM per device.

```python
import math
import jax
import jax.numpy as jnp
from jax import lax

ELEMS = 512
NODES = 10
POINTS = 4
REG_SLOTS = 256
DOM_SLOTS = 128
REG_FINE = 8
DOM_FINE = 4
FINE_MAX = 128
MIGRANTS = 32
TOTAL = 393216
N_REGION = 64
N_DOM = 12
DEVICES = 768


def shuffled(subkey):
    return jax.random.permutation(subkey, ELEMS).astype(jnp.int32)


def shuffled_faces(subkey):
    return jax.random.permutation(subkey, 3 * ELEMS).astype(jnp.int32)


def fine_layout(key):
    base_key = jax.random.fold_in(key, 11)
    first_key, second_key, third_key = jax.random.split(base_key, 3)
    pick_count = jax.random.randint(first_key, (DEVICES,), 0, 3)
    busiest = jax.random.randint(second_key, (), 0, DEVICES)
    heavy = (pick_count == 0) | (jnp.arange(DEVICES) == busiest)
    counts = jnp.where(heavy, FINE_MAX, FINE_MAX // 4)
    orders = jax.vmap(shuffled)(jax.random.split(third_key, DEVICES))
    return jnp.where(orders < counts[:, None], 0, 1).astype(jnp.int32)


def send_lists(key, slot_count, fine_count, offset):
    face_kind = jnp.tile(fine_layout(key), (1, 3))
    column_ids = jnp.arange(3 * ELEMS, dtype=jnp.int32)[None, :]
    chosen = []
    for direction in range(2):
        sub_key = jax.random.fold_in(jax.random.fold_in(key, offset), direction)
        jitter = jax.random.randint(sub_key, (DEVICES, 3 * ELEMS), 0, 4096)
        distinct = jitter * (3 * ELEMS) + column_ids
        fine_first = jnp.argsort(face_kind * 1073741824 + distinct, axis=1, stable=True)[:, :fine_count]
        coarse_first = jnp.argsort((1 - face_kind) * 1073741824 + distinct, axis=1, stable=True)[:, :slot_count - fine_count]
        chosen.append(jnp.concatenate([fine_first, coarse_first], axis=1))
    return jnp.stack(chosen, 0).reshape(2, DEVICES * slot_count).astype(jnp.int32)


def migration_plan(key):
    base_key = jax.random.fold_in(key, 37)
    orders = jax.vmap(shuffled)(jax.random.split(base_key, DEVICES)).reshape(N_REGION, N_DOM, ELEMS)
    inverse = jnp.argsort(orders, axis=2, stable=True).astype(jnp.int32)
    movers = MIGRANTS * (N_DOM - 1)
    dom_ids = jnp.arange(N_DOM, dtype=jnp.int32)[None, :, None]
    region_ids = jnp.arange(N_REGION, dtype=jnp.int32)[:, None, None]
    moving = inverse < movers
    residue = inverse % (N_DOM - 1)
    within = inverse // (N_DOM - 1)
    target_dom = jnp.where(moving, (dom_ids + 1 + residue) % N_DOM, dom_ids)
    vacancy = jnp.clip(residue * MIGRANTS + within, 0, ELEMS - 1)
    arrival = orders[region_ids, target_dom, vacancy]
    own_slot = jnp.broadcast_to(jnp.arange(ELEMS, dtype=jnp.int32)[None, None, :], arrival.shape)
    target_slot = jnp.where(moving, arrival, own_slot)
    return (target_dom.reshape(-1).astype(jnp.int32), target_slot.reshape(-1).astype(jnp.int32))


def draw_metric(key, part):
    first_key, second_key = jax.random.split(jax.random.fold_in(key, 5))
    diagonal = jax.random.uniform(first_key, (2, TOTAL), jnp.float32, 0.3, 0.6)
    skew_part = jax.random.uniform(second_key, (2, TOTAL), jnp.float32, -0.12, 0.12)
    return jnp.stack([diagonal[0], skew_part[0], skew_part[1], diagonal[1]]).astype(jnp.float32)


def draw_cluster(key, part):
    return fine_layout(key).reshape(-1)


def draw_face_code(key, part):
    first_key, second_key = jax.random.split(jax.random.fold_in(key, 23))
    halo_count = 2 * REG_SLOTS + 2 * DOM_SLOTS
    walls = ELEMS // 8
    orders = jax.vmap(shuffled_faces)(jax.random.split(first_key, DEVICES))
    local_codes = jax.random.randint(second_key, (DEVICES, 3 * ELEMS), 0, 3 * ELEMS)
    codes = jnp.where(orders < halo_count, 3 * ELEMS + orders, jnp.where(orders < halo_count + walls, 3 * ELEMS + halo_count, local_codes))
    return codes.reshape(DEVICES, 3, ELEMS).transpose(1, 0, 2).reshape(3, TOTAL).astype(jnp.int32)


def draw_send_region(key, part):
    return send_lists(key, REG_SLOTS, REG_FINE, 51)


def draw_send_dom(key, part):
    return send_lists(key, DOM_SLOTS, DOM_FINE, 53)


def draw_move_dom(key, part):
    return migration_plan(key)[0]


def draw_move_slot(key, part):
    return migration_plan(key)[1]


def level_of(key, extent, cuts, smallest, high):
    factor_of, own = 1.0, jax.random.fold_in(key, 6)
    for axis_at, shards_of in cuts:
        draws = jnp.exp(jax.random.uniform(jax.random.fold_in(own, axis_at), (shards_of,), jnp.float32, smallest / len(cuts), high / len(cuts)))
        factor_of = factor_of * jnp.repeat(draws, extent[axis_at] // shards_of).reshape([-1 if axis == axis_at else 1 for axis in range(len(extent))])
    return factor_of


def centred(rng, extent, scale, bound, cuts=(), kind=jnp.bfloat16):
    factor_of = level_of(rng, extent, cuts, -0.22, 0.18) if cuts else 1.0
    values = jax.random.normal(rng, extent, jnp.float32) * scale * factor_of
    return jnp.minimum(jnp.maximum(values, -bound), bound).astype(kind)


def setup_inputs(seed: int = 0) -> dict:
    key_list = jax.random.split(jax.random.key(seed), 14)
    water_state = centred(key_list[0], (3, NODES, TOTAL), 1.0, 6.0, ((2, 768),), jnp.float32)
    water_depth = jnp.clip(jnp.exp(math.log(3.0) - 2.3025851 * jax.random.uniform(key_list[1], (TOTAL,), jnp.float32) ** level_of(key_list[1], (TOTAL,), ((0, 768),), -0.2, 0.2)), 0.3, 3.0)
    metric = draw_metric(jax.random.fold_in(key_list[13], 71), 0)
    diff_ops = centred(key_list[3], (2, NODES, NODES), NODES ** -0.5, 2.0, (), jnp.float32)
    stiff_ops = centred(key_list[4], (2, NODES, NODES), NODES ** -0.5, 2.0, (), jnp.float32)
    trace_ops = centred(key_list[5], (3, POINTS, NODES), NODES ** -0.5, 2.0, (), jnp.float32)
    lift_ops = centred(key_list[6], (3, NODES, POINTS), POINTS ** -0.5, 3.0, (), jnp.float32)
    cluster = draw_cluster(jax.random.fold_in(key_list[13], 71), 0)
    face_code = draw_face_code(jax.random.fold_in(key_list[13], 71), 0)
    send_region = draw_send_region(jax.random.fold_in(key_list[13], 71), 0)
    send_dom = draw_send_dom(jax.random.fold_in(key_list[13], 71), 0)
    move_dom = draw_move_dom(jax.random.fold_in(key_list[13], 71), 0)
    move_slot = draw_move_slot(jax.random.fold_in(key_list[13], 71), 0)
    return {"water_state": water_state, "water_depth": water_depth, "metric": metric, "diff_ops": diff_ops, "stiff_ops": stiff_ops, "trace_ops": trace_ops, "lift_ops": lift_ops, "cluster": cluster, "face_code": face_code, "send_region": send_region, "send_dom": send_dom, "move_dom": move_dom, "move_slot": move_slot}


HIGHEST = lax.Precision.HIGHEST
FIRST_HALF = (0.5, 0.125, 1.0 / 48.0, 1.0 / 384.0)
SECOND_HALF = (0.5, 0.375, 7.0 / 48.0, 15.0 / 384.0)

def spatial(values, water_depth, metric, diff_ops):
    slopes = jnp.einsum('aij,vjn->avin', diff_ops, values, precision=HIGHEST)
    along_x = metric[0] * slopes[0] + metric[1] * slopes[1]
    along_y = metric[2] * slopes[0] + metric[3] * slopes[1]
    return -jnp.stack([along_x[1] + along_y[2], water_depth * along_x[0], water_depth * along_y[0]])

def predictor(values, water_depth, metric, diff_ops):
    series = [values]
    for degree in range(3):
        series.append(spatial(series[-1], water_depth, metric, diff_ops))
    return series

def integrate(series, factors):
    summed = factors[0] * series[0]
    for factor, member in zip(factors[1:], series[1:]):
        summed = summed + factor * member
    return summed

def face_table(values, trace_ops):
    return jnp.einsum('fqj,vjn->vqfn', trace_ops, values, precision=HIGHEST)

def normal_flux(traces, normal_x, normal_y, water_depth):
    return jnp.stack([traces[1] * normal_x + traces[2] * normal_y, water_depth * traces[0] * normal_x, water_depth * traces[0] * normal_y])

def increment(values, inside, beyond, is_wall, water_depth, metric, stiff_ops, lift_ops):
    flipped = beyond[:, ::-1]
    mirror = jnp.stack([inside[0], -inside[1], -inside[2]])
    outside = jnp.where(is_wall, mirror, flipped)
    normal_x = 2.0 * jnp.stack([-metric[1], metric[0] + metric[1], -metric[0]])
    normal_y = 2.0 * jnp.stack([-metric[3], metric[2] + metric[3], -metric[2]])
    wave_speed = jnp.sqrt(water_depth) * jnp.sqrt(normal_x * normal_x + normal_y * normal_y)
    fluxes = 0.5 * (normal_flux(inside, normal_x, normal_y, water_depth) + normal_flux(outside, normal_x, normal_y, water_depth)) - 0.5 * wave_speed * (outside - inside)
    lifted = jnp.einsum('fjq,vqfn->vjn', lift_ops, fluxes, precision=HIGHEST)
    weak_slopes = jnp.einsum('aij,vjn->avin', stiff_ops, values, precision=HIGHEST)
    weak_x = metric[0] * weak_slopes[0] + metric[1] * weak_slopes[1]
    weak_y = metric[2] * weak_slopes[0] + metric[3] * weak_slopes[1]
    volume = jnp.stack([weak_x[1] + weak_y[2], water_depth * weak_x[0], water_depth * weak_y[0]])
    return volume - lifted

def device_block(array, block, width):
    return lax.dynamic_slice_in_dim(array, (block * width).astype(jnp.int32), width, array.ndim - 1)

def received(region_pay, dom_pay, block):
    region_index = block // N_DOM
    dom_index = block % N_DOM
    from_below = jnp.where(region_index > 0, region_pay[jnp.maximum(block - N_DOM, 0), :, 1], 0.0)
    from_above = jnp.where(region_index < N_REGION - 1, region_pay[jnp.minimum(block + N_DOM, DEVICES - 1), :, 0], 0.0)
    dom_lower = jnp.where(dom_index > 0, dom_pay[jnp.maximum(block - 1, 0), :, 1], 0.0)
    dom_upper = jnp.where(dom_index < N_DOM - 1, dom_pay[jnp.minimum(block + 1, DEVICES - 1), :, 0], 0.0)
    return jnp.concatenate([from_below, from_above, dom_lower, dom_upper], axis=1)

def reference(water_state, water_depth, metric, diff_ops, stiff_ops, trace_ops, lift_ops, cluster, face_code, send_region, send_dom, move_dom, move_slot):
    rows = 3 * POINTS
    wall_code = 3 * ELEMS + 2 * REG_SLOTS + 2 * DOM_SLOTS

    def pieces(block):
        values = device_block(water_state, block, ELEMS)
        depth_here = device_block(water_depth, block, ELEMS)
        metric_here = device_block(metric, block, ELEMS)
        codes_here = device_block(face_code, block, ELEMS)
        return (values, depth_here, metric_here, codes_here)

    def outer_of(table, region_pay, dom_pay, block, codes_here):
        extended = jnp.concatenate([table, received(region_pay, dom_pay, block), jnp.zeros((rows, 1), table.dtype)], axis=1)
        return jnp.take(extended, codes_here.reshape(-1), axis=1).reshape(3, POINTS, 3, ELEMS)

    def opening(block):
        values, depth_here, metric_here, codes_here = pieces(block)
        early = integrate(predictor(values, depth_here, metric_here, diff_ops), FIRST_HALF)
        table = face_table(early, trace_ops).reshape(rows, 3 * ELEMS)
        return (jnp.take(table, device_block(send_region, block, REG_SLOTS), axis=1), jnp.take(table, device_block(send_dom, block, DOM_SLOTS), axis=1))
    blocks = jnp.arange(DEVICES, dtype=jnp.int32)
    region_first, dom_first = lax.map(opening, blocks)

    def middle(block):
        values, depth_here, metric_here, codes_here = pieces(block)
        series = predictor(values, depth_here, metric_here, diff_ops)
        early = integrate(series, FIRST_HALF)
        late = integrate(series, SECOND_HALF)
        inside = face_table(early, trace_ops)
        beyond = outer_of(inside.reshape(rows, 3 * ELEMS), region_first, dom_first, block, codes_here)
        is_wall = codes_here == wall_code
        midway = values + increment(early, inside, beyond, is_wall, depth_here, metric_here, stiff_ops, lift_ops)
        fine_part = integrate(predictor(midway, depth_here, metric_here, diff_ops), FIRST_HALF)
        second = jnp.where(device_block(cluster, block, ELEMS) == 0, fine_part, late)
        table = face_table(second, trace_ops).reshape(rows, 3 * ELEMS)
        return (midway, second, jnp.take(table, device_block(send_region, block, REG_SLOTS), axis=1), jnp.take(table, device_block(send_dom, block, DOM_SLOTS), axis=1))
    midways, seconds, region_second, dom_second = lax.map(middle, blocks)

    def closing(block):
        values, depth_here, metric_here, codes_here = pieces(block)
        second = seconds[block]
        inside = face_table(second, trace_ops)
        beyond = outer_of(inside.reshape(rows, 3 * ELEMS), region_second, dom_second, block, codes_here)
        is_wall = codes_here == wall_code
        return midways[block] + increment(second, inside, beyond, is_wall, depth_here, metric_here, stiff_ops, lift_ops)
    finals = lax.map(closing, blocks)
    stepped = jnp.moveaxis(finals, 0, 2).reshape(3, NODES, TOTAL)
    owner_region = jnp.arange(TOTAL, dtype=jnp.int32) // (ELEMS * N_DOM)
    target = ((owner_region * N_DOM + move_dom) * ELEMS + move_slot).astype(jnp.int32)
    return jnp.zeros_like(stepped).at[:, :, target].set(stepped)
```

```python
import jax
import jax.numpy as jnp
from jax import lax
from jax.experimental import pallas as pl
from jax.experimental.pallas import tpu as pltpu
from jax.sharding import PartitionSpec as P

MESH = pl.DeviceIdType.MESH
HIGHEST = lax.Precision.HIGHEST
F32 = jnp.float32
BF16 = jnp.bfloat16
NODES = 10
FIRST_HALF = (0.5, 0.125, 1.0 / 48.0, 1.0 / 384.0)
SECOND_HALF = (0.5, 0.375, 7.0 / 48.0, 15.0 / 384.0)
MIGRANTS = 32
REG_FINE = 8
DOM_FINE = 4


def iota(shape, dim):
    return lax.broadcasted_iota(jnp.int32, shape, dim)


def ones_where(mask):
    return jnp.where(mask, 1.0, 0.0).astype(F32)


def dot(a, b):
    return jnp.dot(a, b, preferred_element_type=F32)


def exact(a, b):
    return jnp.dot(a, b, preferred_element_type=F32, precision=HIGHEST)


def dot_nt(a, b, precision=None):
    return lax.dot_general(
        a, b, (((1,), (1,)), ((), ())), preferred_element_type=F32, precision=precision
    )


def split_state(values):
    hi = values.astype(BF16)
    lo = (values - hi.astype(F32)).astype(BF16)
    return jnp.concatenate([hi, lo, hi], axis=0)


def split_matrix(wide, low_from):
    hi = wide.astype(BF16).astype(F32)
    lo = wide - hi
    return jnp.where(iota(wide.shape, 1) >= low_from, lo, hi).astype(BF16)


def var_of(row):
    return (row >= NODES).astype(jnp.int32) + (row >= 2 * NODES).astype(jnp.int32)


def state_columns(count):
    column = iota((NODES, count), 1) & 31
    node = column - NODES * var_of(column)
    return ones_where((node == iota((NODES, count), 0)) & (column < 3 * NODES))


def slope_matrix(ops_ref, sign):
    rows, cols = 96, 96
    row = iota((rows, NODES), 0)
    local = jnp.where(row < 64, row & 31, row & 15)
    node = local - NODES * var_of(local)
    second = ((row >= 32) & (row < 64)) | (row >= 80)
    valid = local < jnp.where(row < 64, 3 * NODES, NODES)
    hit = (node == iota((rows, NODES), 1)) & valid
    picked = exact(ones_where(hit & ~second), ops_ref[:, 0, :]) + exact(
        ones_where(hit & second), ops_ref[:, 1, :]
    )
    wide = exact(picked, state_columns(cols)) * sign
    row = iota((rows, cols), 0)
    local = row & 31
    source = jnp.where(row < 64, (local < NODES).astype(jnp.int32), 2)
    column = iota((rows, cols), 1) & 31
    wide = jnp.where(source == var_of(column), wide, 0.0)
    return split_matrix(wide, 64)


def trace_matrix(trace_ref):
    rows, cols = 96, 96
    row = iota((rows, 4), 0)
    point = row & 3
    point = jnp.where(row < 48, 3 - point, point)
    face = (row >> 4) - jnp.where(row < 48, 0, 3)
    picked = jnp.zeros((rows, NODES), F32)
    for f in range(3):
        pick = ones_where((point == iota((rows, 4), 1)) & (face == f))
        picked = picked + exact(pick, trace_ref[f])
    wide = exact(picked, state_columns(cols))
    part = (iota((rows, cols), 0) >> 2) & 3
    source = jnp.where(part == 3, 0, part)
    column = iota((rows, cols), 1) & 31
    wide = jnp.where(source == var_of(column), wide, 0.0)
    return split_matrix(wide, 64)


def lift_matrix(lift_ref):
    rows, cols = 32, 288
    row = iota((rows, NODES), 0)
    node = row - NODES * var_of(row)
    pick = ones_where((node == iota((rows, NODES), 1)) & (row < 3 * NODES))
    wide = jnp.zeros((rows, cols), F32)
    column = iota((4, cols), 1)
    third = column - 96 * ((column >= 96).astype(jnp.int32) + (column >= 192).astype(jnp.int32))
    for f in range(3):
        points = dot_nt(pick, lift_ref[f], HIGHEST)
        place = ones_where(((third >> 5) == f) & ((third & 3) == iota((4, cols), 0)))
        wide = wide + exact(points, place)
    column = iota((rows, cols), 1)
    third = column - 96 * ((column >= 96).astype(jnp.int32) + (column >= 192).astype(jnp.int32))
    jump = (third & 16) != 0
    part = (third >> 2) & 3
    var = var_of(iota((rows, cols), 0))
    centre = (
        ((var == 0) & ((part == 1) | (part == 2)))
        | ((var == 1) & (part == 0))
        | ((var == 2) & (part == 3))
    )
    factor = jnp.where(jump, ones_where(part == var), -ones_where(centre))
    return split_matrix(wide * factor, 192)


def combine(slopes, alpha):
    a1, a2, a3, a4 = alpha
    both = a1 * slopes[0:32] + a2 * slopes[32:64]
    top = a3 * slopes[64:80] + a4 * slopes[80:96]
    return jnp.concatenate([both[0:16] + top, both[16:32]], axis=0)


def pick_columns(load, sources, block, lane, start):
    out = start
    for k in sources:
        found = jnp.take_along_axis(load(k), lane, axis=1)
        out = jnp.where(block == k, found, out)
    return out


def step_kernel(
    n_region,
    n_dom,
    elems,
    state_ref,
    depth_ref,
    metric_ref,
    diff_ref,
    stiff_ref,
    trace_ref,
    lift_ref,
    cluster_ref,
    code_ref,
    send_reg_ref,
    send_dom_ref,
    move_dom_ref,
    move_slot_ref,
    out_ref,
    dense,
    tab_a,
    tab_b,
    tab_c,
    beyond,
    out_reg,
    out_dom,
    in_reg,
    in_dom,
    out_fine,
    in_fine,
    land_out,
    land_in,
    tile_out,
    tile_in,
    ss_reg,
    rs_reg,
    ss_dom,
    rs_dom,
    ss_fine,
    rs_fine,
    ss_land,
    rs_land,
    ss_tile,
    rs_tile,
):
    r = lax.axis_index("region")
    d = lax.axis_index("dom")
    blocks = elems // 128
    has_low = r > 0
    has_high = r < n_region - 1
    dom_low = d > 0
    dom_high = d < n_dom - 1
    sides = (
        (has_high, {"region": r + 1}, 1, 0),
        (has_low, {"region": r - 1}, 0, 1),
        (dom_high, {"dom": d + 1}, 1, 0),
        (dom_low, {"dom": d - 1}, 0, 1),
    )
    comes = (has_low, has_high, dom_low, dom_high)

    barrier = pltpu.get_barrier_semaphore()
    for exists, device, _, _ in sides[:2]:

        @pl.when(exists)
        def _():
            pl.semaphore_signal(barrier, inc=1, device_id=device, device_id_type=MESH)

    for k in range(1, n_dom):
        pl.semaphore_signal(
            barrier, inc=1, device_id={"dom": lax.rem(d + k, n_dom)}, device_id_type=MESH
        )

    dense[30:32, :] = jnp.zeros((2, elems), F32)
    for v in range(3):
        dense[NODES * v : NODES * (v + 1), :] = state_ref[:, v, :]
    state = dense[...]
    depth = depth_ref[...]
    m0, m1, m2, m3 = (metric_ref[i : i + 1, :] for i in range(4))

    row = iota((32, elems), 0)
    a1 = jnp.where(row < 10, m0, jnp.where(row < 20, depth * m0, depth * m2))
    a2 = jnp.where(row < 10, m1, jnp.where(row < 20, depth * m1, depth * m3))
    top = row[0:16] < 10
    a3 = jnp.where(top, m2, 0.0)
    a4 = jnp.where(top, m3, 0.0)
    alpha = (a1, a2, a3, a4)

    slope = slope_matrix(diff_ref, -1.0)
    traces = trace_matrix(trace_ref)

    def series_of(values):
        series = [values]
        for _ in range(3):
            series.append(combine(dot(slope, split_state(series[-1])), alpha))
        return series

    def integrate(series, factors):
        summed = factors[0] * series[0]
        for factor, member in zip(factors[1:], series[1:]):
            summed = summed + factor * member
        return summed

    series = series_of(state)
    early = integrate(series, FIRST_HALF)
    later = integrate(series, SECOND_HALF)
    early_split = split_state(early)
    tab_a[...] = dot(traces, early_split)
    tab_b[...] = dot(traces[0:48], split_state(later))

    def source(table):
        def load(k):
            f, b = divmod(k, blocks)
            return table[16 * f : 16 * f + 16, 128 * b : 128 * b + 128]

        return load

    def spread(vector):
        return jnp.broadcast_to(vector, (16, 128))

    own = range(3 * blocks)
    for which, table in enumerate((tab_a, tab_b)):
        for lane_row in range(2):
            for b in range(2):
                index = spread(send_reg_ref[lane_row : lane_row + 1, 128 * b : 128 * b + 128])
                out_reg[which, lane_row, b] = pick_columns(
                    source(table), own, index >> 7, index & 127, jnp.zeros((16, 128), F32)
                )
            index = spread(send_dom_ref[lane_row : lane_row + 1, :])
            out_dom[which, lane_row] = pick_columns(
                source(table), own, index >> 7, index & 127, jnp.zeros((16, 128), F32)
            )

    lanes = iota((1, elems), 1)
    offset = move_dom_ref[...] - d
    offset = jnp.where(offset < 0, offset + n_dom, offset)
    chosen = jnp.where(iota((16, elems), 0) == offset, 1.0, 0.0)
    before = jnp.where(iota((elems, elems), 0) < iota((elems, elems), 1), 1.0, 0.0).astype(BF16)
    rank = jnp.sum(chosen * dot(chosen.astype(BF16), before), axis=0, keepdims=True)
    slots = n_dom * MIGRANTS
    padded = 384 if slots <= 384 else 128 * (-(-slots // 128))
    position = jnp.where(offset == 0, -1, offset * MIGRANTS + rank.astype(jnp.int32))
    inverse = jnp.where(iota((padded, elems), 0) == position, 1.0, 0.0).astype(BF16)
    place = move_slot_ref[...]
    which_row = iota((8, elems), 0)
    facts = jnp.where(
        which_row == 0,
        lanes >> 1,
        jnp.where(
            which_row == 1, lanes & 1, jnp.where(which_row == 2, place >> 1, place & 1)
        ),
    )
    facts = jnp.where(which_row < 4, facts, 0).astype(F32).astype(BF16)
    found = dot_nt(facts, inverse).astype(jnp.int32)
    leaves = found[0:1] * 2 + found[1:2]
    lands = found[2:3] * 2 + found[3:4]
    for k in range(1, n_dom):
        land_out[k] = lands[:, 128 * (k // 4) : 128 * (k // 4) + 128]

    for i in range(2):

        @pl.when(jnp.logical_not(comes[i]))
        def _():
            in_reg[:, i] = jnp.zeros(in_reg.shape[0:1] + in_reg.shape[2:], F32)

        @pl.when(jnp.logical_not(comes[2 + i]))
        def _():
            in_dom[:, i] = jnp.zeros(in_dom.shape[0:1] + in_dom.shape[2:], F32)

    for i in range(4):

        @pl.when(jnp.logical_not(comes[i]))
        def _():
            in_fine[i] = jnp.zeros((16, 128), F32)

    pl.semaphore_wait(
        barrier, (n_dom - 1) + has_low.astype(jnp.int32) + has_high.astype(jnp.int32)
    )

    def copies_a(which):
        copies = []
        for i, (exists, device, lane_row, at) in enumerate(sides):
            regional = i < 2
            copies.append(
                (
                    exists,
                    comes[2 * (i // 2) + at],
                    pltpu.make_async_remote_copy(
                        src_ref=(out_reg if regional else out_dom).at[which, lane_row],
                        dst_ref=(in_reg if regional else in_dom).at[which, at],
                        send_sem=(ss_reg if regional else ss_dom).at[which, at],
                        recv_sem=(rs_reg if regional else rs_dom).at[which, at],
                        device_id=device,
                        device_id_type=MESH,
                    ),
                )
            )
        return copies

    def start(copies):
        for exists, _, copy in copies:
            pl.when(exists)(copy.start)

    def wait_recv(copies):
        for _, arrives, copy in copies:
            pl.when(arrives)(copy.wait_recv)

    def wait_send(copies):
        for exists, _, copy in copies:
            pl.when(exists)(copy.wait_send)

    first_copies = copies_a(0)
    late_copies = copies_a(1)
    start(first_copies)
    start(late_copies)

    def peer_copies(src, dst, ss, rs):
        return {
            k: pltpu.make_async_remote_copy(
                src_ref=src.at[k],
                dst_ref=dst.at[k],
                send_sem=ss.at[k],
                recv_sem=rs.at[k],
                device_id={"dom": lax.rem(d + k, n_dom)},
                device_id_type=MESH,
            )
            for k in range(1, n_dom)
        }

    nearest = sorted(range(1, n_dom), key=lambda k: min(k, n_dom - k))
    land_copies = peer_copies(land_out, land_in, ss_land, rs_land)
    for k in nearest[::-1]:
        land_copies[k].start()

    stiff = slope_matrix(stiff_ref, 1.0)
    lift = lift_matrix(lift_ref)
    half_x = (-m1, m0 + m1, -m0)
    half_y = (-m3, m2 + m3, -m2)
    root = jnp.sqrt(depth)
    rows16 = iota((16, elems), 0)
    centre_by, jump_by = [], []
    for f in range(3):
        hx, hy = half_x[f], half_y[f]
        centre_by.append(
            jnp.where(
                rows16 < 4,
                depth * hx,
                jnp.where(rows16 < 8, hx, jnp.where(rows16 < 12, hy, depth * hy)),
            )
        )
        jump_by.append(root * jnp.sqrt(hx * hx + hy * hy))
    mirror = jnp.where((iota((16, 128), 0) >= 4) & (iota((16, 128), 0) < 12), -1.0, 1.0)
    first_code = 3 * elems
    regional = 2 * send_reg_ref.shape[1]

    def code_of(f, b):
        return spread(code_ref[f : f + 1, 128 * b : 128 * b + 128])

    def local_part(table):
        for f in range(3):
            for b in range(blocks):
                code = code_of(f, b)
                wall = mirror * table[48 + 16 * f : 64 + 16 * f, 128 * b : 128 * b + 128]
                beyond[f, b] = pick_columns(source(table), own, code >> 7, code & 127, wall)

    def remote_part(which, fine):
        def load(k):
            k = k - 3 * blocks
            if k < 4:
                return in_reg[which, k // 2, k % 2]
            return in_dom[which, k - 4]

        for f in range(3):
            for b in range(blocks):
                code = code_of(f, b)
                beyond[f, b] = pick_columns(
                    load,
                    range(3 * blocks, 3 * blocks + 6),
                    code >> 7,
                    code & 127,
                    beyond[f, b],
                )

    def fine_column(code):
        slot = code - first_code
        reg = slot & 255
        from_reg = jnp.where(
            (slot >= 0) & (slot < regional) & (reg < REG_FINE), (slot >> 8) * REG_FINE + reg, -1
        )
        past = slot - regional
        dom = past & 127
        return jnp.where(
            (past >= 0) & (past < 256) & (dom < DOM_FINE),
            2 * REG_FINE + (past >> 7) * DOM_FINE + dom,
            from_reg,
        )

    def increment(values_split, table):
        volume = combine(dot(stiff, values_split), alpha)
        parts = []
        for f in range(3):
            outside = jnp.concatenate([beyond[f, b] for b in range(blocks)], axis=1)
            inside = table[48 + 16 * f : 64 + 16 * f, :]
            parts.append(centre_by[f] * (outside + inside))
            parts.append(jump_by[f] * (outside - inside))
        return volume + dot(lift, split_state(jnp.concatenate(parts, axis=0)))

    local_part(tab_a)
    wait_recv(first_copies)
    remote_part(0, False)
    midway = state + increment(early_split, tab_a)
    fine = integrate(series_of(midway), FIRST_HALF)
    second = jnp.where(cluster_ref[...] == 0, fine, later)
    second_split = split_state(second)
    tab_c[...] = dot(traces, second_split)

    lane = iota((1, 128), 1)
    wanted = jnp.where(
        lane < REG_FINE,
        send_reg_ref[1:2, 0:128],
        jnp.where(
            lane < 2 * REG_FINE,
            pltpu.roll(send_reg_ref[0:1, 0:128], REG_FINE, 1),
            jnp.where(
                lane < 2 * REG_FINE + DOM_FINE,
                pltpu.roll(send_dom_ref[1:2, :], 2 * REG_FINE, 1),
                pltpu.roll(send_dom_ref[0:1, :], 2 * REG_FINE + DOM_FINE, 1),
            ),
        ),
    )
    wanted = spread(wanted)
    out_fine[...] = pick_columns(
        source(tab_c), own, wanted >> 7, wanted & 127, jnp.zeros((16, 128), F32)
    )
    fine_copies = []
    for i, (exists, device, _, at) in enumerate(sides):
        fine_copies.append(
            (
                exists,
                comes[2 * (i // 2) + at],
                pltpu.make_async_remote_copy(
                    src_ref=out_fine,
                    dst_ref=in_fine.at[i],
                    send_sem=ss_fine.at[i],
                    recv_sem=rs_fine.at[i],
                    device_id=device,
                    device_id_type=MESH,
                ),
            )
        )
    start(fine_copies)

    local_part(tab_c)
    wait_recv(late_copies)
    remote_part(1, True)
    for k in range(1, n_dom):
        land_copies[k].wait_recv()
    kk = iota((1, 128), 1)
    stack = []
    for q in range(padded // 128):
        row_q = jnp.full((1, 128), -1, jnp.int32)
        for k in range(4 * q, min(4 * q + 4, n_dom)):
            if k > 0:
                row_q = jnp.where((kk >> 5) == (k & 3), land_in[k], row_q)
        stack.append(row_q)
    places = jnp.concatenate(stack, axis=1)
    comes_here = jnp.where(iota((elems, padded), 0) == places, 1.0, 0.0).astype(BF16)
    column = iota((8, padded), 1)
    row8 = iota((8, padded), 0)
    facts = jnp.where(row8 == 0, column >> 1, jnp.where(row8 == 1, column & 1, 1))
    found = dot_nt(facts.astype(F32).astype(BF16), comes_here).astype(jnp.int32)
    origin = jnp.where(found[2:3] > 0, found[0:1] * 2 + found[1:2], -1)

    wait_recv(fine_copies)
    lane16 = iota((16, 128), 1)
    fresh = jnp.where(
        lane16 < REG_FINE,
        in_fine[0],
        jnp.where(
            lane16 < 2 * REG_FINE,
            in_fine[1],
            jnp.where(lane16 < 2 * REG_FINE + DOM_FINE, in_fine[2], in_fine[3]),
        ),
    )
    for f in range(3):
        for b in range(blocks):
            column = fine_column(code_of(f, b))
            found = jnp.take_along_axis(fresh, column & 127, axis=1)
            beyond[f, b] = jnp.where(column >= 0, found, beyond[f, b])
    dense[...] = midway + increment(second_split, tab_c)

    def cell(g, b):
        return dense[8 * g : 8 * g + 8, 128 * b : 128 * b + 128]

    group = iota((8, 128), 1) >> 5
    tile_copies = peer_copies(tile_out, tile_in, ss_tile, rs_tile)
    packed = {}
    for q in range(padded // 128):
        index = jnp.broadcast_to(leaves[:, 128 * q : 128 * q + 128], (8, 128))
        for g in range(4):
            packed[g, q] = pick_columns(
                lambda b: cell(g, b), range(blocks), index >> 7, index & 127, jnp.zeros((8, 128), F32)
            )
    for k in nearest[::-1]:
        tile = jnp.zeros((8, 128), F32)
        for g in range(4):
            shift = (32 * (g - (k & 3))) % 128
            moved = packed[g, k // 4]
            if shift:
                moved = pltpu.roll(moved, shift, 1)
            tile = jnp.where(group == g, moved, tile)
        tile_out[k] = tile
        tile_copies[k].start()

    result = {(g, b): cell(g, b) for g in range(4) for b in range(blocks)}
    for k in nearest:
        tile_copies[k].wait_recv()
        tile = tile_in[k]
        for b in range(blocks):
            index = jnp.broadcast_to(origin[:, 128 * b : 128 * b + 128], (8, 128))
            here = (index >> 5) == k
            for g in range(4):
                found = jnp.take_along_axis(tile, (index & 31) + 32 * g, axis=1)
                result[g, b] = jnp.where(here, found, result[g, b])
    for g in range(4):
        for b in range(blocks):
            dense[8 * g : 8 * g + 8, 128 * b : 128 * b + 128] = result[g, b]
    for v in range(3):
        out_ref[:, v, :] = dense[NODES * v : NODES * (v + 1), :]

    wait_send(first_copies)
    wait_send(late_copies)
    wait_send(fine_copies)
    for k in range(1, n_dom):
        land_copies[k].wait_send()
        tile_copies[k].wait_send()


def shards(n_region, n_dom, *args):
    (
        water_state,
        water_depth,
        metric,
        diff_ops,
        stiff_ops,
        trace_ops,
        lift_ops,
        cluster,
        face_code,
        send_region,
        send_dom,
        move_dom,
        move_slot,
    ) = args
    elems = water_state.shape[2]
    blocks = elems // 128
    vmem = pl.BlockSpec(memory_space=pltpu.VMEM)
    dma = pltpu.SemaphoreType.DMA

    def kernel(*refs):
        step_kernel(n_region, n_dom, elems, *refs)

    result = pl.pallas_call(
        kernel,
        out_shape=jax.ShapeDtypeStruct((NODES, 3, elems), F32),
        in_specs=[vmem] * 13,
        out_specs=vmem,
        scratch_shapes=[
            pltpu.VMEM((32, elems), F32),
            pltpu.VMEM((96, elems), F32),
            pltpu.VMEM((48, elems), F32),
            pltpu.VMEM((96, elems), F32),
            pltpu.VMEM((3, blocks, 16, 128), F32),
            pltpu.VMEM((2, 2, 2, 16, 128), F32),
            pltpu.VMEM((2, 2, 16, 128), F32),
            pltpu.VMEM((2, 2, 2, 16, 128), F32),
            pltpu.VMEM((2, 2, 16, 128), F32),
            pltpu.VMEM((16, 128), F32),
            pltpu.VMEM((4, 16, 128), F32),
            pltpu.VMEM((n_dom, 1, 128), jnp.int32),
            pltpu.VMEM((n_dom, 1, 128), jnp.int32),
            pltpu.VMEM((n_dom, 8, 128), F32),
            pltpu.VMEM((n_dom, 8, 128), F32),
            dma((2, 2)),
            dma((2, 2)),
            dma((2, 2)),
            dma((2, 2)),
            dma((4,)),
            dma((4,)),
            dma((n_dom,)),
            dma((n_dom,)),
            dma((n_dom,)),
            dma((n_dom,)),
        ],
        compiler_params=pltpu.CompilerParams(collective_id=0, has_side_effects=True),
        name="wave_step",
    )(
        jnp.transpose(water_state, (1, 0, 2)),
        water_depth.reshape(1, elems),
        metric,
        jnp.transpose(diff_ops, (1, 0, 2)),
        jnp.transpose(stiff_ops, (1, 0, 2)),
        trace_ops,
        jnp.transpose(lift_ops, (0, 2, 1)),
        cluster.reshape(1, elems),
        face_code,
        send_region,
        send_dom,
        move_dom.reshape(1, elems),
        move_slot.reshape(1, elems),
    )
    return jnp.transpose(result, (1, 0, 2))


def solution(mesh):
    both = ("region", "dom")
    wide, flat = P(None, both), P(both)
    placed = (
        P(None, None, both),
        flat,
        wide,
        P(),
        P(),
        P(),
        P(),
        flat,
        wide,
        wide,
        wide,
        flat,
        flat,
    )
    n_region, n_dom = mesh.shape["region"], mesh.shape["dom"]

    def step(*args):
        return shards(n_region, n_dom, *args)

    return jax.shard_map(
        step,
        mesh=mesh,
        in_specs=placed,
        out_specs=P(None, None, both),
        check_vma=False,
    )
```

```python
import jax
import jax.numpy as jnp
from jax import lax
from jax.experimental import pallas as pl
from jax.experimental.pallas import tpu as pltpu
from jax.sharding import PartitionSpec as P

MESH = pl.DeviceIdType.MESH
HIGHEST = lax.Precision.HIGHEST
F32 = jnp.float32
BF16 = jnp.bfloat16
NODES = 10
FIRST_HALF = (0.5, 0.125, 1.0 / 48.0, 1.0 / 384.0)
SECOND_HALF = (0.5, 0.375, 7.0 / 48.0, 15.0 / 384.0)
MIGRANTS = 32
REG_FINE = 8
DOM_FINE = 4


def iota(shape, dim):
    return lax.broadcasted_iota(jnp.int32, shape, dim)


def ones_where(mask):
    return jnp.where(mask, 1.0, 0.0).astype(F32)


def dot(a, b):
    return jnp.dot(a, b, preferred_element_type=F32)


def exact(a, b):
    return jnp.dot(a, b, preferred_element_type=F32, precision=HIGHEST)


def dot_nt(a, b, precision=None):
    return lax.dot_general(
        a, b, (((1,), (1,)), ((), ())), preferred_element_type=F32, precision=precision
    )


def split_state(values):
    hi = values.astype(BF16)
    lo = (values - hi.astype(F32)).astype(BF16)
    return jnp.concatenate([hi, lo, hi], axis=0)


def split_matrix(wide, low_from):
    hi = wide.astype(BF16).astype(F32)
    lo = wide - hi
    return jnp.where(iota(wide.shape, 1) >= low_from, lo, hi).astype(BF16)


def var_of(row):
    return (row >= NODES).astype(jnp.int32) + (row >= 2 * NODES).astype(jnp.int32)


def state_columns(count):
    column = iota((NODES, count), 1) & 31
    node = column - NODES * var_of(column)
    return ones_where((node == iota((NODES, count), 0)) & (column < 3 * NODES))


def slope_matrix(ops_ref, sign):
    rows, cols = 96, 96
    row = iota((rows, NODES), 0)
    local = jnp.where(row < 64, row & 31, row & 15)
    node = local - NODES * var_of(local)
    second = ((row >= 32) & (row < 64)) | (row >= 80)
    valid = local < jnp.where(row < 64, 3 * NODES, NODES)
    hit = (node == iota((rows, NODES), 1)) & valid
    picked = exact(ones_where(hit & ~second), ops_ref[:, 0, :]) + exact(
        ones_where(hit & second), ops_ref[:, 1, :]
    )
    wide = exact(picked, state_columns(cols)) * sign
    row = iota((rows, cols), 0)
    local = row & 31
    source = jnp.where(row < 64, (local < NODES).astype(jnp.int32), 2)
    column = iota((rows, cols), 1) & 31
    wide = jnp.where(source == var_of(column), wide, 0.0)
    return split_matrix(wide, 64)


def trace_matrix(trace_ref):
    rows, cols = 96, 96
    row = iota((rows, 4), 0)
    point = row & 3
    point = jnp.where(row < 48, 3 - point, point)
    face = (row >> 4) - jnp.where(row < 48, 0, 3)
    picked = jnp.zeros((rows, NODES), F32)
    for f in range(3):
        pick = ones_where((point == iota((rows, 4), 1)) & (face == f))
        picked = picked + exact(pick, trace_ref[f])
    wide = exact(picked, state_columns(cols))
    part = (iota((rows, cols), 0) >> 2) & 3
    source = jnp.where(part == 3, 0, part)
    column = iota((rows, cols), 1) & 31
    wide = jnp.where(source == var_of(column), wide, 0.0)
    return split_matrix(wide, 64)


def lift_matrix(lift_ref):
    rows, cols = 32, 288
    row = iota((rows, NODES), 0)
    node = row - NODES * var_of(row)
    pick = ones_where((node == iota((rows, NODES), 1)) & (row < 3 * NODES))
    wide = jnp.zeros((rows, cols), F32)
    column = iota((4, cols), 1)
    third = column - 96 * ((column >= 96).astype(jnp.int32) + (column >= 192).astype(jnp.int32))
    for f in range(3):
        points = dot_nt(pick, lift_ref[f], HIGHEST)
        place = ones_where(((third >> 5) == f) & ((third & 3) == iota((4, cols), 0)))
        wide = wide + exact(points, place)
    column = iota((rows, cols), 1)
    third = column - 96 * ((column >= 96).astype(jnp.int32) + (column >= 192).astype(jnp.int32))
    jump = (third & 16) != 0
    part = (third >> 2) & 3
    var = var_of(iota((rows, cols), 0))
    centre = (
        ((var == 0) & ((part == 1) | (part == 2)))
        | ((var == 1) & (part == 0))
        | ((var == 2) & (part == 3))
    )
    factor = jnp.where(jump, ones_where(part == var), -ones_where(centre))
    return split_matrix(wide * factor, 192)


def combine(slopes, alpha):
    a1, a2, a3, a4 = alpha
    both = a1 * slopes[0:32] + a2 * slopes[32:64]
    top = a3 * slopes[64:80] + a4 * slopes[80:96]
    return jnp.concatenate([both[0:16] + top, both[16:32]], axis=0)


def pick_columns(load, sources, block, lane, start):
    out = start
    for k in sources:
        found = jnp.take_along_axis(load(k), lane, axis=1)
        out = jnp.where(block == k, found, out)
    return out


def step_kernel(
    n_region,
    n_dom,
    elems,
    state_ref,
    depth_ref,
    metric_ref,
    diff_ref,
    stiff_ref,
    trace_ref,
    lift_ref,
    cluster_ref,
    code_ref,
    send_reg_ref,
    send_dom_ref,
    move_dom_ref,
    move_slot_ref,
    out_ref,
    *scratch,
):
    hbm_refs = (
        state_ref,
        depth_ref,
        metric_ref,
        diff_ref,
        stiff_ref,
        trace_ref,
        lift_ref,
        cluster_ref,
        code_ref,
        send_reg_ref,
        send_dom_ref,
        move_dom_ref,
        move_slot_ref,
    )
    step_body(
        n_region, n_dom, elems, hbm_refs, out_ref, scratch[: len(hbm_refs)], *scratch[len(hbm_refs) :]
    )


def step_body(
    n_region,
    n_dom,
    elems,
    hbm_refs,
    out_ref,
    local_refs,
    in_sem,
    ready,
    dense,
    tab_a,
    tab_b,
    tab_c,
    beyond,
    out_reg,
    out_dom,
    in_reg,
    in_dom,
    out_fine,
    in_fine,
    land_out,
    land_in,
    tile_out,
    tile_in,
    ss_reg,
    rs_reg,
    ss_dom,
    rs_dom,
    ss_fine,
    rs_fine,
    ss_land,
    rs_land,
    ss_tile,
    rs_tile,
):
    r = lax.axis_index("region")
    d = lax.axis_index("dom")
    blocks = elems // 128
    has_low = r > 0
    has_high = r < n_region - 1
    dom_low = d > 0
    dom_high = d < n_dom - 1
    sides = (
        (has_high, {"region": r + 1}, 1, 0),
        (has_low, {"region": r - 1}, 0, 1),
        (dom_high, {"dom": d + 1}, 1, 0),
        (dom_low, {"dom": d - 1}, 0, 1),
    )
    comes = (has_low, has_high, dom_low, dom_high)

    loads = [
        pltpu.make_async_copy(src, dst, in_sem.at[i])
        for i, (src, dst) in enumerate(zip(hbm_refs, local_refs))
    ]
    barrier = pltpu.get_barrier_semaphore()

    def ring(k):
        return {"dom": lax.rem(d + k + n_dom, n_dom)}

    for i in (0, 1, 2, 3, 5, 9, 10):
        loads[i].start()
    for exists, device, _, _ in sides[:2]:

        @pl.when(exists)
        def _():
            pl.semaphore_signal(barrier, inc=1, device_id=device, device_id_type=MESH)

    for k in (1, -1):
        pl.semaphore_signal(barrier, inc=1, device_id=ring(k), device_id_type=MESH)
    for i in (4, 6, 7, 8, 11, 12):
        loads[i].start()

    def announce(stage, reach):
        for k in (reach, -reach):
            pl.semaphore_signal(
                ready.at[stage], inc=1, device_id=ring(k), device_id_type=MESH
            )

    (
        state_ref,
        depth_ref,
        metric_ref,
        diff_ref,
        stiff_ref,
        trace_ref,
        lift_ref,
        cluster_ref,
        code_ref,
        send_reg_ref,
        send_dom_ref,
        move_dom_ref,
        move_slot_ref,
    ) = local_refs
    for i in (0, 1, 2, 3, 5, 9, 10):
        loads[i].wait()

    dense[30:32, :] = jnp.zeros((2, elems), F32)
    for v in range(3):
        dense[NODES * v : NODES * (v + 1), :] = state_ref[:, v, :]
    state = dense[...]
    depth = depth_ref[...]
    m0, m1, m2, m3 = (metric_ref[i : i + 1, :] for i in range(4))

    row = iota((32, elems), 0)
    a1 = jnp.where(row < 10, m0, jnp.where(row < 20, depth * m0, depth * m2))
    a2 = jnp.where(row < 10, m1, jnp.where(row < 20, depth * m1, depth * m3))
    top = row[0:16] < 10
    a3 = jnp.where(top, m2, 0.0)
    a4 = jnp.where(top, m3, 0.0)
    alpha = (a1, a2, a3, a4)

    slope = slope_matrix(diff_ref, -1.0)
    traces = trace_matrix(trace_ref)

    def series_of(values):
        series = [values]
        for _ in range(3):
            series.append(combine(dot(slope, split_state(series[-1])), alpha))
        return series

    def integrate(series, factors):
        summed = factors[0] * series[0]
        for factor, member in zip(factors[1:], series[1:]):
            summed = summed + factor * member
        return summed

    series = series_of(state)
    early = integrate(series, FIRST_HALF)
    early_split = split_state(early)
    tab_a[0:48] = dot(traces[0:48], early_split)

    def source(table):
        def load(k):
            f, b = divmod(k, blocks)
            return table[16 * f : 16 * f + 16, 128 * b : 128 * b + 128]

        return load

    def spread(vector):
        return jnp.broadcast_to(vector, (16, 128))

    own = range(3 * blocks)

    def gather_sends(which, table):
        for lane_row in range(2):
            for b in range(2):
                index = spread(send_reg_ref[lane_row : lane_row + 1, 128 * b : 128 * b + 128])
                out_reg[which, lane_row, b] = pick_columns(
                    source(table), own, index >> 7, index & 127, jnp.zeros((16, 128), F32)
                )
            index = spread(send_dom_ref[lane_row : lane_row + 1, :])
            out_dom[which, lane_row] = pick_columns(
                source(table), own, index >> 7, index & 127, jnp.zeros((16, 128), F32)
            )

    gather_sends(0, tab_a)

    def copies_a(which):
        copies = []
        for i, (exists, device, lane_row, at) in enumerate(sides):
            regional = i < 2
            copies.append(
                (
                    exists,
                    comes[2 * (i // 2) + at],
                    pltpu.make_async_remote_copy(
                        src_ref=(out_reg if regional else out_dom).at[which, lane_row],
                        dst_ref=(in_reg if regional else in_dom).at[which, at],
                        send_sem=(ss_reg if regional else ss_dom).at[which, at],
                        recv_sem=(rs_reg if regional else rs_dom).at[which, at],
                        device_id=device,
                        device_id_type=MESH,
                    ),
                )
            )
        return copies

    def start(copies):
        for exists, _, copy in copies:
            pl.when(exists)(copy.start)

    def wait_recv(copies):
        for _, arrives, copy in copies:
            pl.when(arrives)(copy.wait_recv)

    def wait_send(copies):
        for exists, _, copy in copies:
            pl.when(exists)(copy.wait_send)

    first_copies = copies_a(0)
    late_copies = copies_a(1)
    pl.semaphore_wait(barrier, 2 + has_low.astype(jnp.int32) + has_high.astype(jnp.int32))
    start(first_copies)
    announce(0, 1)

    later = integrate(series, SECOND_HALF)
    tab_b[...] = dot(traces[0:48], split_state(later))
    gather_sends(1, tab_b)
    start(late_copies)
    pl.semaphore_wait(ready.at[0], 2)
    announce(1, 2)

    for i in range(2):

        @pl.when(jnp.logical_not(comes[i]))
        def _():
            in_reg[:, i] = jnp.zeros(in_reg.shape[0:1] + in_reg.shape[2:], F32)

        @pl.when(jnp.logical_not(comes[2 + i]))
        def _():
            in_dom[:, i] = jnp.zeros(in_dom.shape[0:1] + in_dom.shape[2:], F32)

    for i in range(4):

        @pl.when(jnp.logical_not(comes[i]))
        def _():
            in_fine[i] = jnp.zeros((16, 128), F32)

    for i in (4, 6, 7, 8, 11, 12):
        loads[i].wait()
    tab_a[48:96] = dot(traces[48:96], early_split)
    stiff = slope_matrix(stiff_ref, 1.0)
    lift = lift_matrix(lift_ref)
    half_x = (-m1, m0 + m1, -m0)
    half_y = (-m3, m2 + m3, -m2)
    root = jnp.sqrt(depth)
    rows16 = iota((16, elems), 0)
    centre_by, jump_by = [], []
    for f in range(3):
        hx, hy = half_x[f], half_y[f]
        centre_by.append(
            jnp.where(
                rows16 < 4,
                depth * hx,
                jnp.where(rows16 < 8, hx, jnp.where(rows16 < 12, hy, depth * hy)),
            )
        )
        jump_by.append(root * jnp.sqrt(hx * hx + hy * hy))
    mirror = jnp.where((iota((16, 128), 0) >= 4) & (iota((16, 128), 0) < 12), -1.0, 1.0)
    first_code = 3 * elems
    regional = 2 * send_reg_ref.shape[1]

    def code_of(f, b):
        return spread(code_ref[f : f + 1, 128 * b : 128 * b + 128])

    def local_part(table):
        for f in range(3):
            for b in range(blocks):
                code = code_of(f, b)
                wall = mirror * table[48 + 16 * f : 64 + 16 * f, 128 * b : 128 * b + 128]
                beyond[f, b] = pick_columns(source(table), own, code >> 7, code & 127, wall)

    def remote_part(which, fine):
        def load(k):
            k = k - 3 * blocks
            if k < 4:
                return in_reg[which, k // 2, k % 2]
            return in_dom[which, k - 4]

        for f in range(3):
            for b in range(blocks):
                code = code_of(f, b)
                beyond[f, b] = pick_columns(
                    load,
                    range(3 * blocks, 3 * blocks + 6),
                    code >> 7,
                    code & 127,
                    beyond[f, b],
                )

    def fine_column(code):
        slot = code - first_code
        reg = slot & 255
        from_reg = jnp.where(
            (slot >= 0) & (slot < regional) & (reg < REG_FINE), (slot >> 8) * REG_FINE + reg, -1
        )
        past = slot - regional
        dom = past & 127
        return jnp.where(
            (past >= 0) & (past < 256) & (dom < DOM_FINE),
            2 * REG_FINE + (past >> 7) * DOM_FINE + dom,
            from_reg,
        )

    def increment(values_split, table):
        volume = combine(dot(stiff, values_split), alpha)
        parts = []
        for f in range(3):
            outside = jnp.concatenate([beyond[f, b] for b in range(blocks)], axis=1)
            inside = table[48 + 16 * f : 64 + 16 * f, :]
            parts.append(centre_by[f] * (outside + inside))
            parts.append(jump_by[f] * (outside - inside))
        return volume + dot(lift, split_state(jnp.concatenate(parts, axis=0)))

    local_part(tab_a)
    pl.semaphore_wait(ready.at[1], 2)
    announce(2, 2)
    nearest = sorted(range(1, n_dom), key=lambda k: min(k, n_dom - k))
    def peer_copies(src, dst, ss, rs):
        return {
            k: pltpu.make_async_remote_copy(
                src_ref=src.at[k],
                dst_ref=dst.at[k],
                send_sem=ss.at[k],
                recv_sem=rs.at[k],
                device_id={"dom": lax.rem(d + k, n_dom)},
                device_id_type=MESH,
            )
            for k in range(1, n_dom)
        }

    wait_recv(first_copies)
    remote_part(0, False)
    midway = state + increment(early_split, tab_a)
    fine = integrate(series_of(midway), FIRST_HALF)
    second = jnp.where(cluster_ref[...] == 0, fine, later)
    second_split = split_state(second)
    tab_c[...] = dot(traces, second_split)

    lane = iota((1, 128), 1)
    wanted = jnp.where(
        lane < REG_FINE,
        send_reg_ref[1:2, 0:128],
        jnp.where(
            lane < 2 * REG_FINE,
            pltpu.roll(send_reg_ref[0:1, 0:128], REG_FINE, 1),
            jnp.where(
                lane < 2 * REG_FINE + DOM_FINE,
                pltpu.roll(send_dom_ref[1:2, :], 2 * REG_FINE, 1),
                pltpu.roll(send_dom_ref[0:1, :], 2 * REG_FINE + DOM_FINE, 1),
            ),
        ),
    )
    wanted = spread(wanted)
    out_fine[...] = pick_columns(
        source(tab_c), own, wanted >> 7, wanted & 127, jnp.zeros((16, 128), F32)
    )
    fine_copies = []
    for i, (exists, device, _, at) in enumerate(sides):
        fine_copies.append(
            (
                exists,
                comes[2 * (i // 2) + at],
                pltpu.make_async_remote_copy(
                    src_ref=out_fine,
                    dst_ref=in_fine.at[i],
                    send_sem=ss_fine.at[i],
                    recv_sem=rs_fine.at[i],
                    device_id=device,
                    device_id_type=MESH,
                ),
            )
        )
    start(fine_copies)

    lanes = iota((1, elems), 1)
    offset = move_dom_ref[...] - d
    offset = jnp.where(offset < 0, offset + n_dom, offset)
    chosen = jnp.where(iota((16, elems), 0) == offset, 1.0, 0.0)
    before = jnp.where(iota((elems, elems), 0) < iota((elems, elems), 1), 1.0, 0.0).astype(BF16)
    rank = jnp.sum(chosen * dot(chosen.astype(BF16), before), axis=0, keepdims=True)
    slots = n_dom * MIGRANTS
    padded = 384 if slots <= 384 else 128 * (-(-slots // 128))
    position = jnp.where(offset == 0, -1, offset * MIGRANTS + rank.astype(jnp.int32))
    inverse = jnp.where(iota((padded, elems), 0) == position, 1.0, 0.0).astype(BF16)
    place = move_slot_ref[...]
    which_row = iota((8, elems), 0)
    facts = jnp.where(
        which_row == 0,
        lanes >> 1,
        jnp.where(
            which_row == 1, lanes & 1, jnp.where(which_row == 2, place >> 1, place & 1)
        ),
    )
    facts = jnp.where(which_row < 4, facts, 0).astype(F32).astype(BF16)
    found = dot_nt(facts, inverse).astype(jnp.int32)
    leaves = found[0:1] * 2 + found[1:2]
    lands = found[2:3] * 2 + found[3:4]
    for k in range(1, n_dom):
        land_out[k] = lands[:, 128 * (k // 4) : 128 * (k // 4) + 128]

    pl.semaphore_wait(ready.at[2], 2)
    land_copies = peer_copies(land_out, land_in, ss_land, rs_land)
    for k in nearest[::-1]:
        land_copies[k].start()
    local_part(tab_c)
    wait_recv(late_copies)
    remote_part(1, True)
    for k in range(1, n_dom):
        land_copies[k].wait_recv()
    kk = iota((1, 128), 1)
    stack = []
    for q in range(padded // 128):
        row_q = jnp.full((1, 128), -1, jnp.int32)
        for k in range(4 * q, min(4 * q + 4, n_dom)):
            if k > 0:
                row_q = jnp.where((kk >> 5) == (k & 3), land_in[k], row_q)
        stack.append(row_q)
    places = jnp.concatenate(stack, axis=1)
    comes_here = jnp.where(iota((elems, padded), 0) == places, 1.0, 0.0).astype(BF16)
    column = iota((8, padded), 1)
    row8 = iota((8, padded), 0)
    facts = jnp.where(row8 == 0, column >> 1, jnp.where(row8 == 1, column & 1, 1))
    found = dot_nt(facts.astype(F32).astype(BF16), comes_here).astype(jnp.int32)
    origin = jnp.where(found[2:3] > 0, found[0:1] * 2 + found[1:2], -1)

    wait_recv(fine_copies)
    lane16 = iota((16, 128), 1)
    fresh = jnp.where(
        lane16 < REG_FINE,
        in_fine[0],
        jnp.where(
            lane16 < 2 * REG_FINE,
            in_fine[1],
            jnp.where(lane16 < 2 * REG_FINE + DOM_FINE, in_fine[2], in_fine[3]),
        ),
    )
    for f in range(3):
        for b in range(blocks):
            column = fine_column(code_of(f, b))
            found = jnp.take_along_axis(fresh, column & 127, axis=1)
            beyond[f, b] = jnp.where(column >= 0, found, beyond[f, b])
    dense[...] = midway + increment(second_split, tab_c)

    def cell(g, b):
        return dense[8 * g : 8 * g + 8, 128 * b : 128 * b + 128]

    group = iota((8, 128), 1) >> 5
    tile_copies = peer_copies(tile_out, tile_in, ss_tile, rs_tile)
    packed = {}
    for q in range(padded // 128):
        index = jnp.broadcast_to(leaves[:, 128 * q : 128 * q + 128], (8, 128))
        for g in range(4):
            packed[g, q] = pick_columns(
                lambda b: cell(g, b), range(blocks), index >> 7, index & 127, jnp.zeros((8, 128), F32)
            )
    for k in nearest[::-1]:
        tile = jnp.zeros((8, 128), F32)
        for g in range(4):
            shift = (32 * (g - (k & 3))) % 128
            moved = packed[g, k // 4]
            if shift:
                moved = pltpu.roll(moved, shift, 1)
            tile = jnp.where(group == g, moved, tile)
        tile_out[k] = tile
        tile_copies[k].start()

    result = {(g, b): cell(g, b) for g in range(4) for b in range(blocks)}
    for k in nearest:
        tile_copies[k].wait_recv()
        tile = tile_in[k]
        for b in range(blocks):
            index = jnp.broadcast_to(origin[:, 128 * b : 128 * b + 128], (8, 128))
            here = (index >> 5) == k
            for g in range(4):
                found = jnp.take_along_axis(tile, (index & 31) + 32 * g, axis=1)
                result[g, b] = jnp.where(here, found, result[g, b])
    for g in range(4):
        for b in range(blocks):
            dense[8 * g : 8 * g + 8, 128 * b : 128 * b + 128] = result[g, b]
    for v in range(3):
        out_ref[:, v, :] = dense[NODES * v : NODES * (v + 1), :]

    wait_send(first_copies)
    wait_send(late_copies)
    wait_send(fine_copies)
    for k in range(1, n_dom):
        land_copies[k].wait_send()
        tile_copies[k].wait_send()


def shards(n_region, n_dom, *args):
    (
        water_state,
        water_depth,
        metric,
        diff_ops,
        stiff_ops,
        trace_ops,
        lift_ops,
        cluster,
        face_code,
        send_region,
        send_dom,
        move_dom,
        move_slot,
    ) = args
    elems = water_state.shape[2]
    blocks = elems // 128
    vmem = pl.BlockSpec(memory_space=pltpu.VMEM)
    dma = pltpu.SemaphoreType.DMA

    def kernel(*refs):
        step_kernel(n_region, n_dom, elems, *refs)

    given = (
        jnp.transpose(water_state, (1, 0, 2)),
        water_depth.reshape(1, elems),
        metric,
        jnp.transpose(diff_ops, (1, 0, 2)),
        jnp.transpose(stiff_ops, (1, 0, 2)),
        trace_ops,
        jnp.transpose(lift_ops, (0, 2, 1)),
        cluster.reshape(1, elems),
        face_code,
        send_region,
        send_dom,
        move_dom.reshape(1, elems),
        move_slot.reshape(1, elems),
    )
    result = pl.pallas_call(
        kernel,
        out_shape=pltpu.VMEM((NODES, 3, elems), F32),
        in_specs=[pl.BlockSpec(memory_space=pl.ANY)] * 13,
        out_specs=vmem,
        scratch_shapes=[pltpu.VMEM(x.shape, x.dtype) for x in given]
        + [
            dma((13,)),
            pltpu.SemaphoreType.REGULAR((3,)),
            pltpu.VMEM((32, elems), F32),
            pltpu.VMEM((96, elems), F32),
            pltpu.VMEM((48, elems), F32),
            pltpu.VMEM((96, elems), F32),
            pltpu.VMEM((3, blocks, 16, 128), F32),
            pltpu.VMEM((2, 2, 2, 16, 128), F32),
            pltpu.VMEM((2, 2, 16, 128), F32),
            pltpu.VMEM((2, 2, 2, 16, 128), F32),
            pltpu.VMEM((2, 2, 16, 128), F32),
            pltpu.VMEM((16, 128), F32),
            pltpu.VMEM((4, 16, 128), F32),
            pltpu.VMEM((n_dom, 1, 128), jnp.int32),
            pltpu.VMEM((n_dom, 1, 128), jnp.int32),
            pltpu.VMEM((n_dom, 8, 128), F32),
            pltpu.VMEM((n_dom, 8, 128), F32),
            dma((2, 2)),
            dma((2, 2)),
            dma((2, 2)),
            dma((2, 2)),
            dma((4,)),
            dma((4,)),
            dma((n_dom,)),
            dma((n_dom,)),
            dma((n_dom,)),
            dma((n_dom,)),
        ],
        compiler_params=pltpu.CompilerParams(collective_id=0, has_side_effects=True),
        name="wave_step",
    )(*given)
    return jnp.transpose(result, (1, 0, 2))


def solution(mesh):
    both = ("region", "dom")
    wide, flat = P(None, both), P(both)
    placed = (
        P(None, None, both),
        flat,
        wide,
        P(),
        P(),
        P(),
        P(),
        flat,
        wide,
        wide,
        wide,
        flat,
        flat,
    )
    n_region, n_dom = mesh.shape["region"], mesh.shape["dom"]

    def step(*args):
        return shards(n_region, n_dom, *args)

    return jax.shard_map(
        step,
        mesh=mesh,
        in_specs=placed,
        out_specs=P(None, None, both),
        check_vma=False,
    )
```

```python
import jax
import jax.numpy as jnp
import numpy as np
from jax import lax
from jax.experimental import pallas as pl
from jax.experimental.pallas import tpu as pltpu
from jax.sharding import PartitionSpec as P

MESH = pl.DeviceIdType.MESH
F32 = jnp.float32
BF16 = jnp.bfloat16
NODES = 10
FIRST_HALF = (0.5, 0.125, 1.0 / 48.0, 1.0 / 384.0)
SECOND_HALF = (0.5, 0.375, 7.0 / 48.0, 15.0 / 384.0)
MIGRANTS = 32
REG_FINE = 8
DOM_FINE = 4
EARLY_LOADS = (3, 5, 13, 14, 15, 0, 1, 2, 9, 10)
LATE_LOADS = (4, 6, 7, 8, 11, 12, 16, 17, 18)


def iota(shape, dim):
    return lax.broadcasted_iota(jnp.int32, shape, dim)


def dot(a, b):
    return jnp.dot(a, b, preferred_element_type=F32)


def dot_nt(a, b):
    return lax.dot_general(a, b, (((1,), (1,)), ((), ())), preferred_element_type=F32)


def split_state(values):
    hi = values.astype(BF16)
    lo = (values - hi.astype(F32)).astype(BF16)
    return jnp.concatenate([hi, lo, hi], axis=0)


def pattern():
    pick = np.zeros((192, 32), np.float32)
    mask = np.zeros((192, 96), np.float32)
    columns = np.zeros((2, 16, 96), np.float32)
    for column in range(96):
        third, at = divmod(column, 32)
        if at < 3 * NODES:
            columns[third // 2, at % NODES, column] = 1.0

    def fill(row, source, var, sign):
        pick[row, source] = 1.0
        for third in range(3):
            first = 32 * third + NODES * var
            mask[row, first : first + NODES] = sign

    for which in range(2):
        for at in range(3 * NODES):
            node, part = at % NODES, at // NODES
            fill(32 * which + at, NODES * which + node, 1 if part == 0 else 0, -1.0)
        for node in range(NODES):
            fill(64 + 16 * which + node, NODES * which + node, 2, -1.0)
    for order in range(2):
        for face in range(3):
            for at in range(16):
                part, point = divmod(at, 4)
                source = 2 * NODES + 4 * face + (point if order else 3 - point)
                fill(96 + 48 * order + 16 * face + at, source, part % 3, 1.0)

    nodes = np.zeros((32, 16), np.float32)
    for row in range(3 * NODES):
        nodes[row, row % NODES] = 1.0
    places = np.zeros((2, 16, 288), np.float32)
    signs = np.zeros((32, 288), np.float32)
    for column in range(288):
        third, rest = divmod(column, 96)
        face, at = divmod(rest, 32)
        jump, at = divmod(at, 16)
        part, point = divmod(at, 4)
        places[third // 2, 4 * face + point, column] = 1.0
        for row in range(3 * NODES):
            var = row // NODES
            if jump:
                signs[row, column] = 1.0 if part == var else 0.0
            else:
                signs[row, column] = -1.0 if part in ((1, 2), (0,), (3,))[var] else 0.0
    return [jnp.asarray(x, BF16) for x in (pick, mask, columns, nodes, places, signs)]


def halves(values):
    hi = values.astype(BF16)
    return hi, (values - hi.astype(F32)).astype(BF16)


def spread_columns(values, columns_ref):
    hi, lo = halves(values)
    return (dot(hi, columns_ref[0]) + dot(lo, columns_ref[1])).astype(BF16)


def combine(slopes, alpha):
    a1, a2, a3, a4 = alpha
    both = a1 * slopes[0:32] + a2 * slopes[32:64]
    top = a3 * slopes[64:80] + a4 * slopes[80:96]
    return jnp.concatenate([both[0:16] + top, both[16:32]], axis=0)


def pick_columns(load, sources, block, lane, start):
    out = start
    for k in sources:
        found = jnp.take_along_axis(load(k), lane, axis=1)
        out = jnp.where(block == k, found, out)
    return out


def step_kernel(
    n_region,
    n_dom,
    elems,
    state_ref,
    depth_ref,
    metric_ref,
    diff_ref,
    stiff_ref,
    trace_ref,
    lift_ref,
    cluster_ref,
    code_ref,
    send_reg_ref,
    send_dom_ref,
    move_dom_ref,
    move_slot_ref,
    pick_ref,
    mask_ref,
    columns_ref,
    nodes_ref,
    places_ref,
    signs_ref,
    out_ref,
    *scratch,
):
    hbm_refs = (
        state_ref,
        depth_ref,
        metric_ref,
        diff_ref,
        stiff_ref,
        trace_ref,
        lift_ref,
        cluster_ref,
        code_ref,
        send_reg_ref,
        send_dom_ref,
        move_dom_ref,
        move_slot_ref,
        pick_ref,
        mask_ref,
        columns_ref,
        nodes_ref,
        places_ref,
        signs_ref,
    )
    step_body(
        n_region, n_dom, elems, hbm_refs, out_ref, scratch[: len(hbm_refs)], *scratch[len(hbm_refs) :]
    )


def step_body(
    n_region,
    n_dom,
    elems,
    hbm_refs,
    out_ref,
    local_refs,
    in_sem,
    ready,
    first_ops,
    second_ops,
    lift_ops,
    dense,
    tab_a,
    tab_b,
    tab_c,
    beyond,
    out_reg,
    out_dom,
    in_reg,
    in_dom,
    out_fine,
    in_fine,
    land_out,
    land_in,
    tile_out,
    tile_in,
    ss_reg,
    rs_reg,
    ss_dom,
    rs_dom,
    ss_fine,
    rs_fine,
    ss_land,
    rs_land,
    ss_tile,
    rs_tile,
):
    r = lax.axis_index("region")
    d = lax.axis_index("dom")
    blocks = elems // 128
    has_low = r > 0
    has_high = r < n_region - 1
    dom_low = d > 0
    dom_high = d < n_dom - 1
    sides = (
        (has_high, {"region": r + 1}, 1, 0),
        (has_low, {"region": r - 1}, 0, 1),
        (dom_high, {"dom": d + 1}, 1, 0),
        (dom_low, {"dom": d - 1}, 0, 1),
    )
    comes = (has_low, has_high, dom_low, dom_high)

    loads = [
        pltpu.make_async_copy(src, dst, in_sem.at[i])
        for i, (src, dst) in enumerate(zip(hbm_refs, local_refs))
    ]
    barrier = pltpu.get_barrier_semaphore()

    def ring(k):
        return {"dom": lax.rem(d + k + n_dom, n_dom)}

    for i in EARLY_LOADS:
        loads[i].start()
    for exists, device, _, _ in sides[:2]:

        @pl.when(exists)
        def _():
            pl.semaphore_signal(barrier, inc=1, device_id=device, device_id_type=MESH)

    for k in (1, -1):
        pl.semaphore_signal(barrier, inc=1, device_id=ring(k), device_id_type=MESH)
    for i in LATE_LOADS:
        loads[i].start()

    def announce(stage, reach):
        for k in (reach, -reach):
            pl.semaphore_signal(
                ready.at[stage], inc=1, device_id=ring(k), device_id_type=MESH
            )

    (
        state_ref,
        depth_ref,
        metric_ref,
        diff_ref,
        stiff_ref,
        trace_ref,
        lift_ref,
        cluster_ref,
        code_ref,
        send_reg_ref,
        send_dom_ref,
        move_dom_ref,
        move_slot_ref,
        pick_ref,
        mask_ref,
        columns_ref,
        nodes_ref,
        places_ref,
        signs_ref,
    ) = local_refs
    first_ops[...] = jnp.zeros((32, 16), F32)
    second_ops[...] = jnp.zeros((32, 16), F32)
    lift_ops[...] = jnp.zeros((16, 16), F32)
    for i in EARLY_LOADS:
        loads[i].wait()

    dense[30:32, :] = jnp.zeros((2, elems), F32)
    for v in range(3):
        dense[NODES * v : NODES * (v + 1), :] = state_ref[:, v, :]
    state = dense[...]
    depth = depth_ref[...]
    m0, m1, m2, m3 = (metric_ref[i : i + 1, :] for i in range(4))

    row = iota((32, elems), 0)
    a1 = jnp.where(row < 10, m0, jnp.where(row < 20, depth * m0, depth * m2))
    a2 = jnp.where(row < 10, m1, jnp.where(row < 20, depth * m1, depth * m3))
    top = row[0:16] < 10
    a3 = jnp.where(top, m2, 0.0)
    a4 = jnp.where(top, m3, 0.0)
    alpha = (a1, a2, a3, a4)

    for a in range(2):
        first_ops[NODES * a : NODES * (a + 1), 0:NODES] = diff_ref[:, a, :]
    for f in range(3):
        first_ops[2 * NODES + 4 * f : 2 * NODES + 4 * f + 4, 0:NODES] = trace_ref[f]
    wide = dot(pick_ref[...], spread_columns(first_ops[...], columns_ref)).astype(BF16)
    wide = wide * mask_ref[...]
    slope, traces = wide[0:96], wide[96:192]

    def series_of(values):
        series = [values]
        for _ in range(3):
            series.append(combine(dot(slope, split_state(series[-1])), alpha))
        return series

    def integrate(series, factors):
        summed = factors[0] * series[0]
        for factor, member in zip(factors[1:], series[1:]):
            summed = summed + factor * member
        return summed

    series = series_of(state)
    early = integrate(series, FIRST_HALF)
    early_split = split_state(early)
    tab_a[0:48] = dot(traces[0:48], early_split)

    def source(table):
        def load(k):
            f, b = divmod(k, blocks)
            return table[16 * f : 16 * f + 16, 128 * b : 128 * b + 128]

        return load

    def spread(vector):
        return jnp.broadcast_to(vector, (16, 128))

    own = range(3 * blocks)

    def gather_sends(which, table):
        for lane_row in range(2):
            for b in range(2):
                index = spread(send_reg_ref[lane_row : lane_row + 1, 128 * b : 128 * b + 128])
                out_reg[which, lane_row, b] = pick_columns(
                    source(table), own, index >> 7, index & 127, jnp.zeros((16, 128), F32)
                )
            index = spread(send_dom_ref[lane_row : lane_row + 1, :])
            out_dom[which, lane_row] = pick_columns(
                source(table), own, index >> 7, index & 127, jnp.zeros((16, 128), F32)
            )

    gather_sends(0, tab_a)

    def copies_a(which):
        copies = []
        for i, (exists, device, lane_row, at) in enumerate(sides):
            regional = i < 2
            copies.append(
                (
                    exists,
                    comes[2 * (i // 2) + at],
                    pltpu.make_async_remote_copy(
                        src_ref=(out_reg if regional else out_dom).at[which, lane_row],
                        dst_ref=(in_reg if regional else in_dom).at[which, at],
                        send_sem=(ss_reg if regional else ss_dom).at[which, at],
                        recv_sem=(rs_reg if regional else rs_dom).at[which, at],
                        device_id=device,
                        device_id_type=MESH,
                    ),
                )
            )
        return copies

    def start(copies):
        for exists, _, copy in copies:
            pl.when(exists)(copy.start)

    def wait_recv(copies):
        for _, arrives, copy in copies:
            pl.when(arrives)(copy.wait_recv)

    def wait_send(copies):
        for exists, _, copy in copies:
            pl.when(exists)(copy.wait_send)

    first_copies = copies_a(0)
    late_copies = copies_a(1)
    pl.semaphore_wait(barrier, 2 + has_low.astype(jnp.int32) + has_high.astype(jnp.int32))
    start(first_copies)
    announce(0, 1)

    later = integrate(series, SECOND_HALF)
    tab_b[...] = dot(traces[0:48], split_state(later))
    gather_sends(1, tab_b)
    start(late_copies)

    for i in range(2):

        @pl.when(jnp.logical_not(comes[i]))
        def _():
            in_reg[:, i] = jnp.zeros(in_reg.shape[0:1] + in_reg.shape[2:], F32)

        @pl.when(jnp.logical_not(comes[2 + i]))
        def _():
            in_dom[:, i] = jnp.zeros(in_dom.shape[0:1] + in_dom.shape[2:], F32)

    for i in range(4):

        @pl.when(jnp.logical_not(comes[i]))
        def _():
            in_fine[i] = jnp.zeros((16, 128), F32)

    for i in LATE_LOADS:
        loads[i].wait()
    tab_a[48:96] = dot(traces[48:96], early_split)
    for a in range(2):
        second_ops[NODES * a : NODES * (a + 1), 0:NODES] = stiff_ref[:, a, :]
    stiff = dot(pick_ref[0:96], spread_columns(second_ops[...], columns_ref)).astype(BF16)
    stiff = -(stiff * mask_ref[0:96])
    for f in range(3):
        lift_ops[4 * f : 4 * f + 4, 0:NODES] = lift_ref[f]
    hi, lo = halves(lift_ops[...])
    lift = dot(dot_nt(nodes_ref[...], hi).astype(BF16), places_ref[0])
    lift = lift + dot(dot_nt(nodes_ref[...], lo).astype(BF16), places_ref[1])
    lift = lift.astype(BF16) * signs_ref[...]
    half_x = (-m1, m0 + m1, -m0)
    half_y = (-m3, m2 + m3, -m2)
    root = jnp.sqrt(depth)
    rows16 = iota((16, elems), 0)
    centre_by, jump_by = [], []
    for f in range(3):
        hx, hy = half_x[f], half_y[f]
        centre_by.append(
            jnp.where(
                rows16 < 4,
                depth * hx,
                jnp.where(rows16 < 8, hx, jnp.where(rows16 < 12, hy, depth * hy)),
            )
        )
        jump_by.append(root * jnp.sqrt(hx * hx + hy * hy))
    mirror = jnp.where((iota((16, 128), 0) >= 4) & (iota((16, 128), 0) < 12), -1.0, 1.0)
    first_code = 3 * elems
    regional = 2 * send_reg_ref.shape[1]

    def code_of(f, b):
        return spread(code_ref[f : f + 1, 128 * b : 128 * b + 128])

    def local_part(table):
        for f in range(3):
            for b in range(blocks):
                code = code_of(f, b)
                wall = mirror * table[48 + 16 * f : 64 + 16 * f, 128 * b : 128 * b + 128]
                beyond[f, b] = pick_columns(source(table), own, code >> 7, code & 127, wall)

    def remote_part(which):
        def load(k):
            k = k - 3 * blocks
            if k < 4:
                return in_reg[which, k // 2, k % 2]
            return in_dom[which, k - 4]

        for f in range(3):
            for b in range(blocks):
                code = code_of(f, b)
                beyond[f, b] = pick_columns(
                    load,
                    range(3 * blocks, 3 * blocks + 6),
                    code >> 7,
                    code & 127,
                    beyond[f, b],
                )

    def fine_column(code):
        slot = code - first_code
        reg = slot & 255
        from_reg = jnp.where(
            (slot >= 0) & (slot < regional) & (reg < REG_FINE), (slot >> 8) * REG_FINE + reg, -1
        )
        past = slot - regional
        dom = past & 127
        return jnp.where(
            (past >= 0) & (past < 256) & (dom < DOM_FINE),
            2 * REG_FINE + (past >> 7) * DOM_FINE + dom,
            from_reg,
        )

    def increment(values_split, table):
        volume = combine(dot(stiff, values_split), alpha)
        parts = []
        for f in range(3):
            outside = jnp.concatenate([beyond[f, b] for b in range(blocks)], axis=1)
            inside = table[48 + 16 * f : 64 + 16 * f, :]
            parts.append(centre_by[f] * (outside + inside))
            parts.append(jump_by[f] * (outside - inside))
        return volume + dot(lift, split_state(jnp.concatenate(parts, axis=0)))

    local_part(tab_a)
    pl.semaphore_wait(ready.at[0], 2)
    announce(1, 2)
    nearest = sorted(range(1, n_dom), key=lambda k: min(k, n_dom - k))
    def peer_copies(src, dst, ss, rs):
        return {
            k: pltpu.make_async_remote_copy(
                src_ref=src.at[k],
                dst_ref=dst.at[k],
                send_sem=ss.at[k],
                recv_sem=rs.at[k],
                device_id={"dom": lax.rem(d + k, n_dom)},
                device_id_type=MESH,
            )
            for k in range(1, n_dom)
        }

    wait_recv(first_copies)
    remote_part(0)
    midway = state + increment(early_split, tab_a)
    fine = integrate(series_of(midway), FIRST_HALF)
    second = jnp.where(cluster_ref[...] == 0, fine, later)
    second_split = split_state(second)
    tab_c[0:48] = dot(traces[0:48], second_split)

    lane = iota((1, 128), 1)
    wanted = jnp.where(
        lane < REG_FINE,
        send_reg_ref[1:2, 0:128],
        jnp.where(
            lane < 2 * REG_FINE,
            pltpu.roll(send_reg_ref[0:1, 0:128], REG_FINE, 1),
            jnp.where(
                lane < 2 * REG_FINE + DOM_FINE,
                pltpu.roll(send_dom_ref[1:2, :], 2 * REG_FINE, 1),
                pltpu.roll(send_dom_ref[0:1, :], 2 * REG_FINE + DOM_FINE, 1),
            ),
        ),
    )
    wanted = spread(wanted)
    out_fine[...] = pick_columns(
        source(tab_c), own, wanted >> 7, wanted & 127, jnp.zeros((16, 128), F32)
    )
    fine_copies = []
    for i, (exists, device, _, at) in enumerate(sides):
        fine_copies.append(
            (
                exists,
                comes[2 * (i // 2) + at],
                pltpu.make_async_remote_copy(
                    src_ref=out_fine,
                    dst_ref=in_fine.at[i],
                    send_sem=ss_fine.at[i],
                    recv_sem=rs_fine.at[i],
                    device_id=device,
                    device_id_type=MESH,
                ),
            )
        )
    start(fine_copies)
    pl.semaphore_wait(ready.at[1], 2)
    announce(2, 2)

    lanes = iota((1, elems), 1)
    offset = move_dom_ref[...] - d
    offset = jnp.where(offset < 0, offset + n_dom, offset)
    chosen = jnp.where(iota((16, elems), 0) == offset, 1.0, 0.0)
    before = jnp.where(iota((elems, elems), 0) < iota((elems, elems), 1), 1.0, 0.0).astype(BF16)
    rank = jnp.sum(chosen * dot(chosen.astype(BF16), before), axis=0, keepdims=True)
    slots = n_dom * MIGRANTS
    padded = 384 if slots <= 384 else 128 * (-(-slots // 128))
    position = jnp.where(offset == 0, -1, offset * MIGRANTS + rank.astype(jnp.int32))
    inverse = jnp.where(iota((padded, elems), 0) == position, 1.0, 0.0).astype(BF16)
    place = move_slot_ref[...]
    which_row = iota((8, elems), 0)
    facts = jnp.where(
        which_row == 0,
        lanes >> 1,
        jnp.where(
            which_row == 1, lanes & 1, jnp.where(which_row == 2, place >> 1, place & 1)
        ),
    )
    facts = jnp.where(which_row < 4, facts, 0).astype(F32).astype(BF16)
    found = dot_nt(facts, inverse).astype(jnp.int32)
    leaves = found[0:1] * 2 + found[1:2]
    lands = found[2:3] * 2 + found[3:4]
    for k in range(1, n_dom):
        land_out[k] = lands[:, 128 * (k // 4) : 128 * (k // 4) + 128]

    tab_c[48:96] = dot(traces[48:96], second_split)
    local_part(tab_c)
    wait_recv(late_copies)
    remote_part(1)
    columns = {}
    for f in range(3):
        for b in range(blocks):
            columns[f, b] = fine_column(code_of(f, b))
            beyond[f, b] = jnp.where(columns[f, b] >= 0, 0.0, beyond[f, b])
    dense[...] = midway + increment(second_split, tab_c)
    pl.semaphore_wait(ready.at[2], 2)
    land_copies = peer_copies(land_out, land_in, ss_land, rs_land)
    for k in nearest[::-1]:
        land_copies[k].start()
    wait_recv(fine_copies)
    lane16 = iota((16, 128), 1)
    fresh = jnp.where(
        lane16 < REG_FINE,
        in_fine[0],
        jnp.where(
            lane16 < 2 * REG_FINE,
            in_fine[1],
            jnp.where(lane16 < 2 * REG_FINE + DOM_FINE, in_fine[2], in_fine[3]),
        ),
    )
    parts = []
    for f in range(3):
        late = []
        for b in range(blocks):
            found = jnp.take_along_axis(fresh, columns[f, b] & 127, axis=1)
            late.append(jnp.where(columns[f, b] >= 0, found, 0.0))
        late = jnp.concatenate(late, axis=1)
        parts.append(centre_by[f] * late)
        parts.append(jump_by[f] * late)
    dense[...] = dense[...] + dot(lift, split_state(jnp.concatenate(parts, axis=0)))

    def cell(g, b):
        return dense[8 * g : 8 * g + 8, 128 * b : 128 * b + 128]

    group = iota((8, 128), 1) >> 5
    tile_copies = peer_copies(tile_out, tile_in, ss_tile, rs_tile)
    packed = {}
    for q in range(padded // 128):
        index = jnp.broadcast_to(leaves[:, 128 * q : 128 * q + 128], (8, 128))
        for g in range(4):
            packed[g, q] = pick_columns(
                lambda b: cell(g, b), range(blocks), index >> 7, index & 127, jnp.zeros((8, 128), F32)
            )
    for k in nearest[::-1]:
        tile = jnp.zeros((8, 128), F32)
        for g in range(4):
            shift = (32 * (g - (k & 3))) % 128
            moved = packed[g, k // 4]
            if shift:
                moved = pltpu.roll(moved, shift, 1)
            tile = jnp.where(group == g, moved, tile)
        tile_out[k] = tile
        tile_copies[k].start()

    for k in range(1, n_dom):
        land_copies[k].wait_recv()
    kk = iota((1, 128), 1)
    stack = []
    for q in range(padded // 128):
        row_q = jnp.full((1, 128), -1, jnp.int32)
        for k in range(4 * q, min(4 * q + 4, n_dom)):
            if k > 0:
                row_q = jnp.where((kk >> 5) == (k & 3), land_in[k], row_q)
        stack.append(row_q)
    places = jnp.concatenate(stack, axis=1)
    comes_here = jnp.where(iota((elems, padded), 0) == places, 1.0, 0.0).astype(BF16)
    column = iota((8, padded), 1)
    row8 = iota((8, padded), 0)
    facts = jnp.where(row8 == 0, column >> 1, jnp.where(row8 == 1, column & 1, 1))
    found = dot_nt(facts.astype(F32).astype(BF16), comes_here).astype(jnp.int32)
    origin = jnp.where(found[2:3] > 0, found[0:1] * 2 + found[1:2], -1)

    result = {(g, b): cell(g, b) for g in range(4) for b in range(blocks)}
    for k in nearest:
        tile_copies[k].wait_recv()
        tile = tile_in[k]
        for b in range(blocks):
            index = jnp.broadcast_to(origin[:, 128 * b : 128 * b + 128], (8, 128))
            here = (index >> 5) == k
            for g in range(4):
                found = jnp.take_along_axis(tile, (index & 31) + 32 * g, axis=1)
                result[g, b] = jnp.where(here, found, result[g, b])
    for g in range(4):
        for b in range(blocks):
            dense[8 * g : 8 * g + 8, 128 * b : 128 * b + 128] = result[g, b]
    for v in range(3):
        out_ref[:, v, :] = dense[NODES * v : NODES * (v + 1), :]

    wait_send(first_copies)
    wait_send(late_copies)
    wait_send(fine_copies)
    for k in range(1, n_dom):
        land_copies[k].wait_send()
        tile_copies[k].wait_send()


def shards(n_region, n_dom, *args):
    (
        water_state,
        water_depth,
        metric,
        diff_ops,
        stiff_ops,
        trace_ops,
        lift_ops,
        cluster,
        face_code,
        send_region,
        send_dom,
        move_dom,
        move_slot,
    ) = args
    elems = water_state.shape[2]
    blocks = elems // 128
    vmem = pl.BlockSpec(memory_space=pltpu.VMEM)
    dma = pltpu.SemaphoreType.DMA

    def kernel(*refs):
        step_kernel(n_region, n_dom, elems, *refs)

    given = (
        jnp.transpose(water_state, (1, 0, 2)),
        water_depth.reshape(1, elems),
        metric,
        jnp.transpose(diff_ops, (1, 0, 2)),
        jnp.transpose(stiff_ops, (1, 0, 2)),
        trace_ops,
        jnp.transpose(lift_ops, (0, 2, 1)),
        cluster.reshape(1, elems),
        face_code,
        send_region,
        send_dom,
        move_dom.reshape(1, elems),
        move_slot.reshape(1, elems),
        *pattern(),
    )
    result = pl.pallas_call(
        kernel,
        out_shape=pltpu.VMEM((NODES, 3, elems), F32),
        in_specs=[pl.BlockSpec(memory_space=pl.ANY)] * len(given),
        out_specs=vmem,
        scratch_shapes=[pltpu.VMEM(x.shape, x.dtype) for x in given]
        + [
            dma((len(given),)),
            pltpu.SemaphoreType.REGULAR((3,)),
            pltpu.VMEM((32, 16), F32),
            pltpu.VMEM((32, 16), F32),
            pltpu.VMEM((16, 16), F32),
            pltpu.VMEM((32, elems), F32),
            pltpu.VMEM((96, elems), F32),
            pltpu.VMEM((48, elems), F32),
            pltpu.VMEM((96, elems), F32),
            pltpu.VMEM((3, blocks, 16, 128), F32),
            pltpu.VMEM((2, 2, 2, 16, 128), F32),
            pltpu.VMEM((2, 2, 16, 128), F32),
            pltpu.VMEM((2, 2, 2, 16, 128), F32),
            pltpu.VMEM((2, 2, 16, 128), F32),
            pltpu.VMEM((16, 128), F32),
            pltpu.VMEM((4, 16, 128), F32),
            pltpu.VMEM((n_dom, 1, 128), jnp.int32),
            pltpu.VMEM((n_dom, 1, 128), jnp.int32),
            pltpu.VMEM((n_dom, 8, 128), F32),
            pltpu.VMEM((n_dom, 8, 128), F32),
            dma((2, 2)),
            dma((2, 2)),
            dma((2, 2)),
            dma((2, 2)),
            dma((4,)),
            dma((4,)),
            dma((n_dom,)),
            dma((n_dom,)),
            dma((n_dom,)),
            dma((n_dom,)),
        ],
        compiler_params=pltpu.CompilerParams(collective_id=0, has_side_effects=True),
        name="wave_step",
    )(*given)
    return jnp.transpose(result, (1, 0, 2))


def solution(mesh):
    both = ("region", "dom")
    wide, flat = P(None, both), P(both)
    placed = (
        P(None, None, both),
        flat,
        wide,
        P(),
        P(),
        P(),
        P(),
        flat,
        wide,
        wide,
        wide,
        flat,
        flat,
    )
    n_region, n_dom = mesh.shape["region"], mesh.shape["dom"]

    def step(*args):
        return shards(n_region, n_dom, *args)

    return jax.shard_map(
        step,
        mesh=mesh,
        in_specs=placed,
        out_specs=P(None, None, both),
        check_vma=False,
    )
```

```python
import jax
import jax.numpy as jnp
import numpy as np
from jax import lax
from jax.experimental import pallas as pl
from jax.experimental.pallas import tpu as pltpu
from jax.sharding import PartitionSpec as P

MESH = pl.DeviceIdType.MESH
F32 = jnp.float32
BF16 = jnp.bfloat16
NODES = 10
FIRST_HALF = (0.5, 0.125, 1.0 / 48.0, 1.0 / 384.0)
SECOND_HALF = (0.5, 0.375, 7.0 / 48.0, 15.0 / 384.0)
MIGRANTS = 32
REG_FINE = 8
DOM_FINE = 4
FINE_LANES = 32
EARLY_LOADS = (3, 5, 13, 14, 15, 0, 1, 2, 9, 10)
LATE_LOADS = (4, 6, 7, 8, 11, 12, 16, 17, 18)


def iota(shape, dim):
    return lax.broadcasted_iota(jnp.int32, shape, dim)


def dot(a, b):
    return jnp.dot(a, b, preferred_element_type=F32)


def dot_nt(a, b):
    return lax.dot_general(a, b, (((1,), (1,)), ((), ())), preferred_element_type=F32)


def split_state(values):
    hi = values.astype(BF16)
    lo = (values - hi.astype(F32)).astype(BF16)
    return jnp.concatenate([hi, lo, hi], axis=0)


def pattern():
    pick = np.zeros((192, 32), np.float32)
    mask = np.zeros((192, 96), np.float32)
    columns = np.zeros((2, 16, 96), np.float32)
    for column in range(96):
        third, at = divmod(column, 32)
        if at < 3 * NODES:
            columns[third // 2, at % NODES, column] = 1.0

    def fill(row, source, var, sign):
        pick[row, source] = 1.0
        for third in range(3):
            first = 32 * third + NODES * var
            mask[row, first : first + NODES] = sign

    for which in range(2):
        for at in range(3 * NODES):
            node, part = at % NODES, at // NODES
            fill(32 * which + at, NODES * which + node, 1 if part == 0 else 0, -1.0)
        for node in range(NODES):
            fill(64 + 16 * which + node, NODES * which + node, 2, -1.0)
    for order in range(2):
        for face in range(3):
            for at in range(16):
                part, point = divmod(at, 4)
                source = 2 * NODES + 4 * face + (point if order else 3 - point)
                fill(96 + 48 * order + 16 * face + at, source, part % 3, 1.0)

    nodes = np.zeros((32, 16), np.float32)
    for row in range(3 * NODES):
        nodes[row, row % NODES] = 1.0
    places = np.zeros((2, 16, 288), np.float32)
    signs = np.zeros((32, 288), np.float32)
    for column in range(288):
        third, rest = divmod(column, 96)
        face, at = divmod(rest, 32)
        jump, at = divmod(at, 16)
        part, point = divmod(at, 4)
        places[third // 2, 4 * face + point, column] = 1.0
        for row in range(3 * NODES):
            var = row // NODES
            if jump:
                signs[row, column] = 1.0 if part == var else 0.0
            else:
                signs[row, column] = -1.0 if part in ((1, 2), (0,), (3,))[var] else 0.0
    return [jnp.asarray(x, BF16) for x in (pick, mask, columns, nodes, places, signs)]


def halves(values):
    hi = values.astype(BF16)
    return hi, (values - hi.astype(F32)).astype(BF16)


def spread_columns(values, columns_ref):
    hi, lo = halves(values)
    return (dot(hi, columns_ref[0]) + dot(lo, columns_ref[1])).astype(BF16)


def combine(slopes, alpha):
    a1, a2, a3, a4 = alpha
    both = a1 * slopes[0:32] + a2 * slopes[32:64]
    top = a3 * slopes[64:80] + a4 * slopes[80:96]
    return jnp.concatenate([both[0:16] + top, both[16:32]], axis=0)


def pick_columns(load, sources, block, lane, start):
    out = start
    for k in sources:
        found = jnp.take_along_axis(load(k), lane, axis=1)
        out = jnp.where(block == k, found, out)
    return out


def step_kernel(
    n_region,
    n_dom,
    elems,
    state_ref,
    depth_ref,
    metric_ref,
    diff_ref,
    stiff_ref,
    trace_ref,
    lift_ref,
    cluster_ref,
    code_ref,
    send_reg_ref,
    send_dom_ref,
    move_dom_ref,
    move_slot_ref,
    pick_ref,
    mask_ref,
    columns_ref,
    nodes_ref,
    places_ref,
    signs_ref,
    out_ref,
    *scratch,
):
    hbm_refs = (
        state_ref,
        depth_ref,
        metric_ref,
        diff_ref,
        stiff_ref,
        trace_ref,
        lift_ref,
        cluster_ref,
        code_ref,
        send_reg_ref,
        send_dom_ref,
        move_dom_ref,
        move_slot_ref,
        pick_ref,
        mask_ref,
        columns_ref,
        nodes_ref,
        places_ref,
        signs_ref,
    )
    step_body(
        n_region, n_dom, elems, hbm_refs, out_ref, scratch[: len(hbm_refs)], *scratch[len(hbm_refs) :]
    )


def step_body(
    n_region,
    n_dom,
    elems,
    hbm_refs,
    out_ref,
    local_refs,
    in_sem,
    ready,
    first_ops,
    second_ops,
    lift_ops,
    dense,
    tab_a,
    tab_b,
    tab_c,
    beyond,
    out_reg,
    out_dom,
    in_reg,
    in_dom,
    out_fine,
    in_fine,
    land_out,
    land_in,
    tile_out,
    tile_in,
    ss_reg,
    rs_reg,
    ss_dom,
    rs_dom,
    ss_fine,
    rs_fine,
    ss_land,
    rs_land,
    ss_tile,
    rs_tile,
):
    r = lax.axis_index("region")
    d = lax.axis_index("dom")
    blocks = elems // 128
    has_low = r > 0
    has_high = r < n_region - 1
    dom_low = d > 0
    dom_high = d < n_dom - 1
    sides = (
        (has_high, {"region": r + 1}, 1, 0),
        (has_low, {"region": r - 1}, 0, 1),
        (dom_high, {"dom": d + 1}, 1, 0),
        (dom_low, {"dom": d - 1}, 0, 1),
    )
    comes = (has_low, has_high, dom_low, dom_high)

    loads = [
        pltpu.make_async_copy(src, dst, in_sem.at[i])
        for i, (src, dst) in enumerate(zip(hbm_refs, local_refs))
    ]
    barrier = pltpu.get_barrier_semaphore()

    def ring(k):
        return {"dom": lax.rem(d + k + n_dom, n_dom)}

    for i in EARLY_LOADS:
        loads[i].start()
    for exists, device, _, _ in sides[:2]:

        @pl.when(exists)
        def _():
            pl.semaphore_signal(barrier, inc=1, device_id=device, device_id_type=MESH)

    for k in (1, -1):
        pl.semaphore_signal(barrier, inc=1, device_id=ring(k), device_id_type=MESH)
    for i in LATE_LOADS:
        loads[i].start()

    def announce(stage, reach):
        for k in (reach, -reach):
            pl.semaphore_signal(
                ready.at[stage], inc=1, device_id=ring(k), device_id_type=MESH
            )

    (
        state_ref,
        depth_ref,
        metric_ref,
        diff_ref,
        stiff_ref,
        trace_ref,
        lift_ref,
        cluster_ref,
        code_ref,
        send_reg_ref,
        send_dom_ref,
        move_dom_ref,
        move_slot_ref,
        pick_ref,
        mask_ref,
        columns_ref,
        nodes_ref,
        places_ref,
        signs_ref,
    ) = local_refs
    first_ops[...] = jnp.zeros((32, 16), F32)
    second_ops[...] = jnp.zeros((32, 16), F32)
    lift_ops[...] = jnp.zeros((16, 16), F32)
    for i in EARLY_LOADS:
        loads[i].wait()

    dense[30:32, :] = jnp.zeros((2, elems), F32)
    for v in range(3):
        dense[NODES * v : NODES * (v + 1), :] = state_ref[:, v, :]
    state = dense[...]
    depth = depth_ref[...]
    m0, m1, m2, m3 = (metric_ref[i : i + 1, :] for i in range(4))

    row = iota((32, elems), 0)
    a1 = jnp.where(row < 10, m0, jnp.where(row < 20, depth * m0, depth * m2))
    a2 = jnp.where(row < 10, m1, jnp.where(row < 20, depth * m1, depth * m3))
    top = row[0:16] < 10
    a3 = jnp.where(top, m2, 0.0)
    a4 = jnp.where(top, m3, 0.0)
    alpha = (a1, a2, a3, a4)

    for a in range(2):
        first_ops[NODES * a : NODES * (a + 1), 0:NODES] = diff_ref[:, a, :]
    for f in range(3):
        first_ops[2 * NODES + 4 * f : 2 * NODES + 4 * f + 4, 0:NODES] = trace_ref[f]
    wide = dot(pick_ref[...], spread_columns(first_ops[...], columns_ref)).astype(BF16)
    wide = wide * mask_ref[...]
    slope, traces = wide[0:96], wide[96:192]

    def series_of(values):
        series = [values]
        for _ in range(3):
            series.append(combine(dot(slope, split_state(series[-1])), alpha))
        return series

    def integrate(series, factors):
        summed = factors[0] * series[0]
        for factor, member in zip(factors[1:], series[1:]):
            summed = summed + factor * member
        return summed

    series = series_of(state)
    early = integrate(series, FIRST_HALF)
    early_split = split_state(early)
    tab_a[0:48] = dot(traces[0:48], early_split)

    def source(table):
        def load(k):
            f, b = divmod(k, blocks)
            return table[16 * f : 16 * f + 16, 128 * b : 128 * b + 128]

        return load

    def spread(vector):
        return jnp.broadcast_to(vector, (16, 128))

    own = range(3 * blocks)

    def gather_sends(which, table, copies):
        for i, (exists, _, copy) in enumerate(copies):
            lane_row = sides[i][2]
            if i < 2:
                for b in range(2):
                    index = spread(send_reg_ref[lane_row : lane_row + 1, 128 * b : 128 * b + 128])
                    out_reg[which, lane_row, b] = pick_columns(
                        source(table), own, index >> 7, index & 127, jnp.zeros((16, 128), F32)
                    )
            else:
                index = spread(send_dom_ref[lane_row : lane_row + 1, :])
                out_dom[which, lane_row] = pick_columns(
                    source(table), own, index >> 7, index & 127, jnp.zeros((16, 128), F32)
                )
            pl.when(exists)(copy.start)

    def copies_a(which):
        copies = []
        for i, (exists, device, lane_row, at) in enumerate(sides):
            regional = i < 2
            copies.append(
                (
                    exists,
                    comes[2 * (i // 2) + at],
                    pltpu.make_async_remote_copy(
                        src_ref=(out_reg if regional else out_dom).at[which, lane_row],
                        dst_ref=(in_reg if regional else in_dom).at[which, at],
                        send_sem=(ss_reg if regional else ss_dom).at[which, at],
                        recv_sem=(rs_reg if regional else rs_dom).at[which, at],
                        device_id=device,
                        device_id_type=MESH,
                    ),
                )
            )
        return copies

    def start(copies):
        for exists, _, copy in copies:
            pl.when(exists)(copy.start)

    def wait_recv(copies):
        for _, arrives, copy in copies:
            pl.when(arrives)(copy.wait_recv)

    def wait_send(copies):
        for exists, _, copy in copies:
            pl.when(exists)(copy.wait_send)

    first_copies = copies_a(0)
    late_copies = copies_a(1)
    pl.semaphore_wait(barrier, 2 + has_low.astype(jnp.int32) + has_high.astype(jnp.int32))
    announce(0, 1)
    gather_sends(0, tab_a, first_copies)

    later = integrate(series, SECOND_HALF)
    tab_b[...] = dot(traces[0:48], split_state(later))
    gather_sends(1, tab_b, late_copies)

    for i in range(2):

        @pl.when(jnp.logical_not(comes[i]))
        def _():
            in_reg[:, i] = jnp.zeros(in_reg.shape[0:1] + in_reg.shape[2:], F32)

        @pl.when(jnp.logical_not(comes[2 + i]))
        def _():
            in_dom[:, i] = jnp.zeros(in_dom.shape[0:1] + in_dom.shape[2:], F32)

    for i in range(4):

        @pl.when(jnp.logical_not(comes[i]))
        def _():
            in_fine[i] = jnp.zeros((8, 128), F32)

    for i in LATE_LOADS:
        loads[i].wait()
    tab_a[48:96] = dot(traces[48:96], early_split)
    for a in range(2):
        second_ops[NODES * a : NODES * (a + 1), 0:NODES] = stiff_ref[:, a, :]
    stiff = dot(pick_ref[0:96], spread_columns(second_ops[...], columns_ref)).astype(BF16)
    stiff = -(stiff * mask_ref[0:96])
    for f in range(3):
        lift_ops[4 * f : 4 * f + 4, 0:NODES] = lift_ref[f]
    hi, lo = halves(lift_ops[...])
    lift = dot(dot_nt(nodes_ref[...], hi).astype(BF16), places_ref[0])
    lift = lift + dot(dot_nt(nodes_ref[...], lo).astype(BF16), places_ref[1])
    lift = lift.astype(BF16) * signs_ref[...]
    half_x = (-m1, m0 + m1, -m0)
    half_y = (-m3, m2 + m3, -m2)
    root = jnp.sqrt(depth)
    rows16 = iota((16, elems), 0)
    centre_by, jump_by = [], []
    for f in range(3):
        hx, hy = half_x[f], half_y[f]
        centre_by.append(
            jnp.where(
                rows16 < 4,
                depth * hx,
                jnp.where(rows16 < 8, hx, jnp.where(rows16 < 12, hy, depth * hy)),
            )
        )
        jump_by.append(root * jnp.sqrt(hx * hx + hy * hy))
    mirror = jnp.where((iota((16, 128), 0) >= 4) & (iota((16, 128), 0) < 12), -1.0, 1.0)
    first_code = 3 * elems
    regional = 2 * send_reg_ref.shape[1]

    def code_of(f, b):
        return spread(code_ref[f : f + 1, 128 * b : 128 * b + 128])

    def local_part(table):
        for f in range(3):
            for b in range(blocks):
                code = code_of(f, b)
                wall = mirror * table[48 + 16 * f : 64 + 16 * f, 128 * b : 128 * b + 128]
                beyond[f, b] = pick_columns(source(table), own, code >> 7, code & 127, wall)

    def remote_part(which):
        def load(k):
            k = k - 3 * blocks
            if k < 4:
                return in_reg[which, k // 2, k % 2]
            return in_dom[which, k - 4]

        for f in range(3):
            for b in range(blocks):
                code = code_of(f, b)
                beyond[f, b] = pick_columns(
                    load,
                    range(3 * blocks, 3 * blocks + 6),
                    code >> 7,
                    code & 127,
                    beyond[f, b],
                )

    def fine_column(code):
        slot = code - first_code
        reg = slot & 255
        from_reg = jnp.where(
            (slot >= 0) & (slot < regional) & (reg < REG_FINE), (slot >> 8) * REG_FINE + reg, -1
        )
        past = slot - regional
        dom = past & 127
        return jnp.where(
            (past >= 0) & (past < 256) & (dom < DOM_FINE),
            2 * REG_FINE + (past >> 7) * DOM_FINE + dom,
            from_reg,
        )

    def increment(values_split, table):
        volume = combine(dot(stiff, values_split), alpha)
        parts = []
        for f in range(3):
            outside = jnp.concatenate([beyond[f, b] for b in range(blocks)], axis=1)
            inside = table[48 + 16 * f : 64 + 16 * f, :]
            parts.append(centre_by[f] * (outside + inside))
            parts.append(jump_by[f] * (outside - inside))
        return volume + dot(lift, split_state(jnp.concatenate(parts, axis=0)))

    local_part(tab_a)
    pl.semaphore_wait(ready.at[0], 2)
    announce(1, 2)
    nearest = sorted(range(1, n_dom), key=lambda k: min(k, n_dom - k))
    def peer_copies(src, dst, ss, rs):
        return {
            k: pltpu.make_async_remote_copy(
                src_ref=src.at[k],
                dst_ref=dst.at[k],
                send_sem=ss.at[k],
                recv_sem=rs.at[k],
                device_id={"dom": lax.rem(d + k, n_dom)},
                device_id_type=MESH,
            )
            for k in range(1, n_dom)
        }

    wait_recv(first_copies)
    remote_part(0)
    midway = state + increment(early_split, tab_a)
    fine = integrate(series_of(midway), FIRST_HALF)
    second = jnp.where(cluster_ref[...] == 0, fine, later)
    second_split = split_state(second)
    tab_c[0:48] = dot(traces[0:48], second_split)

    lane = iota((1, 128), 1)
    wanted = jnp.where(
        lane < REG_FINE,
        send_reg_ref[1:2, 0:128],
        jnp.where(
            lane < 2 * REG_FINE,
            pltpu.roll(send_reg_ref[0:1, 0:128], REG_FINE, 1),
            jnp.where(
                lane < 2 * REG_FINE + DOM_FINE,
                pltpu.roll(send_dom_ref[1:2, :], 2 * REG_FINE, 1),
                pltpu.roll(send_dom_ref[0:1, :], 2 * REG_FINE + DOM_FINE, 1),
            ),
        ),
    )
    wanted = spread(wanted)
    block = pick_columns(
        source(tab_c), own, wanted >> 7, wanted & 127, jnp.zeros((16, 128), F32)
    )
    lane8 = iota((8, 128), 1)
    out_fine[...] = jnp.where(lane8 < FINE_LANES, block[0:8], pltpu.roll(block[8:16], FINE_LANES, 1))
    fine_copies = []
    for i, (exists, device, _, at) in enumerate(sides):
        fine_copies.append(
            (
                exists,
                comes[2 * (i // 2) + at],
                pltpu.make_async_remote_copy(
                    src_ref=out_fine,
                    dst_ref=in_fine.at[i],
                    send_sem=ss_fine.at[i],
                    recv_sem=rs_fine.at[i],
                    device_id=device,
                    device_id_type=MESH,
                ),
            )
        )
    start(fine_copies)
    pl.semaphore_wait(ready.at[1], 2)
    announce(2, 2)

    lanes = iota((1, elems), 1)
    offset = move_dom_ref[...] - d
    offset = jnp.where(offset < 0, offset + n_dom, offset)
    chosen = jnp.where(iota((16, elems), 0) == offset, 1.0, 0.0)
    before = jnp.where(iota((elems, elems), 0) < iota((elems, elems), 1), 1.0, 0.0).astype(BF16)
    rank = jnp.sum(chosen * dot(chosen.astype(BF16), before), axis=0, keepdims=True)
    slots = n_dom * MIGRANTS
    padded = 384 if slots <= 384 else 128 * (-(-slots // 128))
    position = jnp.where(offset == 0, -1, offset * MIGRANTS + rank.astype(jnp.int32))
    inverse = jnp.where(iota((padded, elems), 0) == position, 1.0, 0.0).astype(BF16)
    place = move_slot_ref[...]
    which_row = iota((8, elems), 0)
    facts = jnp.where(
        which_row == 0,
        lanes >> 1,
        jnp.where(
            which_row == 1, lanes & 1, jnp.where(which_row == 2, place >> 1, place & 1)
        ),
    )
    facts = jnp.where(which_row < 4, facts, 0).astype(F32).astype(BF16)
    found = dot_nt(facts, inverse).astype(jnp.int32)
    leaves = found[0:1] * 2 + found[1:2]
    lands = found[2:3] * 2 + found[3:4]
    for k in range(1, n_dom):
        land_out[k] = lands[:, 128 * (k // 4) : 128 * (k // 4) + 128]

    tab_c[48:96] = dot(traces[48:96], second_split)
    local_part(tab_c)
    wait_recv(late_copies)
    remote_part(1)
    columns = {}
    for f in range(3):
        for b in range(blocks):
            columns[f, b] = fine_column(code_of(f, b))
            beyond[f, b] = jnp.where(columns[f, b] >= 0, 0.0, beyond[f, b])
    dense[...] = midway + increment(second_split, tab_c)
    pl.semaphore_wait(ready.at[2], 2)
    land_copies = peer_copies(land_out, land_in, ss_land, rs_land)
    for k in nearest[::-1]:
        land_copies[k].start()
    wait_recv(fine_copies)
    at = lane8 & (FINE_LANES - 1)
    fresh = jnp.where(
        at < REG_FINE,
        in_fine[0],
        jnp.where(
            at < 2 * REG_FINE,
            in_fine[1],
            jnp.where(at < 2 * REG_FINE + DOM_FINE, in_fine[2], in_fine[3]),
        ),
    )
    parts = []
    for f in range(3):
        late = []
        for b in range(blocks):
            column = columns[f, b][0:8] & (FINE_LANES - 1)
            low = jnp.take_along_axis(fresh, column, axis=1)
            high = jnp.take_along_axis(fresh, column + FINE_LANES, axis=1)
            found = jnp.concatenate([low, high], axis=0)
            late.append(jnp.where(columns[f, b] >= 0, found, 0.0))
        late = jnp.concatenate(late, axis=1)
        parts.append(centre_by[f] * late)
        parts.append(jump_by[f] * late)
    dense[...] = dense[...] + dot(lift, split_state(jnp.concatenate(parts, axis=0)))

    def cell(g, b):
        return dense[8 * g : 8 * g + 8, 128 * b : 128 * b + 128]

    group = iota((8, 128), 1) >> 5
    tile_copies = peer_copies(tile_out, tile_in, ss_tile, rs_tile)
    packed = {}
    for q in range(padded // 128):
        index = jnp.broadcast_to(leaves[:, 128 * q : 128 * q + 128], (8, 128))
        for g in range(4):
            packed[g, q] = pick_columns(
                lambda b: cell(g, b), range(blocks), index >> 7, index & 127, jnp.zeros((8, 128), F32)
            )
    for k in nearest[::-1]:
        tile = jnp.zeros((8, 128), F32)
        for g in range(4):
            shift = (32 * (g - (k & 3))) % 128
            moved = packed[g, k // 4]
            if shift:
                moved = pltpu.roll(moved, shift, 1)
            tile = jnp.where(group == g, moved, tile)
        tile_out[k] = tile
    for target in range(n_dom):

        @pl.when(target != d)
        def _():
            k = lax.rem(target - d + n_dom, n_dom)
            pltpu.make_async_remote_copy(
                src_ref=tile_out.at[k],
                dst_ref=tile_in.at[k],
                send_sem=ss_tile.at[k],
                recv_sem=rs_tile.at[k],
                device_id={"dom": target},
                device_id_type=MESH,
            ).start()

    for k in range(1, n_dom):
        land_copies[k].wait_recv()
    kk = iota((1, 128), 1)
    stack = []
    for q in range(padded // 128):
        row_q = jnp.full((1, 128), -1, jnp.int32)
        for k in range(4 * q, min(4 * q + 4, n_dom)):
            if k > 0:
                row_q = jnp.where((kk >> 5) == (k & 3), land_in[k], row_q)
        stack.append(row_q)
    places = jnp.concatenate(stack, axis=1)
    comes_here = jnp.where(iota((elems, padded), 0) == places, 1.0, 0.0).astype(BF16)
    column = iota((8, padded), 1)
    row8 = iota((8, padded), 0)
    facts = jnp.where(row8 == 0, column >> 1, jnp.where(row8 == 1, column & 1, 1))
    found = dot_nt(facts.astype(F32).astype(BF16), comes_here).astype(jnp.int32)
    origin = jnp.where(found[2:3] > 0, found[0:1] * 2 + found[1:2], -1)

    wait_send(first_copies)
    wait_send(late_copies)
    wait_send(fine_copies)
    for k in range(1, n_dom):
        land_copies[k].wait_send()
        tile_copies[k].wait_send()
    result = {(g, b): cell(g, b) for g in range(4) for b in range(blocks)}
    for k in nearest:
        tile_copies[k].wait_recv()
        tile = tile_in[k]
        for b in range(blocks):
            index = jnp.broadcast_to(origin[:, 128 * b : 128 * b + 128], (8, 128))
            here = (index >> 5) == k
            for g in range(4):
                found = jnp.take_along_axis(tile, (index & 31) + 32 * g, axis=1)
                result[g, b] = jnp.where(here, found, result[g, b])
    for g in range(4):
        for b in range(blocks):
            dense[8 * g : 8 * g + 8, 128 * b : 128 * b + 128] = result[g, b]
    for v in range(3):
        out_ref[:, v, :] = dense[NODES * v : NODES * (v + 1), :]


def shards(n_region, n_dom, *args):
    (
        water_state,
        water_depth,
        metric,
        diff_ops,
        stiff_ops,
        trace_ops,
        lift_ops,
        cluster,
        face_code,
        send_region,
        send_dom,
        move_dom,
        move_slot,
    ) = args
    elems = water_state.shape[2]
    blocks = elems // 128
    vmem = pl.BlockSpec(memory_space=pltpu.VMEM)
    dma = pltpu.SemaphoreType.DMA

    def kernel(*refs):
        step_kernel(n_region, n_dom, elems, *refs)

    given = (
        jnp.transpose(water_state, (1, 0, 2)),
        water_depth.reshape(1, elems),
        metric,
        jnp.transpose(diff_ops, (1, 0, 2)),
        jnp.transpose(stiff_ops, (1, 0, 2)),
        trace_ops,
        jnp.transpose(lift_ops, (0, 2, 1)),
        cluster.reshape(1, elems),
        face_code,
        send_region,
        send_dom,
        move_dom.reshape(1, elems),
        move_slot.reshape(1, elems),
        *pattern(),
    )
    result = pl.pallas_call(
        kernel,
        out_shape=pltpu.VMEM((NODES, 3, elems), F32),
        in_specs=[pl.BlockSpec(memory_space=pl.ANY)] * len(given),
        out_specs=vmem,
        scratch_shapes=[pltpu.VMEM(x.shape, x.dtype) for x in given]
        + [
            dma((len(given),)),
            pltpu.SemaphoreType.REGULAR((3,)),
            pltpu.VMEM((32, 16), F32),
            pltpu.VMEM((32, 16), F32),
            pltpu.VMEM((16, 16), F32),
            pltpu.VMEM((32, elems), F32),
            pltpu.VMEM((96, elems), F32),
            pltpu.VMEM((48, elems), F32),
            pltpu.VMEM((96, elems), F32),
            pltpu.VMEM((3, blocks, 16, 128), F32),
            pltpu.VMEM((2, 2, 2, 16, 128), F32),
            pltpu.VMEM((2, 2, 16, 128), F32),
            pltpu.VMEM((2, 2, 2, 16, 128), F32),
            pltpu.VMEM((2, 2, 16, 128), F32),
            pltpu.VMEM((8, 128), F32),
            pltpu.VMEM((4, 8, 128), F32),
            pltpu.VMEM((n_dom, 1, 128), jnp.int32),
            pltpu.VMEM((n_dom, 1, 128), jnp.int32),
            pltpu.VMEM((n_dom, 8, 128), F32),
            pltpu.VMEM((n_dom, 8, 128), F32),
            dma((2, 2)),
            dma((2, 2)),
            dma((2, 2)),
            dma((2, 2)),
            dma((4,)),
            dma((4,)),
            dma((n_dom,)),
            dma((n_dom,)),
            dma((n_dom,)),
            dma((n_dom,)),
        ],
        compiler_params=pltpu.CompilerParams(collective_id=0, has_side_effects=True),
        name="wave_step",
    )(*given)
    return jnp.transpose(result, (1, 0, 2))


def solution(mesh):
    both = ("region", "dom")
    wide, flat = P(None, both), P(both)
    placed = (
        P(None, None, both),
        flat,
        wide,
        P(),
        P(),
        P(),
        P(),
        flat,
        wide,
        wide,
        wide,
        flat,
        flat,
    )
    n_region, n_dom = mesh.shape["region"], mesh.shape["dom"]

    def step(*args):
        return shards(n_region, n_dom, *args)

    return jax.shard_map(
        step,
        mesh=mesh,
        in_specs=placed,
        out_specs=P(None, None, both),
        check_vma=False,
    )
```

```python
import jax
import jax.numpy as jnp
import numpy as np
from jax import lax
from jax.experimental import pallas as pl
from jax.experimental.pallas import tpu as pltpu
from jax.sharding import PartitionSpec as P

MESH = pl.DeviceIdType.MESH
F32 = jnp.float32
BF16 = jnp.bfloat16
NODES = 10
FIRST_HALF = (0.5, 0.125, 1.0 / 48.0, 1.0 / 384.0)
SECOND_HALF = (0.5, 0.375, 7.0 / 48.0, 15.0 / 384.0)
MIGRANTS = 32
REG_FINE = 8
DOM_FINE = 4
FINE_LANES = 32
EARLY_LOADS = (3, 5, 13, 14, 15, 0, 1, 2, 9, 10)
LATE_LOADS = (4, 6, 7, 8, 11, 12, 16, 17, 18)


def iota(shape, dim):
    return lax.broadcasted_iota(jnp.int32, shape, dim)


def dot(a, b):
    return jnp.dot(a, b, preferred_element_type=F32)


def dot_nt(a, b):
    return lax.dot_general(a, b, (((1,), (1,)), ((), ())), preferred_element_type=F32)


def split_state(values):
    hi = values.astype(BF16)
    lo = (values - hi.astype(F32)).astype(BF16)
    return jnp.concatenate([hi, lo, hi], axis=0)


def pattern():
    pick = np.zeros((192, 32), np.float32)
    mask = np.zeros((192, 96), np.float32)
    columns = np.zeros((2, 16, 96), np.float32)
    for column in range(96):
        third, at = divmod(column, 32)
        if at < 3 * NODES:
            columns[third // 2, at % NODES, column] = 1.0

    def fill(row, source, var, sign):
        pick[row, source] = 1.0
        for third in range(3):
            first = 32 * third + NODES * var
            mask[row, first : first + NODES] = sign

    for which in range(2):
        for at in range(3 * NODES):
            node, part = at % NODES, at // NODES
            fill(32 * which + at, NODES * which + node, 1 if part == 0 else 0, -1.0)
        for node in range(NODES):
            fill(64 + 16 * which + node, NODES * which + node, 2, -1.0)
    for order in range(2):
        for face in range(3):
            for at in range(16):
                part, point = divmod(at, 4)
                source = 2 * NODES + 4 * face + (point if order else 3 - point)
                fill(96 + 48 * order + 16 * face + at, source, part % 3, 1.0)

    nodes = np.zeros((32, 16), np.float32)
    for row in range(3 * NODES):
        nodes[row, row % NODES] = 1.0
    places = np.zeros((2, 16, 288), np.float32)
    signs = np.zeros((32, 288), np.float32)
    for column in range(288):
        third, rest = divmod(column, 96)
        face, at = divmod(rest, 32)
        jump, at = divmod(at, 16)
        part, point = divmod(at, 4)
        places[third // 2, 4 * face + point, column] = 1.0
        for row in range(3 * NODES):
            var = row // NODES
            if jump:
                signs[row, column] = 1.0 if part == var else 0.0
            else:
                signs[row, column] = -1.0 if part in ((1, 2), (0,), (3,))[var] else 0.0
    return [jnp.asarray(x, BF16) for x in (pick, mask, columns, nodes, places, signs)]


def halves(values):
    hi = values.astype(BF16)
    return hi, (values - hi.astype(F32)).astype(BF16)


def spread_columns(values, columns_ref):
    hi, lo = halves(values)
    return (dot(hi, columns_ref[0]) + dot(lo, columns_ref[1])).astype(BF16)


def combine(slopes, alpha):
    a1, a2, a3, a4 = alpha
    both = a1 * slopes[0:32] + a2 * slopes[32:64]
    top = a3 * slopes[64:80] + a4 * slopes[80:96]
    return jnp.concatenate([both[0:16] + top, both[16:32]], axis=0)


def alpha_of(depth, m0, m1, m2, m3):
    row = iota((32, depth.shape[1]), 0)
    top = row[0:16] < NODES
    return (
        jnp.where(row < 10, m0, jnp.where(row < 20, depth * m0, depth * m2)),
        jnp.where(row < 10, m1, jnp.where(row < 20, depth * m1, depth * m3)),
        jnp.where(top, m2, 0.0),
        jnp.where(top, m3, 0.0),
    )


def flux_factors(depth, m0, m1, m2, m3):
    rows = iota((16, depth.shape[1]), 0)
    root = jnp.sqrt(depth)
    factors = []
    for hx, hy in ((-m1, -m3), (m0 + m1, m2 + m3), (-m0, -m2)):
        centre = jnp.where(
            rows < 4,
            depth * hx,
            jnp.where(rows < 8, hx, jnp.where(rows < 12, hy, depth * hy)),
        )
        factors.append((centre, root * jnp.sqrt(hx * hx + hy * hy)))
    return factors


def lifted(lift, factors, sums, differences):
    parts = []
    for (centre, jump), added, taken in zip(factors, sums, differences):
        parts.append(centre * added)
        parts.append(jump * taken)
    return dot(lift, split_state(jnp.concatenate(parts, axis=0)))


def pick_columns(load, sources, block, lane, start):
    out = start
    for k in sources:
        found = jnp.take_along_axis(load(k), lane, axis=1)
        out = jnp.where(block == k, found, out)
    return out


def step_kernel(
    n_region,
    n_dom,
    elems,
    state_ref,
    depth_ref,
    metric_ref,
    diff_ref,
    stiff_ref,
    trace_ref,
    lift_ref,
    cluster_ref,
    code_ref,
    send_reg_ref,
    send_dom_ref,
    move_dom_ref,
    move_slot_ref,
    pick_ref,
    mask_ref,
    columns_ref,
    nodes_ref,
    places_ref,
    signs_ref,
    out_ref,
    *scratch,
):
    hbm_refs = (
        state_ref,
        depth_ref,
        metric_ref,
        diff_ref,
        stiff_ref,
        trace_ref,
        lift_ref,
        cluster_ref,
        code_ref,
        send_reg_ref,
        send_dom_ref,
        move_dom_ref,
        move_slot_ref,
        pick_ref,
        mask_ref,
        columns_ref,
        nodes_ref,
        places_ref,
        signs_ref,
    )
    step_body(
        n_region, n_dom, elems, hbm_refs, out_ref, scratch[: len(hbm_refs)], *scratch[len(hbm_refs) :]
    )


def step_body(
    n_region,
    n_dom,
    elems,
    hbm_refs,
    out_ref,
    local_refs,
    in_sem,
    ready,
    first_ops,
    second_ops,
    lift_ops,
    dense,
    base,
    geometry,
    tab_a,
    tab_b,
    tab_c,
    beyond,
    out_reg,
    out_dom,
    in_reg,
    in_dom,
    out_fine,
    in_fine,
    land_out,
    land_in,
    tile_out,
    tile_in,
    ss_reg,
    rs_reg,
    ss_dom,
    rs_dom,
    ss_fine,
    rs_fine,
    ss_land,
    rs_land,
    ss_tile,
    rs_tile,
):
    r = lax.axis_index("region")
    d = lax.axis_index("dom")
    blocks = elems // 128
    has_low = r > 0
    has_high = r < n_region - 1
    dom_low = d > 0
    dom_high = d < n_dom - 1
    sides = (
        (has_high, {"region": r + 1}, 1, 0),
        (has_low, {"region": r - 1}, 0, 1),
        (dom_high, {"dom": d + 1}, 1, 0),
        (dom_low, {"dom": d - 1}, 0, 1),
    )
    comes = (has_low, has_high, dom_low, dom_high)

    loads = [
        pltpu.make_async_copy(src, dst, in_sem.at[i])
        for i, (src, dst) in enumerate(zip(hbm_refs, local_refs))
    ]
    barrier = pltpu.get_barrier_semaphore()

    def ring(k):
        return {"dom": lax.rem(d + k + n_dom, n_dom)}

    for i in EARLY_LOADS:
        loads[i].start()
    for exists, device, _, _ in sides[:2]:

        @pl.when(exists)
        def _():
            pl.semaphore_signal(barrier, inc=1, device_id=device, device_id_type=MESH)

    for k in (1, -1):
        pl.semaphore_signal(barrier, inc=1, device_id=ring(k), device_id_type=MESH)
    for i in LATE_LOADS:
        loads[i].start()

    def announce(stage, reach):
        for k in (reach, -reach):
            pl.semaphore_signal(
                ready.at[stage], inc=1, device_id=ring(k), device_id_type=MESH
            )

    (
        state_ref,
        depth_ref,
        metric_ref,
        diff_ref,
        stiff_ref,
        trace_ref,
        lift_ref,
        cluster_ref,
        code_ref,
        send_reg_ref,
        send_dom_ref,
        move_dom_ref,
        move_slot_ref,
        pick_ref,
        mask_ref,
        columns_ref,
        nodes_ref,
        places_ref,
        signs_ref,
    ) = local_refs
    first_ops[...] = jnp.zeros((32, 16), F32)
    second_ops[...] = jnp.zeros((32, 16), F32)
    lift_ops[...] = jnp.zeros((16, 16), F32)
    for i in EARLY_LOADS:
        loads[i].wait()

    dense[30:32, :] = jnp.zeros((2, elems), F32)
    for v in range(3):
        dense[NODES * v : NODES * (v + 1), :] = state_ref[:, v, :]
    state = dense[...]
    depth = depth_ref[...]
    m0, m1, m2, m3 = (metric_ref[i : i + 1, :] for i in range(4))

    alpha = alpha_of(depth, m0, m1, m2, m3)

    for a in range(2):
        first_ops[NODES * a : NODES * (a + 1), 0:NODES] = diff_ref[:, a, :]
    for f in range(3):
        first_ops[2 * NODES + 4 * f : 2 * NODES + 4 * f + 4, 0:NODES] = trace_ref[f]
    wide = dot(pick_ref[...], spread_columns(first_ops[...], columns_ref)).astype(BF16)
    wide = wide * mask_ref[...]
    slope, traces = wide[0:96], wide[96:192]

    def series_of(values, alpha):
        series = [values]
        for _ in range(3):
            series.append(combine(dot(slope, split_state(series[-1])), alpha))
        return series

    def integrate(series, factors):
        summed = factors[0] * series[0]
        for factor, member in zip(factors[1:], series[1:]):
            summed = summed + factor * member
        return summed

    series = series_of(state, alpha)
    early = integrate(series, FIRST_HALF)
    early_split = split_state(early)
    tab_a[0:48] = dot(traces[0:48], early_split)

    def source(table):
        def load(k):
            f, b = divmod(k, blocks)
            return table[16 * f : 16 * f + 16, 128 * b : 128 * b + 128]

        return load

    def spread(vector):
        return jnp.broadcast_to(vector, (16, 128))

    own = range(3 * blocks)

    def gather_sends(which, table, copies):
        for i, (exists, _, copy) in enumerate(copies):
            lane_row = sides[i][2]
            if i < 2:
                for b in range(2):
                    index = spread(send_reg_ref[lane_row : lane_row + 1, 128 * b : 128 * b + 128])
                    out_reg[which, lane_row, b] = pick_columns(
                        source(table), own, index >> 7, index & 127, jnp.zeros((16, 128), F32)
                    )
            else:
                index = spread(send_dom_ref[lane_row : lane_row + 1, :])
                out_dom[which, lane_row] = pick_columns(
                    source(table), own, index >> 7, index & 127, jnp.zeros((16, 128), F32)
                )
            pl.when(exists)(copy.start)

    def copies_a(which):
        copies = []
        for i, (exists, device, lane_row, at) in enumerate(sides):
            regional = i < 2
            copies.append(
                (
                    exists,
                    comes[2 * (i // 2) + at],
                    pltpu.make_async_remote_copy(
                        src_ref=(out_reg if regional else out_dom).at[which, lane_row],
                        dst_ref=(in_reg if regional else in_dom).at[which, at],
                        send_sem=(ss_reg if regional else ss_dom).at[which, at],
                        recv_sem=(rs_reg if regional else rs_dom).at[which, at],
                        device_id=device,
                        device_id_type=MESH,
                    ),
                )
            )
        return copies

    def start(copies):
        for exists, _, copy in copies:
            pl.when(exists)(copy.start)

    def wait_recv(copies):
        for _, arrives, copy in copies:
            pl.when(arrives)(copy.wait_recv)

    def wait_send(copies):
        for exists, _, copy in copies:
            pl.when(exists)(copy.wait_send)

    first_copies = copies_a(0)
    late_copies = copies_a(1)
    pl.semaphore_wait(barrier, 2 + has_low.astype(jnp.int32) + has_high.astype(jnp.int32))
    announce(0, 1)
    gather_sends(0, tab_a, first_copies)

    later = integrate(series, SECOND_HALF)
    tab_b[...] = dot(traces[0:48], split_state(later))
    gather_sends(1, tab_b, late_copies)

    tile_in[0] = jnp.zeros((8, 128), F32)
    for i in range(2):

        @pl.when(jnp.logical_not(comes[i]))
        def _():
            in_reg[:, i] = jnp.zeros(in_reg.shape[0:1] + in_reg.shape[2:], F32)

        @pl.when(jnp.logical_not(comes[2 + i]))
        def _():
            in_dom[:, i] = jnp.zeros(in_dom.shape[0:1] + in_dom.shape[2:], F32)

    for i in range(4):

        @pl.when(jnp.logical_not(comes[i]))
        def _():
            in_fine[i] = jnp.zeros((8, 128), F32)

    for i in LATE_LOADS:
        loads[i].wait()
    tab_a[48:96] = dot(traces[48:96], early_split)
    for a in range(2):
        second_ops[NODES * a : NODES * (a + 1), 0:NODES] = stiff_ref[:, a, :]
    stiff = dot(pick_ref[0:96], spread_columns(second_ops[...], columns_ref)).astype(BF16)
    stiff = -(stiff * mask_ref[0:96])
    for f in range(3):
        lift_ops[4 * f : 4 * f + 4, 0:NODES] = lift_ref[f]
    hi, lo = halves(lift_ops[...])
    lift = dot(dot_nt(nodes_ref[...], hi).astype(BF16), places_ref[0])
    lift = lift + dot(dot_nt(nodes_ref[...], lo).astype(BF16), places_ref[1])
    lift = lift.astype(BF16) * signs_ref[...]
    factors = flux_factors(depth, m0, m1, m2, m3)
    mirror = jnp.where((iota((16, 128), 0) >= 4) & (iota((16, 128), 0) < 12), -1.0, 1.0)
    first_code = 3 * elems
    regional = 2 * send_reg_ref.shape[1]
    wall_code = first_code + regional + 2 * send_dom_ref.shape[1]
    remote = range(3 * blocks, 3 * blocks + 6)

    def code_of(f, b):
        return spread(code_ref[f : f + 1, 128 * b : 128 * b + 128])

    def local_part(table):
        for f in range(3):
            for b in range(blocks):
                code = code_of(f, b)
                wall = mirror * table[48 + 16 * f : 64 + 16 * f, 128 * b : 128 * b + 128]
                wall = jnp.where(code == wall_code, wall, 0.0)
                beyond[f, b] = pick_columns(source(table), own, code >> 7, code & 127, wall)

    def increment(values_split, table):
        volume = combine(dot(stiff, values_split), alpha)
        outside = [jnp.concatenate([beyond[f, b] for b in range(blocks)], axis=1) for f in range(3)]
        inside = [table[48 + 16 * f : 64 + 16 * f, :] for f in range(3)]
        return volume + lifted(
            lift,
            factors,
            [x + y for x, y in zip(outside, inside)],
            [x - y for x, y in zip(outside, inside)],
        )

    def fine_column(code):
        slot = code - first_code
        reg = slot & 255
        from_reg = jnp.where(
            (slot >= 0) & (slot < regional) & (reg < REG_FINE), (slot >> 8) * REG_FINE + reg, -1
        )
        past = slot - regional
        dom = past & 127
        return jnp.where(
            (past >= 0) & (past < 256) & (dom < DOM_FINE),
            2 * REG_FINE + (past >> 7) * DOM_FINE + dom,
            from_reg,
        )

    local_part(tab_a)
    base[...] = state + increment(early_split, tab_a)
    pl.semaphore_wait(ready.at[0], 2)
    announce(1, 2)
    nearest = sorted(range(1, n_dom), key=lambda k: min(k, n_dom - k))

    def peer_copies(src, dst, ss, rs):
        return {
            k: pltpu.make_async_remote_copy(
                src_ref=src.at[k],
                dst_ref=dst.at[k],
                send_sem=ss.at[k],
                recv_sem=rs.at[k],
                device_id={"dom": lax.rem(d + k, n_dom)},
                device_id_type=MESH,
            )
            for k in range(1, n_dom)
        }

    lanes = iota((1, elems), 1)
    offset = move_dom_ref[...] - d
    offset = jnp.where(offset < 0, offset + n_dom, offset)
    fine_row = 15
    is_fine = cluster_ref[...] == 0
    kind = iota((16, elems), 0)
    chosen = jnp.where(kind == offset, 1.0, 0.0)
    chosen = jnp.where(kind == fine_row, jnp.where(is_fine, 1.0, 0.0), chosen)
    before = jnp.where(iota((elems, elems), 0) < iota((elems, elems), 1), 1.0, 0.0).astype(BF16)
    ranks = dot(chosen.astype(BF16), before)
    rank = jnp.sum(jnp.where(kind < fine_row, chosen * ranks, 0.0), axis=0, keepdims=True)
    fine_rank = ranks[fine_row:].astype(jnp.int32)
    fine_position = jnp.where(is_fine, fine_rank, -1)
    slots = n_dom * MIGRANTS
    padded = 384 if slots <= 384 else 128 * (-(-slots // 128))
    position = jnp.where(offset == 0, -1, offset * MIGRANTS + rank.astype(jnp.int32))
    inverse = jnp.concatenate(
        [
            jnp.where(iota((padded, elems), 0) == position, 1.0, 0.0),
            jnp.where(iota((128, elems), 0) == fine_position, 1.0, 0.0),
        ],
        axis=0,
    ).astype(BF16)
    place = move_slot_ref[...]
    which_row = iota((8, elems), 0)
    facts = jnp.where(
        which_row == 0,
        lanes >> 1,
        jnp.where(
            which_row == 1, lanes & 1, jnp.where(which_row == 2, place >> 1, place & 1)
        ),
    )
    facts = jnp.where(which_row < 4, facts, 0).astype(F32).astype(BF16)
    found = dot_nt(facts, inverse).astype(jnp.int32)
    leaves = found[0:1] * 2 + found[1:2]
    lands = found[2:3] * 2 + found[3:4]
    fine_at = leaves[:, padded : padded + 128]
    for k in range(1, n_dom):
        land_out[k] = lands[:, 128 * (k // 4) : 128 * (k // 4) + 128]

    geometry[0:1] = depth
    geometry[1:5] = metric_ref[...]
    geometry[5:8] = code_ref[...].astype(F32)

    def squeeze(load, index):
        index = jnp.broadcast_to(index, (8, 128))
        return pick_columns(load, range(blocks), index >> 7, index & 127, jnp.zeros((8, 128), F32))

    def block_of(ref, g):
        return lambda b: ref[8 * g : 8 * g + 8, 128 * b : 128 * b + 128]

    fine_base = jnp.concatenate([squeeze(block_of(base, g), fine_at) for g in range(4)], axis=0)
    facts = squeeze(block_of(geometry, 0), fine_at)
    fine_geometry = [facts[i : i + 1] for i in range(5)]
    fine_alpha = alpha_of(*fine_geometry)
    fine_factors = flux_factors(*fine_geometry)
    fine_codes = [spread(facts[5 + f : 6 + f].astype(jnp.int32)) for f in range(3)]

    lane = iota((1, 128), 1)
    wanted = jnp.where(
        lane < REG_FINE,
        send_reg_ref[1:2, 0:128],
        jnp.where(
            lane < 2 * REG_FINE,
            pltpu.roll(send_reg_ref[0:1, 0:128], REG_FINE, 1),
            jnp.where(
                lane < 2 * REG_FINE + DOM_FINE,
                pltpu.roll(send_dom_ref[1:2, :], 2 * REG_FINE, 1),
                pltpu.roll(send_dom_ref[0:1, :], 2 * REG_FINE + DOM_FINE, 1),
            ),
        ),
    )
    wanted_face = (wanted >= elems).astype(jnp.int32) + (wanted >= 2 * elems).astype(jnp.int32)
    wanted_face = spread(wanted_face)
    rank_rows = jnp.broadcast_to(fine_rank.astype(F32), (8, elems))
    wanted_at = squeeze(
        lambda b: rank_rows[:, 128 * b : 128 * b + 128], wanted - elems * wanted_face[0:1]
    ).astype(jnp.int32)
    wanted_at = spread(wanted_at[0:1]) & 127

    wait_recv(first_copies)

    def early_slot(k):
        k = k - 3 * blocks
        return in_reg[0, k // 2, k % 2] if k < 4 else in_dom[0, k - 4]

    outer = [
        pick_columns(early_slot, remote, code >> 7, code & 127, jnp.zeros((16, 128), F32))
        for code in fine_codes
    ]
    fine_midway = fine_base + lifted(lift, fine_factors, outer, outer)
    fine = integrate(series_of(fine_midway, fine_alpha), FIRST_HALF)
    fine_table = dot(traces[0:48], split_state(fine))

    block = jnp.zeros((16, 128), F32)
    for f in range(3):
        found = jnp.take_along_axis(fine_table[16 * f : 16 * f + 16], wanted_at, axis=1)
        block = jnp.where(wanted_face == f, found, block)
    lane8 = iota((8, 128), 1)
    out_fine[...] = jnp.where(lane8 < FINE_LANES, block[0:8], pltpu.roll(block[8:16], FINE_LANES, 1))
    fine_copies = []
    for i, (exists, device, _, at) in enumerate(sides):
        fine_copies.append(
            (
                exists,
                comes[2 * (i // 2) + at],
                pltpu.make_async_remote_copy(
                    src_ref=out_fine,
                    dst_ref=in_fine.at[i],
                    send_sem=ss_fine.at[i],
                    recv_sem=rs_fine.at[i],
                    device_id=device,
                    device_id_type=MESH,
                ),
            )
        )
    start(fine_copies)
    pl.semaphore_wait(ready.at[1], 2)
    announce(2, 2)

    for b in range(blocks):
        columns = slice(128 * b, 128 * b + 128)
        index = jnp.broadcast_to(fine_rank[:, columns] & 127, (8, 128))
        mine = jnp.broadcast_to(cluster_ref[:, columns], (8, 128)) == 0
        for g in range(4):
            rows = slice(8 * g, 8 * g + 8)
            found = jnp.take_along_axis(fine[rows], index, axis=1)
            dense[rows, columns] = jnp.where(mine, found, later[rows, columns])
    second_split = split_state(dense[...])
    tab_c[...] = dot(traces, second_split)
    local_part(tab_c)
    wait_recv(late_copies)

    lane16 = iota((16, 128), 1)
    both = []
    for k in range(6):
        first = early_slot(3 * blocks + k)
        if k < 4:
            coarse = in_reg[1, k // 2, k % 2]
            if k % 2 == 0:
                coarse = jnp.where(lane16 < REG_FINE, 0.0, coarse)
        else:
            coarse = jnp.where(lane16 < DOM_FINE, 0.0, in_dom[1, k - 4])
        both.append(first + coarse)
    columns = {}
    for f in range(3):
        for b in range(blocks):
            code = code_of(f, b)
            columns[f, b] = fine_column(code)
            beyond[f, b] = pick_columns(
                lambda k: both[k - 3 * blocks], remote, code >> 7, code & 127, beyond[f, b]
            )
    dense[...] = base[...] + increment(second_split, tab_c)
    pl.semaphore_wait(ready.at[2], 2)
    land_copies = peer_copies(land_out, land_in, ss_land, rs_land)
    for k in nearest[::-1]:
        land_copies[k].start()
    wait_recv(fine_copies)
    at = lane8 & (FINE_LANES - 1)
    fresh = jnp.where(
        at < REG_FINE,
        in_fine[0],
        jnp.where(
            at < 2 * REG_FINE,
            in_fine[1],
            jnp.where(at < 2 * REG_FINE + DOM_FINE, in_fine[2], in_fine[3]),
        ),
    )
    outer = []
    for f in range(3):
        late = []
        for b in range(blocks):
            column = columns[f, b][0:8] & (FINE_LANES - 1)
            low = jnp.take_along_axis(fresh, column, axis=1)
            high = jnp.take_along_axis(fresh, column + FINE_LANES, axis=1)
            found = jnp.concatenate([low, high], axis=0)
            late.append(jnp.where(columns[f, b] >= 0, found, 0.0))
        outer.append(jnp.concatenate(late, axis=1))
    dense[...] = dense[...] + lifted(lift, factors, outer, outer)

    def cell(g, b):
        return dense[8 * g : 8 * g + 8, 128 * b : 128 * b + 128]

    group = iota((8, 128), 1) >> 5
    tile_copies = peer_copies(tile_out, tile_in, ss_tile, rs_tile)
    packed = {}
    for q in range(padded // 128):
        index = jnp.broadcast_to(leaves[:, 128 * q : 128 * q + 128], (8, 128))
        for g in range(4):
            packed[g, q] = pick_columns(
                lambda b: cell(g, b), range(blocks), index >> 7, index & 127, jnp.zeros((8, 128), F32)
            )
    for k in nearest[::-1]:
        tile = jnp.zeros((8, 128), F32)
        for g in range(4):
            shift = (32 * (g - (k & 3))) % 128
            moved = packed[g, k // 4]
            if shift:
                moved = pltpu.roll(moved, shift, 1)
            tile = jnp.where(group == g, moved, tile)
        tile_out[k] = tile
        tile_copies[k].start()
    for k in range(1, n_dom):
        land_copies[k].wait_recv()
    kk = iota((1, 128), 1)
    stack = []
    for q in range(padded // 128):
        row_q = jnp.full((1, 128), -1, jnp.int32)
        for k in range(4 * q, min(4 * q + 4, n_dom)):
            if k > 0:
                row_q = jnp.where((kk >> 5) == (k & 3), land_in[k], row_q)
        stack.append(row_q)
    places = jnp.concatenate(stack, axis=1)
    comes_here = jnp.where(iota((elems, padded), 0) == places, 1.0, 0.0).astype(BF16)
    column = iota((8, padded), 1)
    row8 = iota((8, padded), 0)
    facts = jnp.where(row8 == 0, column >> 1, jnp.where(row8 == 1, column & 1, 1))
    found = dot_nt(facts.astype(F32).astype(BF16), comes_here).astype(jnp.int32)
    origin = jnp.where(found[2:3] > 0, found[0:1] * 2 + found[1:2], -1)

    wait_send(first_copies)
    wait_send(late_copies)
    wait_send(fine_copies)
    for k in range(1, n_dom):
        land_copies[k].wait_send()
        tile_copies[k].wait_send()
    result = {(g, b): cell(g, b) for g in range(4) for b in range(blocks)}
    half = n_dom // 2
    for sender in [*range(half), *reversed(range(half, n_dom))]:
        k = lax.rem(d - sender + n_dom, n_dom)

        @pl.when(sender != d)
        def _():
            pltpu.make_async_remote_copy(
                src_ref=tile_out.at[k],
                dst_ref=tile_in.at[k],
                send_sem=ss_tile.at[k],
                recv_sem=rs_tile.at[k],
                device_id={"dom": sender},
                device_id_type=MESH,
            ).wait_recv()

        tile = tile_in[k]
        for b in range(blocks):
            index = jnp.broadcast_to(origin[:, 128 * b : 128 * b + 128], (8, 128))
            here = (index >> 5) == k
            for g in range(4):
                found = jnp.take_along_axis(tile, (index & 31) + 32 * g, axis=1)
                result[g, b] = jnp.where(here, found, result[g, b])
    for g in range(4):
        for b in range(blocks):
            dense[8 * g : 8 * g + 8, 128 * b : 128 * b + 128] = result[g, b]
    for v in range(3):
        out_ref[:, v, :] = dense[NODES * v : NODES * (v + 1), :]


def shards(n_region, n_dom, *args):
    (
        water_state,
        water_depth,
        metric,
        diff_ops,
        stiff_ops,
        trace_ops,
        lift_ops,
        cluster,
        face_code,
        send_region,
        send_dom,
        move_dom,
        move_slot,
    ) = args
    elems = water_state.shape[2]
    blocks = elems // 128
    vmem = pl.BlockSpec(memory_space=pltpu.VMEM)
    dma = pltpu.SemaphoreType.DMA

    def kernel(*refs):
        step_kernel(n_region, n_dom, elems, *refs)

    given = (
        jnp.transpose(water_state, (1, 0, 2)),
        water_depth.reshape(1, elems),
        metric,
        jnp.transpose(diff_ops, (1, 0, 2)),
        jnp.transpose(stiff_ops, (1, 0, 2)),
        trace_ops,
        jnp.transpose(lift_ops, (0, 2, 1)),
        cluster.reshape(1, elems),
        face_code,
        send_region,
        send_dom,
        move_dom.reshape(1, elems),
        move_slot.reshape(1, elems),
        *pattern(),
    )
    result = pl.pallas_call(
        kernel,
        out_shape=pltpu.VMEM((NODES, 3, elems), F32),
        in_specs=[pl.BlockSpec(memory_space=pl.ANY)] * len(given),
        out_specs=vmem,
        scratch_shapes=[pltpu.VMEM(x.shape, x.dtype) for x in given]
        + [
            dma((len(given),)),
            pltpu.SemaphoreType.REGULAR((3,)),
            pltpu.VMEM((32, 16), F32),
            pltpu.VMEM((32, 16), F32),
            pltpu.VMEM((16, 16), F32),
            pltpu.VMEM((32, elems), F32),
            pltpu.VMEM((32, elems), F32),
            pltpu.VMEM((8, elems), F32),
            pltpu.VMEM((96, elems), F32),
            pltpu.VMEM((48, elems), F32),
            pltpu.VMEM((96, elems), F32),
            pltpu.VMEM((3, blocks, 16, 128), F32),
            pltpu.VMEM((2, 2, 2, 16, 128), F32),
            pltpu.VMEM((2, 2, 16, 128), F32),
            pltpu.VMEM((2, 2, 2, 16, 128), F32),
            pltpu.VMEM((2, 2, 16, 128), F32),
            pltpu.VMEM((8, 128), F32),
            pltpu.VMEM((4, 8, 128), F32),
            pltpu.VMEM((n_dom, 1, 128), jnp.int32),
            pltpu.VMEM((n_dom, 1, 128), jnp.int32),
            pltpu.VMEM((n_dom, 8, 128), F32),
            pltpu.VMEM((n_dom, 8, 128), F32),
            dma((2, 2)),
            dma((2, 2)),
            dma((2, 2)),
            dma((2, 2)),
            dma((4,)),
            dma((4,)),
            dma((n_dom,)),
            dma((n_dom,)),
            dma((n_dom,)),
            dma((n_dom,)),
        ],
        compiler_params=pltpu.CompilerParams(collective_id=0, has_side_effects=True),
        name="wave_step",
    )(*given)
    return jnp.transpose(result, (1, 0, 2))


def solution(mesh):
    both = ("region", "dom")
    wide, flat = P(None, both), P(both)
    placed = (
        P(None, None, both),
        flat,
        wide,
        P(),
        P(),
        P(),
        P(),
        flat,
        wide,
        wide,
        wide,
        flat,
        flat,
    )
    n_region, n_dom = mesh.shape["region"], mesh.shape["dom"]

    def step(*args):
        return shards(n_region, n_dom, *args)

    return jax.shard_map(
        step,
        mesh=mesh,
        in_specs=placed,
        out_specs=P(None, None, both),
        check_vma=False,
    )
```

```python
import jax
import jax.numpy as jnp
import numpy as np
from jax import lax
from jax.experimental import pallas as pl
from jax.experimental.pallas import tpu as pltpu
from jax.sharding import PartitionSpec as P

MESH = pl.DeviceIdType.MESH
F32 = jnp.float32
BF16 = jnp.bfloat16
NODES = 10
FIRST_HALF = (0.5, 0.125, 1.0 / 48.0, 1.0 / 384.0)
SECOND_HALF = (0.5, 0.375, 7.0 / 48.0, 15.0 / 384.0)
MIGRANTS = 32
REG_FINE = 8
DOM_FINE = 4
FINE_LANES = 32
EARLY_LOADS = (3, 5, 13, 14, 15, 0, 1, 2, 9, 10)
LATE_LOADS = (4, 6, 7, 8, 11, 12, 16, 17, 18)


def iota(shape, dim):
    return lax.broadcasted_iota(jnp.int32, shape, dim)


def dot(a, b):
    return jnp.dot(a, b, preferred_element_type=F32)


def dot_nt(a, b):
    return lax.dot_general(a, b, (((1,), (1,)), ((), ())), preferred_element_type=F32)


def split_state(values):
    hi = values.astype(BF16)
    lo = (values - hi.astype(F32)).astype(BF16)
    return jnp.concatenate([hi, lo, hi], axis=0)


def pattern():
    pick = np.zeros((192, 32), np.float32)
    mask = np.zeros((192, 96), np.float32)
    columns = np.zeros((2, 16, 96), np.float32)
    for column in range(96):
        third, at = divmod(column, 32)
        if at < 3 * NODES:
            columns[third // 2, at % NODES, column] = 1.0

    def fill(row, source, var, sign):
        pick[row, source] = 1.0
        for third in range(3):
            first = 32 * third + NODES * var
            mask[row, first : first + NODES] = sign

    for which in range(2):
        for at in range(3 * NODES):
            node, part = at % NODES, at // NODES
            fill(32 * which + at, NODES * which + node, 1 if part == 0 else 0, -1.0)
        for node in range(NODES):
            fill(64 + 16 * which + node, NODES * which + node, 2, -1.0)
    for order in range(2):
        for face in range(3):
            for at in range(16):
                part, point = divmod(at, 4)
                source = 2 * NODES + 4 * face + (point if order else 3 - point)
                fill(96 + 48 * order + 16 * face + at, source, part % 3, 1.0)

    nodes = np.zeros((32, 16), np.float32)
    for row in range(3 * NODES):
        nodes[row, row % NODES] = 1.0
    places = np.zeros((2, 16, 288), np.float32)
    signs = np.zeros((32, 288), np.float32)
    for column in range(288):
        third, rest = divmod(column, 96)
        face, at = divmod(rest, 32)
        jump, at = divmod(at, 16)
        part, point = divmod(at, 4)
        places[third // 2, 4 * face + point, column] = 1.0
        for row in range(3 * NODES):
            var = row // NODES
            if jump:
                signs[row, column] = 1.0 if part == var else 0.0
            else:
                signs[row, column] = -1.0 if part in ((1, 2), (0,), (3,))[var] else 0.0
    return [jnp.asarray(x, BF16) for x in (pick, mask, columns, nodes, places, signs)]


def halves(values):
    hi = values.astype(BF16)
    return hi, (values - hi.astype(F32)).astype(BF16)


def spread_columns(values, columns_ref):
    hi, lo = halves(values)
    return (dot(hi, columns_ref[0]) + dot(lo, columns_ref[1])).astype(BF16)


def combine(slopes, alpha):
    a1, a2, a3, a4 = alpha
    both = a1 * slopes[0:32] + a2 * slopes[32:64]
    top = a3 * slopes[64:80] + a4 * slopes[80:96]
    return jnp.concatenate([both[0:16] + top, both[16:32]], axis=0)


def alpha_of(depth, m0, m1, m2, m3):
    row = iota((32, depth.shape[1]), 0)
    top = row[0:16] < NODES
    return (
        jnp.where(row < 10, m0, jnp.where(row < 20, depth * m0, depth * m2)),
        jnp.where(row < 10, m1, jnp.where(row < 20, depth * m1, depth * m3)),
        jnp.where(top, m2, 0.0),
        jnp.where(top, m3, 0.0),
    )


def flux_factors(depth, m0, m1, m2, m3):
    rows = iota((16, depth.shape[1]), 0)
    root = jnp.sqrt(depth)
    factors = []
    for hx, hy in ((-m1, -m3), (m0 + m1, m2 + m3), (-m0, -m2)):
        centre = jnp.where(
            rows < 4,
            depth * hx,
            jnp.where(rows < 8, hx, jnp.where(rows < 12, hy, depth * hy)),
        )
        factors.append((centre, root * jnp.sqrt(hx * hx + hy * hy)))
    return factors


def lifted(lift, factors, sums, differences):
    parts = []
    for (centre, jump), added, taken in zip(factors, sums, differences):
        parts.append(centre * added)
        parts.append(jump * taken)
    return dot(lift, split_state(jnp.concatenate(parts, axis=0)))


def pick_columns(load, sources, block, lane, start):
    out = start
    for k in sources:
        found = jnp.take_along_axis(load(k), lane, axis=1)
        out = jnp.where(block == k, found, out)
    return out


def step_kernel(
    n_region,
    n_dom,
    elems,
    state_ref,
    depth_ref,
    metric_ref,
    diff_ref,
    stiff_ref,
    trace_ref,
    lift_ref,
    cluster_ref,
    code_ref,
    send_reg_ref,
    send_dom_ref,
    move_dom_ref,
    move_slot_ref,
    pick_ref,
    mask_ref,
    columns_ref,
    nodes_ref,
    places_ref,
    signs_ref,
    out_ref,
    *scratch,
):
    hbm_refs = (
        state_ref,
        depth_ref,
        metric_ref,
        diff_ref,
        stiff_ref,
        trace_ref,
        lift_ref,
        cluster_ref,
        code_ref,
        send_reg_ref,
        send_dom_ref,
        move_dom_ref,
        move_slot_ref,
        pick_ref,
        mask_ref,
        columns_ref,
        nodes_ref,
        places_ref,
        signs_ref,
    )
    step_body(
        n_region, n_dom, elems, hbm_refs, out_ref, scratch[: len(hbm_refs)], *scratch[len(hbm_refs) :]
    )


def step_body(
    n_region,
    n_dom,
    elems,
    hbm_refs,
    out_ref,
    local_refs,
    in_sem,
    ready,
    first_ops,
    second_ops,
    lift_ops,
    dense,
    base,
    geometry,
    tab_a,
    tab_b,
    tab_c,
    beyond,
    out_reg,
    out_dom,
    in_reg,
    in_dom,
    out_fine,
    in_fine,
    land_out,
    land_in,
    tile_out,
    tile_in,
    ss_reg,
    rs_reg,
    ss_dom,
    rs_dom,
    ss_fine,
    rs_fine,
    ss_land,
    rs_land,
    ss_tile,
    rs_tile,
):
    r = lax.axis_index("region")
    d = lax.axis_index("dom")
    blocks = elems // 128
    has_low = r > 0
    has_high = r < n_region - 1
    dom_low = d > 0
    dom_high = d < n_dom - 1
    sides = (
        (has_high, {"region": r + 1}, 1, 0),
        (has_low, {"region": r - 1}, 0, 1),
        (dom_high, {"dom": d + 1}, 1, 0),
        (dom_low, {"dom": d - 1}, 0, 1),
    )
    comes = (has_low, has_high, dom_low, dom_high)

    loads = [
        pltpu.make_async_copy(src, dst, in_sem.at[i])
        for i, (src, dst) in enumerate(zip(hbm_refs, local_refs))
    ]
    barrier = pltpu.get_barrier_semaphore()

    def ring(k):
        return {"dom": lax.rem(d + k + n_dom, n_dom)}

    for i in EARLY_LOADS:
        loads[i].start()
    for exists, device, _, _ in sides[:2]:

        @pl.when(exists)
        def _():
            pl.semaphore_signal(barrier, inc=1, device_id=device, device_id_type=MESH)

    for k in (1, -1):
        pl.semaphore_signal(barrier, inc=1, device_id=ring(k), device_id_type=MESH)
    for i in LATE_LOADS:
        loads[i].start()

    def announce(stage, reach):
        for k in (reach, -reach):
            pl.semaphore_signal(
                ready.at[stage], inc=1, device_id=ring(k), device_id_type=MESH
            )

    (
        state_ref,
        depth_ref,
        metric_ref,
        diff_ref,
        stiff_ref,
        trace_ref,
        lift_ref,
        cluster_ref,
        code_ref,
        send_reg_ref,
        send_dom_ref,
        move_dom_ref,
        move_slot_ref,
        pick_ref,
        mask_ref,
        columns_ref,
        nodes_ref,
        places_ref,
        signs_ref,
    ) = local_refs
    first_ops[...] = jnp.zeros((32, 16), F32)
    second_ops[...] = jnp.zeros((32, 16), F32)
    lift_ops[...] = jnp.zeros((16, 16), F32)
    for i in EARLY_LOADS:
        loads[i].wait()

    dense[30:32, :] = jnp.zeros((2, elems), F32)
    for v in range(3):
        dense[NODES * v : NODES * (v + 1), :] = state_ref[:, v, :]
    state = dense[...]
    depth = depth_ref[...]
    m0, m1, m2, m3 = (metric_ref[i : i + 1, :] for i in range(4))

    alpha = alpha_of(depth, m0, m1, m2, m3)

    for a in range(2):
        first_ops[NODES * a : NODES * (a + 1), 0:NODES] = diff_ref[:, a, :]
    for f in range(3):
        first_ops[2 * NODES + 4 * f : 2 * NODES + 4 * f + 4, 0:NODES] = trace_ref[f]
    wide = dot(pick_ref[...], spread_columns(first_ops[...], columns_ref)).astype(BF16)
    wide = wide * mask_ref[...]
    slope, traces = wide[0:96], wide[96:192]

    def series_of(values, alpha):
        series = [values]
        for _ in range(3):
            series.append(combine(dot(slope, split_state(series[-1])), alpha))
        return series

    def integrate(series, factors):
        summed = factors[0] * series[0]
        for factor, member in zip(factors[1:], series[1:]):
            summed = summed + factor * member
        return summed

    series = series_of(state, alpha)
    early = integrate(series, FIRST_HALF)
    early_split = split_state(early)
    tab_a[0:48] = dot(traces[0:48], early_split)

    def source(table):
        def load(k):
            f, b = divmod(k, blocks)
            return table[16 * f : 16 * f + 16, 128 * b : 128 * b + 128]

        return load

    def spread(vector):
        return jnp.broadcast_to(vector, (16, 128))

    own = range(3 * blocks)

    def gather_sends(which, table, copies):
        for i, (exists, _, copy) in enumerate(copies):
            lane_row = sides[i][2]
            if i < 2:
                for b in range(2):
                    index = spread(send_reg_ref[lane_row : lane_row + 1, 128 * b : 128 * b + 128])
                    out_reg[which, lane_row, b] = pick_columns(
                        source(table), own, index >> 7, index & 127, jnp.zeros((16, 128), F32)
                    )
            else:
                index = spread(send_dom_ref[lane_row : lane_row + 1, :])
                out_dom[which, lane_row] = pick_columns(
                    source(table), own, index >> 7, index & 127, jnp.zeros((16, 128), F32)
                )
            pl.when(exists)(copy.start)

    def copies_a(which):
        copies = []
        for i, (exists, device, lane_row, at) in enumerate(sides):
            regional = i < 2
            copies.append(
                (
                    exists,
                    comes[2 * (i // 2) + at],
                    pltpu.make_async_remote_copy(
                        src_ref=(out_reg if regional else out_dom).at[which, lane_row],
                        dst_ref=(in_reg if regional else in_dom).at[which, at],
                        send_sem=(ss_reg if regional else ss_dom).at[which, at],
                        recv_sem=(rs_reg if regional else rs_dom).at[which, at],
                        device_id=device,
                        device_id_type=MESH,
                    ),
                )
            )
        return copies

    def start(copies):
        for exists, _, copy in copies:
            pl.when(exists)(copy.start)

    def wait_recv(copies):
        for _, arrives, copy in copies:
            pl.when(arrives)(copy.wait_recv)

    def wait_send(copies):
        for exists, _, copy in copies:
            pl.when(exists)(copy.wait_send)

    first_copies = copies_a(0)
    late_copies = copies_a(1)
    pl.semaphore_wait(barrier, 2 + has_low.astype(jnp.int32) + has_high.astype(jnp.int32))
    announce(0, 1)
    gather_sends(0, tab_a, first_copies)

    later = integrate(series, SECOND_HALF)
    tab_b[...] = dot(traces[0:48], split_state(later))
    gather_sends(1, tab_b, late_copies)

    tile_in[d] = jnp.zeros((8, 128), F32)
    land_in[d] = jnp.full((1, 128), -1, jnp.int32)
    for i in range(2):

        @pl.when(jnp.logical_not(comes[i]))
        def _():
            in_reg[:, i] = jnp.zeros(in_reg.shape[0:1] + in_reg.shape[2:], F32)

        @pl.when(jnp.logical_not(comes[2 + i]))
        def _():
            in_dom[:, i] = jnp.zeros(in_dom.shape[0:1] + in_dom.shape[2:], F32)

    for i in range(4):

        @pl.when(jnp.logical_not(comes[i]))
        def _():
            in_fine[i] = jnp.zeros((8, 128), F32)

    for i in LATE_LOADS:
        loads[i].wait()
    tab_a[48:96] = dot(traces[48:96], early_split)
    for a in range(2):
        second_ops[NODES * a : NODES * (a + 1), 0:NODES] = stiff_ref[:, a, :]
    stiff = dot(pick_ref[0:96], spread_columns(second_ops[...], columns_ref)).astype(BF16)
    stiff = -(stiff * mask_ref[0:96])
    for f in range(3):
        lift_ops[4 * f : 4 * f + 4, 0:NODES] = lift_ref[f]
    hi, lo = halves(lift_ops[...])
    lift = dot(dot_nt(nodes_ref[...], hi).astype(BF16), places_ref[0])
    lift = lift + dot(dot_nt(nodes_ref[...], lo).astype(BF16), places_ref[1])
    lift = lift.astype(BF16) * signs_ref[...]
    factors = flux_factors(depth, m0, m1, m2, m3)
    mirror = jnp.where((iota((16, 128), 0) >= 4) & (iota((16, 128), 0) < 12), -1.0, 1.0)
    first_code = 3 * elems
    regional = 2 * send_reg_ref.shape[1]
    wall_code = first_code + regional + 2 * send_dom_ref.shape[1]
    remote = range(3 * blocks, 3 * blocks + 6)

    def code_of(f, b):
        return spread(code_ref[f : f + 1, 128 * b : 128 * b + 128])

    def local_part(table):
        for f in range(3):
            for b in range(blocks):
                code = code_of(f, b)
                wall = mirror * table[48 + 16 * f : 64 + 16 * f, 128 * b : 128 * b + 128]
                wall = jnp.where(code == wall_code, wall, 0.0)
                beyond[f, b] = pick_columns(source(table), own, code >> 7, code & 127, wall)

    def increment(values_split, table):
        volume = combine(dot(stiff, values_split), alpha)
        outside = [jnp.concatenate([beyond[f, b] for b in range(blocks)], axis=1) for f in range(3)]
        inside = [table[48 + 16 * f : 64 + 16 * f, :] for f in range(3)]
        return volume + lifted(
            lift,
            factors,
            [x + y for x, y in zip(outside, inside)],
            [x - y for x, y in zip(outside, inside)],
        )

    def fine_column(code):
        slot = code - first_code
        reg = slot & 255
        from_reg = jnp.where(
            (slot >= 0) & (slot < regional) & (reg < REG_FINE), (slot >> 8) * REG_FINE + reg, -1
        )
        past = slot - regional
        dom = past & 127
        return jnp.where(
            (past >= 0) & (past < 256) & (dom < DOM_FINE),
            2 * REG_FINE + (past >> 7) * DOM_FINE + dom,
            from_reg,
        )

    local_part(tab_a)
    base[...] = state + increment(early_split, tab_a)
    pl.semaphore_wait(ready.at[0], 2)
    announce(1, 2)

    def to_peers(src, dst, ss, rs):
        return [
            pltpu.make_async_remote_copy(
                src_ref=src.at[t],
                dst_ref=dst.at[d],
                send_sem=ss.at[t],
                recv_sem=rs.at[d],
                device_id={"dom": t},
                device_id_type=MESH,
            )
            for t in range(n_dom)
        ]

    def from_peers(src, dst, ss, rs):
        return [
            pltpu.make_async_remote_copy(
                src_ref=src.at[t],
                dst_ref=dst.at[t],
                send_sem=ss.at[t],
                recv_sem=rs.at[t],
                device_id={"dom": t},
                device_id_type=MESH,
            )
            for t in range(n_dom)
        ]

    def unless_own(t, action):
        pl.when(t != d)(action)

    land_copies = to_peers(land_out, land_in, ss_land, rs_land)
    tile_copies = to_peers(tile_out, tile_in, ss_tile, rs_tile)
    land_comes = from_peers(land_out, land_in, ss_land, rs_land)
    tile_comes = from_peers(tile_out, tile_in, ss_tile, rs_tile)

    def within(t, reach):
        apart = lax.rem(t - d + n_dom, n_dom)
        return (apart != 0) & ((apart <= reach) | (apart >= n_dom - reach))

    lanes = iota((1, elems), 1)
    target = move_dom_ref[...]
    target = jnp.where(target == d, -1, target)
    fine_row = 15
    is_fine = cluster_ref[...] == 0
    kind = iota((16, elems), 0)
    chosen = jnp.where(kind == target, 1.0, 0.0)
    chosen = jnp.where(kind == fine_row, jnp.where(is_fine, 1.0, 0.0), chosen)
    before = jnp.where(iota((elems, elems), 0) < iota((elems, elems), 1), 1.0, 0.0).astype(BF16)
    ranks = dot(chosen.astype(BF16), before)
    rank = jnp.sum(jnp.where(kind < fine_row, chosen * ranks, 0.0), axis=0, keepdims=True)
    fine_rank = ranks[fine_row:].astype(jnp.int32)
    fine_position = jnp.where(is_fine, fine_rank, -1)
    slots = n_dom * MIGRANTS
    padded = 384 if slots <= 384 else 128 * (-(-slots // 128))
    position = jnp.where(target < 0, -1, target * MIGRANTS + rank.astype(jnp.int32))
    inverse = jnp.concatenate(
        [
            jnp.where(iota((padded, elems), 0) == position, 1.0, 0.0),
            jnp.where(iota((128, elems), 0) == fine_position, 1.0, 0.0),
        ],
        axis=0,
    ).astype(BF16)
    place = move_slot_ref[...]
    which_row = iota((8, elems), 0)
    facts = jnp.where(
        which_row == 0,
        lanes >> 1,
        jnp.where(
            which_row == 1, lanes & 1, jnp.where(which_row == 2, place >> 1, place & 1)
        ),
    )
    facts = jnp.where(which_row < 4, facts, 0).astype(F32).astype(BF16)
    found = dot_nt(facts, inverse).astype(jnp.int32)
    leaves = found[0:1] * 2 + found[1:2]
    lands = found[2:3] * 2 + found[3:4]
    fine_at = leaves[:, padded : padded + 128]
    for t in range(n_dom):
        row = jnp.broadcast_to(lands[:, 128 * (t // 4) : 128 * (t // 4) + 128], (8, 128))
        row = jnp.take_along_axis(row, (iota((8, 128), 1) & 31) + 32 * (t & 3), axis=1)
        land_out[t] = row[0:1]

    geometry[0:1] = depth
    geometry[1:5] = metric_ref[...]
    geometry[5:8] = code_ref[...].astype(F32)

    def squeeze(load, index):
        index = jnp.broadcast_to(index, (8, 128))
        return pick_columns(load, range(blocks), index >> 7, index & 127, jnp.zeros((8, 128), F32))

    def block_of(ref, g):
        return lambda b: ref[8 * g : 8 * g + 8, 128 * b : 128 * b + 128]

    fine_base = jnp.concatenate([squeeze(block_of(base, g), fine_at) for g in range(4)], axis=0)
    facts = squeeze(block_of(geometry, 0), fine_at)
    fine_geometry = [facts[i : i + 1] for i in range(5)]
    fine_alpha = alpha_of(*fine_geometry)
    fine_factors = flux_factors(*fine_geometry)
    fine_codes = [spread(facts[5 + f : 6 + f].astype(jnp.int32)) for f in range(3)]

    lane = iota((1, 128), 1)
    wanted = jnp.where(
        lane < REG_FINE,
        send_reg_ref[1:2, 0:128],
        jnp.where(
            lane < 2 * REG_FINE,
            pltpu.roll(send_reg_ref[0:1, 0:128], REG_FINE, 1),
            jnp.where(
                lane < 2 * REG_FINE + DOM_FINE,
                pltpu.roll(send_dom_ref[1:2, :], 2 * REG_FINE, 1),
                pltpu.roll(send_dom_ref[0:1, :], 2 * REG_FINE + DOM_FINE, 1),
            ),
        ),
    )
    wanted_face = (wanted >= elems).astype(jnp.int32) + (wanted >= 2 * elems).astype(jnp.int32)
    wanted_face = spread(wanted_face)
    rank_rows = jnp.broadcast_to(fine_rank.astype(F32), (8, elems))
    wanted_at = squeeze(
        lambda b: rank_rows[:, 128 * b : 128 * b + 128], wanted - elems * wanted_face[0:1]
    ).astype(jnp.int32)
    wanted_at = spread(wanted_at[0:1]) & 127

    wait_recv(first_copies)

    def early_slot(k):
        k = k - 3 * blocks
        return in_reg[0, k // 2, k % 2] if k < 4 else in_dom[0, k - 4]

    outer = [
        pick_columns(early_slot, remote, code >> 7, code & 127, jnp.zeros((16, 128), F32))
        for code in fine_codes
    ]
    fine_midway = fine_base + lifted(lift, fine_factors, outer, outer)
    fine = integrate(series_of(fine_midway, fine_alpha), FIRST_HALF)
    fine_table = dot(traces[0:48], split_state(fine))

    block = jnp.zeros((16, 128), F32)
    for f in range(3):
        found = jnp.take_along_axis(fine_table[16 * f : 16 * f + 16], wanted_at, axis=1)
        block = jnp.where(wanted_face == f, found, block)
    lane8 = iota((8, 128), 1)
    out_fine[...] = jnp.where(lane8 < FINE_LANES, block[0:8], pltpu.roll(block[8:16], FINE_LANES, 1))
    fine_copies = []
    for i, (exists, device, _, at) in enumerate(sides):
        fine_copies.append(
            (
                exists,
                comes[2 * (i // 2) + at],
                pltpu.make_async_remote_copy(
                    src_ref=out_fine,
                    dst_ref=in_fine.at[i],
                    send_sem=ss_fine.at[i],
                    recv_sem=rs_fine.at[i],
                    device_id=device,
                    device_id_type=MESH,
                ),
            )
        )
    start(fine_copies)
    pl.semaphore_wait(ready.at[1], 2)
    announce(2, 2)
    for t in range(n_dom):
        pl.when(within(t, 4))(land_copies[t].start)

    for b in range(blocks):
        columns = slice(128 * b, 128 * b + 128)
        index = jnp.broadcast_to(fine_rank[:, columns] & 127, (8, 128))
        mine = jnp.broadcast_to(cluster_ref[:, columns], (8, 128)) == 0
        for g in range(4):
            rows = slice(8 * g, 8 * g + 8)
            found = jnp.take_along_axis(fine[rows], index, axis=1)
            dense[rows, columns] = jnp.where(mine, found, later[rows, columns])
    second_split = split_state(dense[...])
    tab_c[...] = dot(traces, second_split)
    local_part(tab_c)
    wait_recv(late_copies)

    lane16 = iota((16, 128), 1)
    both = []
    for k in range(6):
        first = early_slot(3 * blocks + k)
        if k < 4:
            coarse = in_reg[1, k // 2, k % 2]
            if k % 2 == 0:
                coarse = jnp.where(lane16 < REG_FINE, 0.0, coarse)
        else:
            coarse = jnp.where(lane16 < DOM_FINE, 0.0, in_dom[1, k - 4])
        both.append(first + coarse)
    columns = {}
    for f in range(3):
        for b in range(blocks):
            code = code_of(f, b)
            columns[f, b] = fine_column(code)
            beyond[f, b] = pick_columns(
                lambda k: both[k - 3 * blocks], remote, code >> 7, code & 127, beyond[f, b]
            )
    dense[...] = base[...] + increment(second_split, tab_c)
    pl.semaphore_wait(ready.at[2], 2)
    for t in range(n_dom):
        pl.when((t != d) & jnp.logical_not(within(t, 4)))(land_copies[t].start)
    wait_recv(fine_copies)
    at = lane8 & (FINE_LANES - 1)
    fresh = jnp.where(
        at < REG_FINE,
        in_fine[0],
        jnp.where(
            at < 2 * REG_FINE,
            in_fine[1],
            jnp.where(at < 2 * REG_FINE + DOM_FINE, in_fine[2], in_fine[3]),
        ),
    )
    outer = []
    for f in range(3):
        late = []
        for b in range(blocks):
            column = columns[f, b][0:8] & (FINE_LANES - 1)
            low = jnp.take_along_axis(fresh, column, axis=1)
            high = jnp.take_along_axis(fresh, column + FINE_LANES, axis=1)
            found = jnp.concatenate([low, high], axis=0)
            late.append(jnp.where(columns[f, b] >= 0, found, 0.0))
        outer.append(jnp.concatenate(late, axis=1))
    dense[...] = dense[...] + lifted(lift, factors, outer, outer)

    def cell(g, b):
        return dense[8 * g : 8 * g + 8, 128 * b : 128 * b + 128]

    group = iota((8, 128), 1) >> 5
    packed = {}
    for q in range(padded // 128):
        index = jnp.broadcast_to(leaves[:, 128 * q : 128 * q + 128], (8, 128))
        for g in range(4):
            packed[g, q] = pick_columns(
                lambda b: cell(g, b), range(blocks), index >> 7, index & 127, jnp.zeros((8, 128), F32)
            )
    for t in range(n_dom):
        tile = jnp.zeros((8, 128), F32)
        for g in range(4):
            shift = (32 * (g - (t & 3))) % 128
            moved = packed[g, t // 4]
            if shift:
                moved = pltpu.roll(moved, shift, 1)
            tile = jnp.where(group == g, moved, tile)
        tile_out[t] = tile
        unless_own(t, tile_copies[t].start)
    for t in range(n_dom):
        unless_own(t, land_comes[t].wait_recv)
    kk = iota((1, 128), 1)
    stack = []
    for q in range(padded // 128):
        row_q = jnp.full((1, 128), -1, jnp.int32)
        for k in range(4 * q, min(4 * q + 4, n_dom)):
            row_q = jnp.where((kk >> 5) == (k & 3), land_in[k], row_q)
        stack.append(row_q)
    places = jnp.concatenate(stack, axis=1)
    comes_here = jnp.where(iota((elems, padded), 0) == places, 1.0, 0.0).astype(BF16)
    column = iota((8, padded), 1)
    row8 = iota((8, padded), 0)
    facts = jnp.where(row8 == 0, column >> 1, jnp.where(row8 == 1, column & 1, 1))
    found = dot_nt(facts.astype(F32).astype(BF16), comes_here).astype(jnp.int32)
    origin = jnp.where(found[2:3] > 0, found[0:1] * 2 + found[1:2], -1)

    wait_send(first_copies)
    wait_send(late_copies)
    wait_send(fine_copies)
    for t in range(n_dom):
        unless_own(t, land_copies[t].wait_send)
        unless_own(t, tile_copies[t].wait_send)
    result = {(g, b): cell(g, b) for g in range(4) for b in range(blocks)}
    for q in range(padded // 128):
        senders = range(4 * q, min(4 * q + 4, n_dom))
        for t in senders:
            unless_own(t, tile_comes[t].wait_recv)
        for g in range(4):
            rows = jnp.zeros((8, 128), F32)
            for t in senders:
                shift = (32 * ((t & 3) - g)) % 128
                moved = tile_in[t]
                if shift:
                    moved = pltpu.roll(moved, shift, 1)
                rows = jnp.where(group == (t & 3), moved, rows)
            for b in range(blocks):
                index = jnp.broadcast_to(origin[:, 128 * b : 128 * b + 128], (8, 128))
                found = jnp.take_along_axis(rows, index & 127, axis=1)
                result[g, b] = jnp.where((index >> 7) == q, found, result[g, b])
    for g in range(4):
        for b in range(blocks):
            dense[8 * g : 8 * g + 8, 128 * b : 128 * b + 128] = result[g, b]
    for v in range(3):
        out_ref[:, v, :] = dense[NODES * v : NODES * (v + 1), :]


def shards(n_region, n_dom, *args):
    (
        water_state,
        water_depth,
        metric,
        diff_ops,
        stiff_ops,
        trace_ops,
        lift_ops,
        cluster,
        face_code,
        send_region,
        send_dom,
        move_dom,
        move_slot,
    ) = args
    elems = water_state.shape[2]
    blocks = elems // 128
    vmem = pl.BlockSpec(memory_space=pltpu.VMEM)
    dma = pltpu.SemaphoreType.DMA

    def kernel(*refs):
        step_kernel(n_region, n_dom, elems, *refs)

    given = (
        jnp.transpose(water_state, (1, 0, 2)),
        water_depth.reshape(1, elems),
        metric,
        jnp.transpose(diff_ops, (1, 0, 2)),
        jnp.transpose(stiff_ops, (1, 0, 2)),
        trace_ops,
        jnp.transpose(lift_ops, (0, 2, 1)),
        cluster.reshape(1, elems),
        face_code,
        send_region,
        send_dom,
        move_dom.reshape(1, elems),
        move_slot.reshape(1, elems),
        *pattern(),
    )
    result = pl.pallas_call(
        kernel,
        out_shape=pltpu.VMEM((NODES, 3, elems), F32),
        in_specs=[pl.BlockSpec(memory_space=pl.ANY)] * len(given),
        out_specs=vmem,
        scratch_shapes=[pltpu.VMEM(x.shape, x.dtype) for x in given]
        + [
            dma((len(given),)),
            pltpu.SemaphoreType.REGULAR((3,)),
            pltpu.VMEM((32, 16), F32),
            pltpu.VMEM((32, 16), F32),
            pltpu.VMEM((16, 16), F32),
            pltpu.VMEM((32, elems), F32),
            pltpu.VMEM((32, elems), F32),
            pltpu.VMEM((8, elems), F32),
            pltpu.VMEM((96, elems), F32),
            pltpu.VMEM((48, elems), F32),
            pltpu.VMEM((96, elems), F32),
            pltpu.VMEM((3, blocks, 16, 128), F32),
            pltpu.VMEM((2, 2, 2, 16, 128), F32),
            pltpu.VMEM((2, 2, 16, 128), F32),
            pltpu.VMEM((2, 2, 2, 16, 128), F32),
            pltpu.VMEM((2, 2, 16, 128), F32),
            pltpu.VMEM((8, 128), F32),
            pltpu.VMEM((4, 8, 128), F32),
            pltpu.VMEM((n_dom, 1, 128), jnp.int32),
            pltpu.VMEM((n_dom, 1, 128), jnp.int32),
            pltpu.VMEM((n_dom, 8, 128), F32),
            pltpu.VMEM((n_dom, 8, 128), F32),
            dma((2, 2)),
            dma((2, 2)),
            dma((2, 2)),
            dma((2, 2)),
            dma((4,)),
            dma((4,)),
            dma((n_dom,)),
            dma((n_dom,)),
            dma((n_dom,)),
            dma((n_dom,)),
        ],
        compiler_params=pltpu.CompilerParams(collective_id=0, has_side_effects=True),
        name="wave_step",
    )(*given)
    return jnp.transpose(result, (1, 0, 2))


def solution(mesh):
    both = ("region", "dom")
    wide, flat = P(None, both), P(both)
    placed = (
        P(None, None, both),
        flat,
        wide,
        P(),
        P(),
        P(),
        P(),
        flat,
        wide,
        wide,
        wide,
        flat,
        flat,
    )
    n_region, n_dom = mesh.shape["region"], mesh.shape["dom"]

    def step(*args):
        return shards(n_region, n_dom, *args)

    return jax.shard_map(
        step,
        mesh=mesh,
        in_specs=placed,
        out_specs=P(None, None, both),
        check_vma=False,
    )
```

```python
import jax
import jax.numpy as jnp
import numpy as np
from jax import lax
from jax.experimental import pallas as pl
from jax.experimental.pallas import tpu as pltpu
from jax.sharding import PartitionSpec as P

MESH = pl.DeviceIdType.MESH
F32 = jnp.float32
BF16 = jnp.bfloat16
NODES = 10
FIRST_HALF = (0.5, 0.125, 1.0 / 48.0, 1.0 / 384.0)
SECOND_HALF = (0.5, 0.375, 7.0 / 48.0, 15.0 / 384.0)
MIGRANTS = 32
REG_FINE = 8
DOM_FINE = 4
FINE_LANES = 32
EARLY_LOADS = (3, 5, 13, 0, 1, 2, 9, 10)
LATE_LOADS = (4, 6, 7, 8, 11, 12, 14)


def iota(shape, dim):
    return lax.broadcasted_iota(jnp.int32, shape, dim)


def dot(a, b):
    return jnp.dot(a, b, preferred_element_type=F32)


def dot_nt(a, b):
    return lax.dot_general(a, b, (((1,), (1,)), ((), ())), preferred_element_type=F32)


def split_state(values):
    hi = values.astype(BF16)
    lo = (values - hi.astype(F32)).astype(BF16)
    return jnp.concatenate([hi, lo, hi], axis=0)


def pattern():
    pick = np.zeros((192, 32), np.float32)
    mask = np.zeros((192, 96), np.float32)
    columns = np.zeros((2, 16, 96), np.float32)
    for column in range(96):
        third, at = divmod(column, 32)
        if at < 3 * NODES:
            columns[third // 2, at % NODES, column] = 1.0

    def fill(row, source, var, sign):
        pick[row, source] = 1.0
        for third in range(3):
            first = 32 * third + NODES * var
            mask[row, first : first + NODES] = sign

    for which in range(2):
        for at in range(3 * NODES):
            node, part = at % NODES, at // NODES
            fill(32 * which + at, NODES * which + node, 1 if part == 0 else 0, -1.0)
        for node in range(NODES):
            fill(64 + 16 * which + node, NODES * which + node, 2, -1.0)
    for order in range(2):
        for face in range(3):
            for at in range(16):
                part, point = divmod(at, 4)
                source = 2 * NODES + 4 * face + (point if order else 3 - point)
                fill(96 + 48 * order + 16 * face + at, source, part % 3, 1.0)

    nodes = np.zeros((32, 16), np.float32)
    for row in range(3 * NODES):
        nodes[row, row % NODES] = 1.0
    places = np.zeros((2, 16, 288), np.float32)
    signs = np.zeros((32, 288), np.float32)
    for column in range(288):
        third, rest = divmod(column, 96)
        face, at = divmod(rest, 32)
        jump, at = divmod(at, 16)
        part, point = divmod(at, 4)
        places[third // 2, 4 * face + point, column] = 1.0
        for row in range(3 * NODES):
            var = row // NODES
            if jump:
                signs[row, column] = 1.0 if part == var else 0.0
            else:
                signs[row, column] = -1.0 if part in ((1, 2), (0,), (3,))[var] else 0.0
    first = np.zeros((416, 128), np.float32)
    first[0:192, 0:96] = mask
    first[192:384, 0:32] = pick
    first[384:416, 0:96] = columns.reshape(32, 96)
    second = np.zeros((96, 288), np.float32)
    second[0:32] = places.reshape(32, 288)
    second[32:64] = signs
    second[64:96, 0:16] = nodes
    return [jnp.asarray(x, BF16) for x in (first, second)]


def halves(values):
    hi = values.astype(BF16)
    return hi, (values - hi.astype(F32)).astype(BF16)


def spread_columns(values, first_ref):
    hi, lo = halves(values)
    return (
        dot(hi, first_ref[384:400, 0:96]) + dot(lo, first_ref[400:416, 0:96])
    ).astype(BF16)


def combine(slopes, alpha):
    a1, a2, a3, a4 = alpha
    both = a1 * slopes[0:32] + a2 * slopes[32:64]
    top = a3 * slopes[64:80] + a4 * slopes[80:96]
    return jnp.concatenate([both[0:16] + top, both[16:32]], axis=0)


def alpha_of(depth, m0, m1, m2, m3):
    row = iota((32, depth.shape[1]), 0)
    top = row[0:16] < NODES
    return (
        jnp.where(row < 10, m0, jnp.where(row < 20, depth * m0, depth * m2)),
        jnp.where(row < 10, m1, jnp.where(row < 20, depth * m1, depth * m3)),
        jnp.where(top, m2, 0.0),
        jnp.where(top, m3, 0.0),
    )


def flux_factors(depth, m0, m1, m2, m3):
    rows = iota((16, depth.shape[1]), 0)
    root = jnp.sqrt(depth)
    factors = []
    for hx, hy in ((-m1, -m3), (m0 + m1, m2 + m3), (-m0, -m2)):
        centre = jnp.where(
            rows < 4,
            depth * hx,
            jnp.where(rows < 8, hx, jnp.where(rows < 12, hy, depth * hy)),
        )
        factors.append((centre, root * jnp.sqrt(hx * hx + hy * hy)))
    return factors


def lifted(lift, factors, sums, differences):
    parts = []
    for (centre, jump), added, taken in zip(factors, sums, differences):
        parts.append(centre * added)
        parts.append(jump * taken)
    return dot(lift, split_state(jnp.concatenate(parts, axis=0)))


def pick_columns(load, sources, block, lane, start):
    out = start
    for k in sources:
        found = jnp.take_along_axis(load(k), lane, axis=1)
        out = jnp.where(block == k, found, out)
    return out


def step_kernel(
    n_region,
    n_dom,
    elems,
    state_ref,
    depth_ref,
    metric_ref,
    diff_ref,
    stiff_ref,
    trace_ref,
    lift_ref,
    cluster_ref,
    code_ref,
    send_reg_ref,
    send_dom_ref,
    move_dom_ref,
    move_slot_ref,
    first_ref,
    second_ref,
    out_ref,
    *scratch,
):
    hbm_refs = (
        state_ref,
        depth_ref,
        metric_ref,
        diff_ref,
        stiff_ref,
        trace_ref,
        lift_ref,
        cluster_ref,
        code_ref,
        send_reg_ref,
        send_dom_ref,
        move_dom_ref,
        move_slot_ref,
        first_ref,
        second_ref,
    )
    step_body(
        n_region, n_dom, elems, hbm_refs, out_ref, scratch[: len(hbm_refs)], *scratch[len(hbm_refs) :]
    )


def step_body(
    n_region,
    n_dom,
    elems,
    hbm_refs,
    out_ref,
    local_refs,
    in_sem,
    ready,
    first_ops,
    second_ops,
    lift_ops,
    dense,
    base,
    geometry,
    tab_a,
    tab_b,
    tab_c,
    beyond,
    out_reg,
    out_dom,
    in_reg,
    in_dom,
    out_fine,
    in_fine,
    land_out,
    land_in,
    tile_out,
    tile_in,
    ss_reg,
    rs_reg,
    ss_dom,
    rs_dom,
    ss_fine,
    rs_fine,
    ss_land,
    rs_land,
    ss_tile,
    rs_tile,
):
    r = lax.axis_index("region")
    d = lax.axis_index("dom")
    blocks = elems // 128
    has_low = r > 0
    has_high = r < n_region - 1
    dom_low = d > 0
    dom_high = d < n_dom - 1
    sides = (
        (has_high, {"region": r + 1}, 1, 0),
        (has_low, {"region": r - 1}, 0, 1),
        (dom_high, {"dom": d + 1}, 1, 0),
        (dom_low, {"dom": d - 1}, 0, 1),
    )
    comes = (has_low, has_high, dom_low, dom_high)

    loads = [
        pltpu.make_async_copy(src, dst, in_sem.at[i])
        for i, (src, dst) in enumerate(zip(hbm_refs, local_refs))
    ]
    barrier = pltpu.get_barrier_semaphore()

    def ring(k):
        return {"dom": lax.rem(d + k + n_dom, n_dom)}

    for i in EARLY_LOADS:
        loads[i].start()
    for exists, device, _, _ in sides[:2]:

        @pl.when(exists)
        def _():
            pl.semaphore_signal(barrier, inc=1, device_id=device, device_id_type=MESH)

    for k in (1, -1):
        pl.semaphore_signal(barrier, inc=1, device_id=ring(k), device_id_type=MESH)
    for i in LATE_LOADS:
        loads[i].start()

    def announce(stage, reach):
        for k in (reach, -reach):
            pl.semaphore_signal(
                ready.at[stage], inc=1, device_id=ring(k), device_id_type=MESH
            )

    (
        state_ref,
        depth_ref,
        metric_ref,
        diff_ref,
        stiff_ref,
        trace_ref,
        lift_ref,
        cluster_ref,
        code_ref,
        send_reg_ref,
        send_dom_ref,
        move_dom_ref,
        move_slot_ref,
        first_ref,
        second_ref,
    ) = local_refs
    first_ops[...] = jnp.zeros((32, 16), F32)
    second_ops[...] = jnp.zeros((32, 16), F32)
    lift_ops[...] = jnp.zeros((16, 16), F32)
    for i in EARLY_LOADS:
        loads[i].wait()

    dense[30:32, :] = jnp.zeros((2, elems), F32)
    for v in range(3):
        dense[NODES * v : NODES * (v + 1), :] = state_ref[:, v, :]
    state = dense[...]
    depth = depth_ref[...]
    m0, m1, m2, m3 = (metric_ref[i : i + 1, :] for i in range(4))

    alpha = alpha_of(depth, m0, m1, m2, m3)

    for a in range(2):
        first_ops[NODES * a : NODES * (a + 1), 0:NODES] = diff_ref[:, a, :]
    for f in range(3):
        first_ops[2 * NODES + 4 * f : 2 * NODES + 4 * f + 4, 0:NODES] = trace_ref[f]
    wide = dot(first_ref[192:384, 0:32], spread_columns(first_ops[...], first_ref)).astype(BF16)
    wide = wide * first_ref[0:192, 0:96]
    slope, traces = wide[0:96], wide[96:192]

    def series_of(values, alpha):
        series = [values]
        for _ in range(3):
            series.append(combine(dot(slope, split_state(series[-1])), alpha))
        return series

    def integrate(series, factors):
        summed = factors[0] * series[0]
        for factor, member in zip(factors[1:], series[1:]):
            summed = summed + factor * member
        return summed

    series = series_of(state, alpha)
    early = integrate(series, FIRST_HALF)
    early_split = split_state(early)
    tab_a[0:48] = dot(traces[0:48], early_split)

    def source(table):
        def load(k):
            f, b = divmod(k, blocks)
            return table[16 * f : 16 * f + 16, 128 * b : 128 * b + 128]

        return load

    def spread(vector):
        return jnp.broadcast_to(vector, (16, 128))

    own = range(3 * blocks)

    def gather_sends(which, table, copies):
        for i, (exists, _, copy) in enumerate(copies):
            lane_row = sides[i][2]
            if i < 2:
                for b in range(2):
                    index = spread(send_reg_ref[lane_row : lane_row + 1, 128 * b : 128 * b + 128])
                    out_reg[which, lane_row, b] = pick_columns(
                        source(table), own, index >> 7, index & 127, jnp.zeros((16, 128), F32)
                    )
            else:
                index = spread(send_dom_ref[lane_row : lane_row + 1, :])
                out_dom[which, lane_row] = pick_columns(
                    source(table), own, index >> 7, index & 127, jnp.zeros((16, 128), F32)
                )
            pl.when(exists)(copy.start)

    def copies_a(which):
        copies = []
        for i, (exists, device, lane_row, at) in enumerate(sides):
            regional = i < 2
            copies.append(
                (
                    exists,
                    comes[2 * (i // 2) + at],
                    pltpu.make_async_remote_copy(
                        src_ref=(out_reg if regional else out_dom).at[which, lane_row],
                        dst_ref=(in_reg if regional else in_dom).at[which, at],
                        send_sem=(ss_reg if regional else ss_dom).at[which],
                        recv_sem=(rs_reg if regional else rs_dom).at[which],
                        device_id=device,
                        device_id_type=MESH,
                    ),
                )
            )
        return copies

    def start(copies):
        for exists, _, copy in copies:
            pl.when(exists)(copy.start)

    def sizes(src, dst, ss, rs):
        return pltpu.make_async_remote_copy(
            src_ref=src,
            dst_ref=dst,
            send_sem=ss,
            recv_sem=rs,
            device_id=ring(1),
            device_id_type=MESH,
        )

    def either(condition, yes, no):
        pl.when(condition)(yes)
        pl.when(jnp.logical_not(condition))(no)

    inner = (has_low & has_high, dom_low & dom_high)

    def pairs_a(which):
        return [
            (sizes(src.at[which], dst.at[which], *sems), sizes(src.at[which, 0], dst.at[which, 0], *sems))
            for src, dst, sems in (
                (out_reg, in_reg, (ss_reg.at[which], rs_reg.at[which])),
                (out_dom, in_dom, (ss_dom.at[which], rs_dom.at[which])),
            )
        ]

    def wait_recv(pairs):
        for condition, (two, one) in zip(inner, pairs):
            either(condition, two.wait_recv, one.wait_recv)

    def wait_send(pairs):
        for condition, (two, one) in zip(inner, pairs):
            either(condition, two.wait_send, one.wait_send)

    first_copies = copies_a(0)
    late_copies = copies_a(1)
    first_pairs, late_pairs = pairs_a(0), pairs_a(1)
    pl.semaphore_wait(barrier, 2 + has_low.astype(jnp.int32) + has_high.astype(jnp.int32))
    announce(0, 1)
    gather_sends(0, tab_a, first_copies)

    later = integrate(series, SECOND_HALF)
    tab_b[...] = dot(traces[0:48], split_state(later))
    gather_sends(1, tab_b, late_copies)

    tile_in[d] = jnp.zeros((8, 128), F32)
    land_in[d] = jnp.full((1, 128), -1, jnp.int32)
    for i in range(2):

        @pl.when(jnp.logical_not(comes[i]))
        def _():
            in_reg[:, i] = jnp.zeros(in_reg.shape[0:1] + in_reg.shape[2:], F32)

        @pl.when(jnp.logical_not(comes[2 + i]))
        def _():
            in_dom[:, i] = jnp.zeros(in_dom.shape[0:1] + in_dom.shape[2:], F32)

    for i in range(4):

        @pl.when(jnp.logical_not(comes[i]))
        def _():
            in_fine[i] = jnp.zeros((8, 128), F32)

    for i in LATE_LOADS:
        loads[i].wait()
    tab_a[48:96] = dot(traces[48:96], early_split)
    for a in range(2):
        second_ops[NODES * a : NODES * (a + 1), 0:NODES] = stiff_ref[:, a, :]
    stiff = dot(first_ref[192:288, 0:32], spread_columns(second_ops[...], first_ref)).astype(BF16)
    stiff = -(stiff * first_ref[0:96, 0:96])
    for f in range(3):
        lift_ops[4 * f : 4 * f + 4, 0:NODES] = lift_ref[f]
    hi, lo = halves(lift_ops[...])
    nodes = second_ref[64:96, 0:16]
    lift = dot(dot_nt(nodes, hi).astype(BF16), second_ref[0:16])
    lift = lift + dot(dot_nt(nodes, lo).astype(BF16), second_ref[16:32])
    lift = lift.astype(BF16) * second_ref[32:64]
    factors = flux_factors(depth, m0, m1, m2, m3)
    mirror = jnp.where((iota((16, 128), 0) >= 4) & (iota((16, 128), 0) < 12), -1.0, 1.0)
    first_code = 3 * elems
    regional = 2 * send_reg_ref.shape[1]
    wall_code = first_code + regional + 2 * send_dom_ref.shape[1]
    remote = range(3 * blocks, 3 * blocks + 6)

    def code_of(f, b):
        return spread(code_ref[f : f + 1, 128 * b : 128 * b + 128])

    def local_part(table):
        for f in range(3):
            for b in range(blocks):
                code = code_of(f, b)
                wall = mirror * table[48 + 16 * f : 64 + 16 * f, 128 * b : 128 * b + 128]
                wall = jnp.where(code == wall_code, wall, 0.0)
                beyond[f, b] = pick_columns(source(table), own, code >> 7, code & 127, wall)

    def increment(values_split, table):
        volume = combine(dot(stiff, values_split), alpha)
        outside = [jnp.concatenate([beyond[f, b] for b in range(blocks)], axis=1) for f in range(3)]
        inside = [table[48 + 16 * f : 64 + 16 * f, :] for f in range(3)]
        return volume + lifted(
            lift,
            factors,
            [x + y for x, y in zip(outside, inside)],
            [x - y for x, y in zip(outside, inside)],
        )

    def fine_column(code):
        slot = code - first_code
        reg = slot & 255
        from_reg = jnp.where(
            (slot >= 0) & (slot < regional) & (reg < REG_FINE), (slot >> 8) * REG_FINE + reg, -1
        )
        past = slot - regional
        dom = past & 127
        return jnp.where(
            (past >= 0) & (past < 256) & (dom < DOM_FINE),
            2 * REG_FINE + (past >> 7) * DOM_FINE + dom,
            from_reg,
        )

    local_part(tab_a)
    base[...] = state + increment(early_split, tab_a)
    pl.semaphore_wait(ready.at[0], 2)
    announce(1, 2)

    def to_peers(src, dst, ss, rs):
        return [
            pltpu.make_async_remote_copy(
                src_ref=src.at[t],
                dst_ref=dst.at[d],
                send_sem=ss,
                recv_sem=rs,
                device_id={"dom": t},
                device_id_type=MESH,
            )
            for t in range(n_dom)
        ]

    others = pl.ds(0, n_dom - 1)
    land_copies = to_peers(land_out, land_in, ss_land, rs_land)
    land_all = sizes(land_out.at[others], land_in.at[others], ss_land, rs_land)
    tile_copies = to_peers(tile_out, tile_in, ss_tile, rs_tile.at[d // 4])
    tile_all = sizes(tile_out.at[others], tile_in.at[others], ss_tile, rs_tile.at[0])

    def within(t, reach):
        apart = lax.rem(t - d + n_dom, n_dom)
        return (apart != 0) & ((apart <= reach) | (apart >= n_dom - reach))

    lanes = iota((1, elems), 1)
    target = move_dom_ref[...]
    target = jnp.where(target == d, -1, target)
    fine_row = 15
    is_fine = cluster_ref[...] == 0
    kind = iota((16, elems), 0)
    chosen = jnp.where(kind == target, 1.0, 0.0)
    chosen = jnp.where(kind == fine_row, jnp.where(is_fine, 1.0, 0.0), chosen)
    before = jnp.where(iota((elems, elems), 0) < iota((elems, elems), 1), 1.0, 0.0).astype(BF16)
    ranks = dot(chosen.astype(BF16), before)
    rank = jnp.sum(jnp.where(kind < fine_row, chosen * ranks, 0.0), axis=0, keepdims=True)
    fine_rank = ranks[fine_row:].astype(jnp.int32)
    fine_position = jnp.where(is_fine, fine_rank, -1)
    slots = n_dom * MIGRANTS
    padded = 384 if slots <= 384 else 128 * (-(-slots // 128))
    position = jnp.where(target < 0, -1, target * MIGRANTS + rank.astype(jnp.int32))
    inverse = jnp.concatenate(
        [
            jnp.where(iota((padded, elems), 0) == position, 1.0, 0.0),
            jnp.where(iota((128, elems), 0) == fine_position, 1.0, 0.0),
        ],
        axis=0,
    ).astype(BF16)
    place = move_slot_ref[...]
    which_row = iota((8, elems), 0)
    facts = jnp.where(
        which_row == 0,
        lanes >> 1,
        jnp.where(
            which_row == 1, lanes & 1, jnp.where(which_row == 2, place >> 1, place & 1)
        ),
    )
    facts = jnp.where(which_row < 4, facts, 0).astype(F32).astype(BF16)
    found = dot_nt(facts, inverse).astype(jnp.int32)
    leaves = found[0:1] * 2 + found[1:2]
    lands = found[2:3] * 2 + found[3:4]
    fine_at = leaves[:, padded : padded + 128]
    for t in range(n_dom):
        row = jnp.broadcast_to(lands[:, 128 * (t // 4) : 128 * (t // 4) + 128], (8, 128))
        row = jnp.take_along_axis(row, (iota((8, 128), 1) & 31) + 32 * (t & 3), axis=1)
        land_out[t] = row[0:1]

    geometry[0:1] = depth
    geometry[1:5] = metric_ref[...]
    geometry[5:8] = code_ref[...].astype(F32)

    def squeeze(load, index):
        index = jnp.broadcast_to(index, (8, 128))
        return pick_columns(load, range(blocks), index >> 7, index & 127, jnp.zeros((8, 128), F32))

    def block_of(ref, g):
        return lambda b: ref[8 * g : 8 * g + 8, 128 * b : 128 * b + 128]

    fine_base = jnp.concatenate([squeeze(block_of(base, g), fine_at) for g in range(4)], axis=0)
    facts = squeeze(block_of(geometry, 0), fine_at)
    fine_geometry = [facts[i : i + 1] for i in range(5)]
    fine_alpha = alpha_of(*fine_geometry)
    fine_factors = flux_factors(*fine_geometry)
    fine_codes = [spread(facts[5 + f : 6 + f].astype(jnp.int32)) for f in range(3)]

    lane = iota((1, 128), 1)
    wanted = jnp.where(
        lane < REG_FINE,
        send_reg_ref[1:2, 0:128],
        jnp.where(
            lane < 2 * REG_FINE,
            pltpu.roll(send_reg_ref[0:1, 0:128], REG_FINE, 1),
            jnp.where(
                lane < 2 * REG_FINE + DOM_FINE,
                pltpu.roll(send_dom_ref[1:2, :], 2 * REG_FINE, 1),
                pltpu.roll(send_dom_ref[0:1, :], 2 * REG_FINE + DOM_FINE, 1),
            ),
        ),
    )
    wanted_face = (wanted >= elems).astype(jnp.int32) + (wanted >= 2 * elems).astype(jnp.int32)
    wanted_face = spread(wanted_face)
    rank_rows = jnp.broadcast_to(fine_rank.astype(F32), (8, elems))
    wanted_at = squeeze(
        lambda b: rank_rows[:, 128 * b : 128 * b + 128], wanted - elems * wanted_face[0:1]
    ).astype(jnp.int32)
    wanted_at = spread(wanted_at[0:1]) & 127

    wait_recv(first_pairs)

    def early_slot(k):
        k = k - 3 * blocks
        return in_reg[0, k // 2, k % 2] if k < 4 else in_dom[0, k - 4]

    outer = [
        pick_columns(early_slot, remote, code >> 7, code & 127, jnp.zeros((16, 128), F32))
        for code in fine_codes
    ]
    fine_midway = fine_base + lifted(lift, fine_factors, outer, outer)
    fine = integrate(series_of(fine_midway, fine_alpha), FIRST_HALF)
    fine_table = dot(traces[0:48], split_state(fine))

    block = jnp.zeros((16, 128), F32)
    for f in range(3):
        found = jnp.take_along_axis(fine_table[16 * f : 16 * f + 16], wanted_at, axis=1)
        block = jnp.where(wanted_face == f, found, block)
    lane8 = iota((8, 128), 1)
    block = jnp.where(lane8 < FINE_LANES, block[0:8], pltpu.roll(block[8:16], FINE_LANES, 1))
    out_fine[0] = block
    out_fine[1] = block
    fine_copies = []
    for i, (exists, device, _, at) in enumerate(sides):
        fine_copies.append(
            (
                exists,
                comes[2 * (i // 2) + at],
                pltpu.make_async_remote_copy(
                    src_ref=out_fine.at[at],
                    dst_ref=in_fine.at[i],
                    send_sem=ss_fine.at[i // 2],
                    recv_sem=rs_fine.at[i // 2],
                    device_id=device,
                    device_id_type=MESH,
                ),
            )
        )
    start(fine_copies)
    fine_pairs = [
        (
            sizes(out_fine, in_fine.at[pl.ds(2 * i, 2)], ss_fine.at[i], rs_fine.at[i]),
            sizes(out_fine.at[0], in_fine.at[2 * i], ss_fine.at[i], rs_fine.at[i]),
        )
        for i in range(2)
    ]
    pl.semaphore_wait(ready.at[1], 2)
    announce(2, 2)
    for t in range(n_dom):
        pl.when(within(t, 4))(land_copies[t].start)

    for b in range(blocks):
        columns = slice(128 * b, 128 * b + 128)
        index = jnp.broadcast_to(fine_rank[:, columns] & 127, (8, 128))
        mine = jnp.broadcast_to(cluster_ref[:, columns], (8, 128)) == 0
        for g in range(4):
            rows = slice(8 * g, 8 * g + 8)
            found = jnp.take_along_axis(fine[rows], index, axis=1)
            dense[rows, columns] = jnp.where(mine, found, later[rows, columns])
    second_split = split_state(dense[...])
    tab_c[...] = dot(traces, second_split)
    local_part(tab_c)
    wait_recv(late_pairs)

    lane16 = iota((16, 128), 1)
    both = []
    for k in range(6):
        first = early_slot(3 * blocks + k)
        if k < 4:
            coarse = in_reg[1, k // 2, k % 2]
            if k % 2 == 0:
                coarse = jnp.where(lane16 < REG_FINE, 0.0, coarse)
        else:
            coarse = jnp.where(lane16 < DOM_FINE, 0.0, in_dom[1, k - 4])
        both.append(first + coarse)
    columns = {}
    for f in range(3):
        for b in range(blocks):
            code = code_of(f, b)
            columns[f, b] = fine_column(code)
            beyond[f, b] = pick_columns(
                lambda k: both[k - 3 * blocks], remote, code >> 7, code & 127, beyond[f, b]
            )
    dense[...] = base[...] + increment(second_split, tab_c)
    pl.semaphore_wait(ready.at[2], 2)
    for t in range(n_dom):
        pl.when((t != d) & jnp.logical_not(within(t, 4)))(land_copies[t].start)
    wait_recv(fine_pairs)
    at = lane8 & (FINE_LANES - 1)
    fresh = jnp.where(
        at < REG_FINE,
        in_fine[0],
        jnp.where(
            at < 2 * REG_FINE,
            in_fine[1],
            jnp.where(at < 2 * REG_FINE + DOM_FINE, in_fine[2], in_fine[3]),
        ),
    )
    outer = []
    for f in range(3):
        late = []
        for b in range(blocks):
            column = columns[f, b][0:8] & (FINE_LANES - 1)
            low = jnp.take_along_axis(fresh, column, axis=1)
            high = jnp.take_along_axis(fresh, column + FINE_LANES, axis=1)
            found = jnp.concatenate([low, high], axis=0)
            late.append(jnp.where(columns[f, b] >= 0, found, 0.0))
        outer.append(jnp.concatenate(late, axis=1))
    dense[...] = dense[...] + lifted(lift, factors, outer, outer)

    def cell(g, b):
        return dense[8 * g : 8 * g + 8, 128 * b : 128 * b + 128]

    group = iota((8, 128), 1) >> 5
    packed = {}
    for q in range(padded // 128):
        index = jnp.broadcast_to(leaves[:, 128 * q : 128 * q + 128], (8, 128))
        for g in range(4):
            packed[g, q] = pick_columns(
                lambda b: cell(g, b), range(blocks), index >> 7, index & 127, jnp.zeros((8, 128), F32)
            )
    for t in range(n_dom):
        tile = jnp.zeros((8, 128), F32)
        for g in range(4):
            shift = (32 * (g - (t & 3))) % 128
            moved = packed[g, t // 4]
            if shift:
                moved = pltpu.roll(moved, shift, 1)
            tile = jnp.where(group == g, moved, tile)
        tile_out[t] = tile
        pl.when(t != d)(tile_copies[t].start)
    land_all.wait_recv()
    kk = iota((1, 128), 1)
    stack = []
    for q in range(padded // 128):
        row_q = jnp.full((1, 128), -1, jnp.int32)
        for k in range(4 * q, min(4 * q + 4, n_dom)):
            row_q = jnp.where((kk >> 5) == (k & 3), land_in[k], row_q)
        stack.append(row_q)
    places = jnp.concatenate(stack, axis=1)
    comes_here = jnp.where(iota((elems, padded), 0) == places, 1.0, 0.0).astype(BF16)
    column = iota((8, padded), 1)
    row8 = iota((8, padded), 0)
    facts = jnp.where(row8 == 0, column >> 1, jnp.where(row8 == 1, column & 1, 1))
    found = dot_nt(facts.astype(F32).astype(BF16), comes_here).astype(jnp.int32)
    origin = jnp.where(found[2:3] > 0, found[0:1] * 2 + found[1:2], -1)

    wait_send(first_pairs)
    wait_send(late_pairs)
    wait_send(fine_pairs)
    land_all.wait_send()
    tile_all.wait_send()
    result = {(g, b): cell(g, b) for g in range(4) for b in range(blocks)}
    for q in range(padded // 128):
        senders = range(4 * q, min(4 * q + 4, n_dom))
        if not senders:
            continue
        full, short = (
            sizes(tile_out.at[rows], tile_in.at[rows], ss_tile, rs_tile.at[q])
            for rows in (pl.ds(4 * q, len(senders)), pl.ds(4 * q, len(senders) - 1))
        )
        either(d // 4 == q, short.wait_recv, full.wait_recv)
        for g in range(4):
            rows = jnp.zeros((8, 128), F32)
            for t in senders:
                shift = (32 * ((t & 3) - g)) % 128
                moved = tile_in[t]
                if shift:
                    moved = pltpu.roll(moved, shift, 1)
                rows = jnp.where(group == (t & 3), moved, rows)
            for b in range(blocks):
                index = jnp.broadcast_to(origin[:, 128 * b : 128 * b + 128], (8, 128))
                found = jnp.take_along_axis(rows, index & 127, axis=1)
                result[g, b] = jnp.where((index >> 7) == q, found, result[g, b])
    for g in range(4):
        for b in range(blocks):
            dense[8 * g : 8 * g + 8, 128 * b : 128 * b + 128] = result[g, b]
    for v in range(3):
        out_ref[:, v, :] = dense[NODES * v : NODES * (v + 1), :]


def shards(n_region, n_dom, *args):
    (
        water_state,
        water_depth,
        metric,
        diff_ops,
        stiff_ops,
        trace_ops,
        lift_ops,
        cluster,
        face_code,
        send_region,
        send_dom,
        move_dom,
        move_slot,
    ) = args
    elems = water_state.shape[2]
    blocks = elems // 128
    vmem = pl.BlockSpec(memory_space=pltpu.VMEM)
    dma = pltpu.SemaphoreType.DMA

    def kernel(*refs):
        step_kernel(n_region, n_dom, elems, *refs)

    given = (
        jnp.transpose(water_state, (1, 0, 2)),
        water_depth.reshape(1, elems),
        metric,
        jnp.transpose(diff_ops, (1, 0, 2)),
        jnp.transpose(stiff_ops, (1, 0, 2)),
        trace_ops,
        jnp.transpose(lift_ops, (0, 2, 1)),
        cluster.reshape(1, elems),
        face_code,
        send_region,
        send_dom,
        move_dom.reshape(1, elems),
        move_slot.reshape(1, elems),
        *pattern(),
    )
    result = pl.pallas_call(
        kernel,
        out_shape=pltpu.VMEM((NODES, 3, elems), F32),
        in_specs=[pl.BlockSpec(memory_space=pl.ANY)] * len(given),
        out_specs=vmem,
        scratch_shapes=[pltpu.VMEM(x.shape, x.dtype) for x in given]
        + [
            dma((len(given),)),
            pltpu.SemaphoreType.REGULAR((3,)),
            pltpu.VMEM((32, 16), F32),
            pltpu.VMEM((32, 16), F32),
            pltpu.VMEM((16, 16), F32),
            pltpu.VMEM((32, elems), F32),
            pltpu.VMEM((32, elems), F32),
            pltpu.VMEM((8, elems), F32),
            pltpu.VMEM((96, elems), F32),
            pltpu.VMEM((48, elems), F32),
            pltpu.VMEM((96, elems), F32),
            pltpu.VMEM((3, blocks, 16, 128), F32),
            pltpu.VMEM((2, 2, 2, 16, 128), F32),
            pltpu.VMEM((2, 2, 16, 128), F32),
            pltpu.VMEM((2, 2, 2, 16, 128), F32),
            pltpu.VMEM((2, 2, 16, 128), F32),
            pltpu.VMEM((2, 8, 128), F32),
            pltpu.VMEM((4, 8, 128), F32),
            pltpu.VMEM((n_dom, 1, 128), jnp.int32),
            pltpu.VMEM((n_dom, 1, 128), jnp.int32),
            pltpu.VMEM((n_dom, 8, 128), F32),
            pltpu.VMEM((n_dom, 8, 128), F32),
            dma((2,)),
            dma((2,)),
            dma((2,)),
            dma((2,)),
            dma((2,)),
            dma((2,)),
            dma,
            dma,
            dma,
            dma((-(-n_dom // 4),)),
        ],
        compiler_params=pltpu.CompilerParams(collective_id=0, has_side_effects=True),
        name="wave_step",
    )(*given)
    return jnp.transpose(result, (1, 0, 2))


def solution(mesh):
    both = ("region", "dom")
    wide, flat = P(None, both), P(both)
    placed = (
        P(None, None, both),
        flat,
        wide,
        P(),
        P(),
        P(),
        P(),
        flat,
        wide,
        wide,
        wide,
        flat,
        flat,
    )
    n_region, n_dom = mesh.shape["region"], mesh.shape["dom"]

    def step(*args):
        return shards(n_region, n_dom, *args)

    return jax.shard_map(
        step,
        mesh=mesh,
        in_specs=placed,
        out_specs=P(None, None, both),
        check_vma=False,
    )
```

```python
import jax
import jax.numpy as jnp
import numpy as np
from jax import lax
from jax.experimental import pallas as pl
from jax.experimental.pallas import tpu as pltpu
from jax.sharding import PartitionSpec as P

MESH = pl.DeviceIdType.MESH
F32 = jnp.float32
BF16 = jnp.bfloat16
NODES = 10
FIRST_HALF = (0.5, 0.125, 1.0 / 48.0, 1.0 / 384.0)
SECOND_HALF = (0.5, 0.375, 7.0 / 48.0, 15.0 / 384.0)
MIGRANTS = 32
REG_FINE = 8
DOM_FINE = 4
FINE_LANES = 32
EARLY_LOADS = (3, 5, 13, 0, 1, 2, 9, 10)
LATE_LOADS = (4, 6, 7, 8, 11, 12, 14)


def iota(shape, dim):
    return lax.broadcasted_iota(jnp.int32, shape, dim)


def dot(a, b):
    return jnp.dot(a, b, preferred_element_type=F32)


def dot_nt(a, b):
    return lax.dot_general(a, b, (((1,), (1,)), ((), ())), preferred_element_type=F32)


def split_state(values):
    hi = values.astype(BF16)
    lo = (values - hi.astype(F32)).astype(BF16)
    return jnp.concatenate([hi, lo, hi], axis=0)


def pattern():
    pick = np.zeros((192, 32), np.float32)
    mask = np.zeros((192, 96), np.float32)
    columns = np.zeros((2, 16, 96), np.float32)
    for column in range(96):
        third, at = divmod(column, 32)
        if at < 3 * NODES:
            columns[third // 2, at % NODES, column] = 1.0

    def fill(row, source, var, sign):
        pick[row, source] = 1.0
        for third in range(3):
            first = 32 * third + NODES * var
            mask[row, first : first + NODES] = sign

    for which in range(2):
        for at in range(3 * NODES):
            node, part = at % NODES, at // NODES
            fill(32 * which + at, NODES * which + node, 1 if part == 0 else 0, -1.0)
        for node in range(NODES):
            fill(64 + 16 * which + node, NODES * which + node, 2, -1.0)
    for order in range(2):
        for face in range(3):
            for at in range(16):
                part, point = divmod(at, 4)
                source = 2 * NODES + 4 * face + (point if order else 3 - point)
                fill(96 + 48 * order + 16 * face + at, source, part % 3, 1.0)

    nodes = np.zeros((32, 16), np.float32)
    for row in range(3 * NODES):
        nodes[row, row % NODES] = 1.0
    places = np.zeros((2, 16, 288), np.float32)
    signs = np.zeros((32, 288), np.float32)
    for column in range(288):
        third, rest = divmod(column, 96)
        face, at = divmod(rest, 32)
        jump, at = divmod(at, 16)
        part, point = divmod(at, 4)
        places[third // 2, 4 * face + point, column] = 1.0
        for row in range(3 * NODES):
            var = row // NODES
            if jump:
                signs[row, column] = 1.0 if part == var else 0.0
            else:
                signs[row, column] = -1.0 if part in ((1, 2), (0,), (3,))[var] else 0.0
    first = np.zeros((416, 128), np.float32)
    first[0:192, 0:96] = mask
    first[192:384, 0:32] = pick
    first[384:416, 0:96] = columns.reshape(32, 96)
    second = np.zeros((96, 288), np.float32)
    second[0:32] = places.reshape(32, 288)
    second[32:64] = signs
    second[64:96, 0:16] = nodes
    return [jnp.asarray(x, BF16) for x in (first, second)]


def halves(values):
    hi = values.astype(BF16)
    return hi, (values - hi.astype(F32)).astype(BF16)


def spread_columns(values, first_ref):
    hi, lo = halves(values)
    return (
        dot(hi, first_ref[384:400, 0:96]) + dot(lo, first_ref[400:416, 0:96])
    ).astype(BF16)


def combine(slopes, alpha):
    a1, a2, a3, a4 = alpha
    both = a1 * slopes[0:32] + a2 * slopes[32:64]
    top = a3 * slopes[64:80] + a4 * slopes[80:96]
    return jnp.concatenate([both[0:16] + top, both[16:32]], axis=0)


def alpha_of(depth, m0, m1, m2, m3):
    row = iota((32, depth.shape[1]), 0)
    top = row[0:16] < NODES
    return (
        jnp.where(row < 10, m0, jnp.where(row < 20, depth * m0, depth * m2)),
        jnp.where(row < 10, m1, jnp.where(row < 20, depth * m1, depth * m3)),
        jnp.where(top, m2, 0.0),
        jnp.where(top, m3, 0.0),
    )


def flux_factors(depth, m0, m1, m2, m3):
    rows = iota((16, depth.shape[1]), 0)
    root = jnp.sqrt(depth)
    factors = []
    for hx, hy in ((-m1, -m3), (m0 + m1, m2 + m3), (-m0, -m2)):
        centre = jnp.where(
            rows < 4,
            depth * hx,
            jnp.where(rows < 8, hx, jnp.where(rows < 12, hy, depth * hy)),
        )
        factors.append((centre, root * jnp.sqrt(hx * hx + hy * hy)))
    return factors


def lifted(lift, factors, sums, differences):
    parts = []
    for (centre, jump), added, taken in zip(factors, sums, differences):
        parts.append(centre * added)
        parts.append(jump * taken)
    return dot(lift, split_state(jnp.concatenate(parts, axis=0)))


def pick_columns(load, sources, block, lane, start):
    out = start
    for k in sources:
        found = jnp.take_along_axis(load(k), lane, axis=1)
        out = jnp.where(block == k, found, out)
    return out


def step_kernel(
    n_region,
    n_dom,
    elems,
    state_ref,
    depth_ref,
    metric_ref,
    diff_ref,
    stiff_ref,
    trace_ref,
    lift_ref,
    cluster_ref,
    code_ref,
    send_reg_ref,
    send_dom_ref,
    move_dom_ref,
    move_slot_ref,
    first_ref,
    second_ref,
    out_ref,
    *scratch,
):
    hbm_refs = (
        state_ref,
        depth_ref,
        metric_ref,
        diff_ref,
        stiff_ref,
        trace_ref,
        lift_ref,
        cluster_ref,
        code_ref,
        send_reg_ref,
        send_dom_ref,
        move_dom_ref,
        move_slot_ref,
        first_ref,
        second_ref,
    )
    step_body(
        n_region, n_dom, elems, hbm_refs, out_ref, scratch[: len(hbm_refs)], *scratch[len(hbm_refs) :]
    )


def step_body(
    n_region,
    n_dom,
    elems,
    hbm_refs,
    out_ref,
    local_refs,
    in_sem,
    ready,
    first_ops,
    second_ops,
    lift_ops,
    dense,
    base,
    geometry,
    tab_a,
    tab_b,
    tab_c,
    beyond,
    out_reg,
    out_dom,
    in_reg,
    in_dom,
    out_fine,
    in_fine,
    land_out,
    land_in,
    tile_out,
    tile_in,
    ss_reg,
    rs_reg,
    ss_dom,
    rs_dom,
    ss_fine,
    rs_fine,
    ss_land,
    rs_land,
    ss_tile,
    rs_tile,
):
    r = lax.axis_index("region")
    d = lax.axis_index("dom")
    blocks = elems // 128
    has_low = r > 0
    has_high = r < n_region - 1
    dom_low = d > 0
    dom_high = d < n_dom - 1
    sides = (
        (has_high, {"region": r + 1}, 1, 0),
        (has_low, {"region": r - 1}, 0, 1),
        (dom_high, {"dom": d + 1}, 1, 0),
        (dom_low, {"dom": d - 1}, 0, 1),
    )
    comes = (has_low, has_high, dom_low, dom_high)

    loads = [
        pltpu.make_async_copy(src, dst, in_sem.at[i])
        for i, (src, dst) in enumerate(zip(hbm_refs, local_refs))
    ]
    barrier = pltpu.get_barrier_semaphore()

    def ring(k):
        return {"dom": lax.rem(d + k + n_dom, n_dom)}

    for i in EARLY_LOADS:
        loads[i].start()
    for exists, device, _, _ in sides[:2]:

        @pl.when(exists)
        def _():
            pl.semaphore_signal(barrier, inc=1, device_id=device, device_id_type=MESH)

    for k in (1, -1):
        pl.semaphore_signal(barrier, inc=1, device_id=ring(k), device_id_type=MESH)
    for i in LATE_LOADS:
        loads[i].start()

    def announce(stage, reach):
        for k in (reach, -reach):
            pl.semaphore_signal(
                ready.at[stage], inc=1, device_id=ring(k), device_id_type=MESH
            )

    (
        state_ref,
        depth_ref,
        metric_ref,
        diff_ref,
        stiff_ref,
        trace_ref,
        lift_ref,
        cluster_ref,
        code_ref,
        send_reg_ref,
        send_dom_ref,
        move_dom_ref,
        move_slot_ref,
        first_ref,
        second_ref,
    ) = local_refs
    first_ops[...] = jnp.zeros((32, 16), F32)
    second_ops[...] = jnp.zeros((32, 16), F32)
    lift_ops[...] = jnp.zeros((16, 16), F32)
    for i in EARLY_LOADS[:3]:
        loads[i].wait()

    for a in range(2):
        first_ops[NODES * a : NODES * (a + 1), 0:NODES] = diff_ref[:, a, :]
    for f in range(3):
        first_ops[2 * NODES + 4 * f : 2 * NODES + 4 * f + 4, 0:NODES] = trace_ref[f]
    wide = dot(first_ref[192:384, 0:32], spread_columns(first_ops[...], first_ref)).astype(BF16)
    wide = wide * first_ref[0:192, 0:96]
    slope, traces = wide[0:96], wide[96:192]

    for i in EARLY_LOADS[3:]:
        loads[i].wait()

    dense[30:32, :] = jnp.zeros((2, elems), F32)
    for v in range(3):
        dense[NODES * v : NODES * (v + 1), :] = state_ref[:, v, :]
    state = dense[...]
    depth = depth_ref[...]
    m0, m1, m2, m3 = (metric_ref[i : i + 1, :] for i in range(4))

    alpha = alpha_of(depth, m0, m1, m2, m3)

    def series_of(values, alpha):
        series = [values]
        for _ in range(3):
            series.append(combine(dot(slope, split_state(series[-1])), alpha))
        return series

    def integrate(series, factors):
        summed = factors[0] * series[0]
        for factor, member in zip(factors[1:], series[1:]):
            summed = summed + factor * member
        return summed

    series = series_of(state, alpha)
    early = integrate(series, FIRST_HALF)
    early_split = split_state(early)
    tab_a[0:48] = dot(traces[0:48], early_split)

    def source(table):
        def load(k):
            f, b = divmod(k, blocks)
            return table[16 * f : 16 * f + 16, 128 * b : 128 * b + 128]

        return load

    def spread(vector):
        return jnp.broadcast_to(vector, (16, 128))

    own = range(3 * blocks)

    def gather_sends(which, table, copies):
        for i, (exists, _, copy) in enumerate(copies):
            lane_row = sides[i][2]
            if i < 2:
                for b in range(2):
                    index = spread(send_reg_ref[lane_row : lane_row + 1, 128 * b : 128 * b + 128])
                    out_reg[which, lane_row, b] = pick_columns(
                        source(table), own, index >> 7, index & 127, jnp.zeros((16, 128), F32)
                    )
            else:
                index = spread(send_dom_ref[lane_row : lane_row + 1, :])
                out_dom[which, lane_row] = pick_columns(
                    source(table), own, index >> 7, index & 127, jnp.zeros((16, 128), F32)
                )
            pl.when(exists)(copy.start)

    def copies_a(which):
        copies = []
        for i, (exists, device, lane_row, at) in enumerate(sides):
            regional = i < 2
            copies.append(
                (
                    exists,
                    comes[2 * (i // 2) + at],
                    pltpu.make_async_remote_copy(
                        src_ref=(out_reg if regional else out_dom).at[which, lane_row],
                        dst_ref=(in_reg if regional else in_dom).at[which, at],
                        send_sem=(ss_reg if regional else ss_dom).at[which],
                        recv_sem=(rs_reg if regional else rs_dom).at[which],
                        device_id=device,
                        device_id_type=MESH,
                    ),
                )
            )
        return copies

    def start(copies):
        for exists, _, copy in copies:
            pl.when(exists)(copy.start)

    def sizes(src, dst, ss, rs):
        return pltpu.make_async_remote_copy(
            src_ref=src,
            dst_ref=dst,
            send_sem=ss,
            recv_sem=rs,
            device_id=ring(1),
            device_id_type=MESH,
        )

    def either(condition, yes, no):
        pl.when(condition)(yes)
        pl.when(jnp.logical_not(condition))(no)

    inner = (has_low & has_high, dom_low & dom_high)

    def pairs_a(which):
        return [
            (sizes(src.at[which], dst.at[which], *sems), sizes(src.at[which, 0], dst.at[which, 0], *sems))
            for src, dst, sems in (
                (out_reg, in_reg, (ss_reg.at[which], rs_reg.at[which])),
                (out_dom, in_dom, (ss_dom.at[which], rs_dom.at[which])),
            )
        ]

    def wait_recv(pairs):
        for condition, (two, one) in zip(inner, pairs):
            either(condition, two.wait_recv, one.wait_recv)

    def wait_send(pairs):
        for condition, (two, one) in zip(inner, pairs):
            either(condition, two.wait_send, one.wait_send)

    first_copies = copies_a(0)
    late_copies = copies_a(1)
    first_pairs, late_pairs = pairs_a(0), pairs_a(1)
    pl.semaphore_wait(barrier, 2 + has_low.astype(jnp.int32) + has_high.astype(jnp.int32))
    announce(0, 1)
    gather_sends(0, tab_a, first_copies)

    later = integrate(series, SECOND_HALF)
    tab_b[...] = dot(traces[0:48], split_state(later))
    gather_sends(1, tab_b, late_copies)

    tile_in[d] = jnp.zeros((8, 128), F32)
    land_in[d] = jnp.full((1, 128), -1, jnp.int32)
    for i in range(2):

        @pl.when(jnp.logical_not(comes[i]))
        def _():
            in_reg[:, i] = jnp.zeros(in_reg.shape[0:1] + in_reg.shape[2:], F32)

        @pl.when(jnp.logical_not(comes[2 + i]))
        def _():
            in_dom[:, i] = jnp.zeros(in_dom.shape[0:1] + in_dom.shape[2:], F32)

    for i in range(4):

        @pl.when(jnp.logical_not(comes[i]))
        def _():
            in_fine[i] = jnp.zeros((8, 128), F32)

    for i in LATE_LOADS:
        loads[i].wait()
    tab_a[48:96] = dot(traces[48:96], early_split)
    for a in range(2):
        second_ops[NODES * a : NODES * (a + 1), 0:NODES] = stiff_ref[:, a, :]
    stiff = dot(first_ref[192:288, 0:32], spread_columns(second_ops[...], first_ref)).astype(BF16)
    stiff = -(stiff * first_ref[0:96, 0:96])
    for f in range(3):
        lift_ops[4 * f : 4 * f + 4, 0:NODES] = lift_ref[f]
    hi, lo = halves(lift_ops[...])
    nodes = second_ref[64:96, 0:16]
    lift = dot(dot_nt(nodes, hi).astype(BF16), second_ref[0:16])
    lift = lift + dot(dot_nt(nodes, lo).astype(BF16), second_ref[16:32])
    lift = lift.astype(BF16) * second_ref[32:64]
    factors = flux_factors(depth, m0, m1, m2, m3)
    mirror = jnp.where((iota((16, 128), 0) >= 4) & (iota((16, 128), 0) < 12), -1.0, 1.0)
    first_code = 3 * elems
    regional = 2 * send_reg_ref.shape[1]
    wall_code = first_code + regional + 2 * send_dom_ref.shape[1]
    remote = range(3 * blocks, 3 * blocks + 6)

    def code_of(f, b):
        return spread(code_ref[f : f + 1, 128 * b : 128 * b + 128])

    def local_part(table):
        for f in range(3):
            for b in range(blocks):
                code = code_of(f, b)
                wall = mirror * table[48 + 16 * f : 64 + 16 * f, 128 * b : 128 * b + 128]
                wall = jnp.where(code == wall_code, wall, 0.0)
                beyond[f, b] = pick_columns(source(table), own, code >> 7, code & 127, wall)

    def increment(values_split, table):
        volume = combine(dot(stiff, values_split), alpha)
        outside = [jnp.concatenate([beyond[f, b] for b in range(blocks)], axis=1) for f in range(3)]
        inside = [table[48 + 16 * f : 64 + 16 * f, :] for f in range(3)]
        return volume + lifted(
            lift,
            factors,
            [x + y for x, y in zip(outside, inside)],
            [x - y for x, y in zip(outside, inside)],
        )

    def fine_column(code):
        slot = code - first_code
        reg = slot & 255
        from_reg = jnp.where(
            (slot >= 0) & (slot < regional) & (reg < REG_FINE), (slot >> 8) * REG_FINE + reg, -1
        )
        past = slot - regional
        dom = past & 127
        return jnp.where(
            (past >= 0) & (past < 256) & (dom < DOM_FINE),
            2 * REG_FINE + (past >> 7) * DOM_FINE + dom,
            from_reg,
        )

    local_part(tab_a)
    base[...] = state + increment(early_split, tab_a)
    pl.semaphore_wait(ready.at[0], 2)
    announce(1, 2)

    def to_peers(src, dst, ss, rs):
        return [
            pltpu.make_async_remote_copy(
                src_ref=src.at[t],
                dst_ref=dst.at[d],
                send_sem=ss,
                recv_sem=rs,
                device_id={"dom": t},
                device_id_type=MESH,
            )
            for t in range(n_dom)
        ]

    others = pl.ds(0, n_dom - 1)
    land_copies = to_peers(land_out, land_in, ss_land, rs_land)
    land_all = sizes(land_out.at[others], land_in.at[others], ss_land, rs_land)
    tile_copies = to_peers(tile_out, tile_in, ss_tile, rs_tile.at[d // 4])
    tile_all = sizes(tile_out.at[others], tile_in.at[others], ss_tile, rs_tile.at[0])

    def within(t, reach):
        apart = lax.rem(t - d + n_dom, n_dom)
        return (apart != 0) & ((apart <= reach) | (apart >= n_dom - reach))

    lanes = iota((1, elems), 1)
    target = move_dom_ref[...]
    target = jnp.where(target == d, -1, target)
    fine_row = 15
    is_fine = cluster_ref[...] == 0
    kind = iota((16, elems), 0)
    chosen = jnp.where(kind == target, 1.0, 0.0)
    chosen = jnp.where(kind == fine_row, jnp.where(is_fine, 1.0, 0.0), chosen)
    before = jnp.where(iota((elems, elems), 0) < iota((elems, elems), 1), 1.0, 0.0).astype(BF16)
    ranks = dot(chosen.astype(BF16), before)
    rank = jnp.sum(jnp.where(kind < fine_row, chosen * ranks, 0.0), axis=0, keepdims=True)
    fine_rank = ranks[fine_row:].astype(jnp.int32)
    fine_position = jnp.where(is_fine, fine_rank, -1)
    slots = n_dom * MIGRANTS
    padded = 384 if slots <= 384 else 128 * (-(-slots // 128))
    position = jnp.where(target < 0, -1, target * MIGRANTS + rank.astype(jnp.int32))
    inverse = jnp.concatenate(
        [
            jnp.where(iota((padded, elems), 0) == position, 1.0, 0.0),
            jnp.where(iota((128, elems), 0) == fine_position, 1.0, 0.0),
        ],
        axis=0,
    ).astype(BF16)
    place = move_slot_ref[...]
    which_row = iota((8, elems), 0)
    facts = jnp.where(
        which_row == 0,
        lanes >> 1,
        jnp.where(
            which_row == 1, lanes & 1, jnp.where(which_row == 2, place >> 1, place & 1)
        ),
    )
    facts = jnp.where(which_row < 4, facts, 0).astype(F32).astype(BF16)
    found = dot_nt(facts, inverse).astype(jnp.int32)
    leaves = found[0:1] * 2 + found[1:2]
    lands = found[2:3] * 2 + found[3:4]
    fine_at = leaves[:, padded : padded + 128]
    for t in range(n_dom):
        row = jnp.broadcast_to(lands[:, 128 * (t // 4) : 128 * (t // 4) + 128], (8, 128))
        row = jnp.take_along_axis(row, (iota((8, 128), 1) & 31) + 32 * (t & 3), axis=1)
        land_out[t] = row[0:1]

    geometry[0:1] = depth
    geometry[1:5] = metric_ref[...]
    geometry[5:8] = code_ref[...].astype(F32)

    def squeeze(load, index):
        index = jnp.broadcast_to(index, (8, 128))
        return pick_columns(load, range(blocks), index >> 7, index & 127, jnp.zeros((8, 128), F32))

    def block_of(ref, g):
        return lambda b: ref[8 * g : 8 * g + 8, 128 * b : 128 * b + 128]

    fine_base = jnp.concatenate([squeeze(block_of(base, g), fine_at) for g in range(4)], axis=0)
    facts = squeeze(block_of(geometry, 0), fine_at)
    fine_geometry = [facts[i : i + 1] for i in range(5)]
    fine_alpha = alpha_of(*fine_geometry)
    fine_factors = flux_factors(*fine_geometry)
    fine_codes = [spread(facts[5 + f : 6 + f].astype(jnp.int32)) for f in range(3)]

    lane = iota((1, 128), 1)
    wanted = jnp.where(
        lane < REG_FINE,
        send_reg_ref[1:2, 0:128],
        jnp.where(
            lane < 2 * REG_FINE,
            pltpu.roll(send_reg_ref[0:1, 0:128], REG_FINE, 1),
            jnp.where(
                lane < 2 * REG_FINE + DOM_FINE,
                pltpu.roll(send_dom_ref[1:2, :], 2 * REG_FINE, 1),
                pltpu.roll(send_dom_ref[0:1, :], 2 * REG_FINE + DOM_FINE, 1),
            ),
        ),
    )
    wanted_face = (wanted >= elems).astype(jnp.int32) + (wanted >= 2 * elems).astype(jnp.int32)
    wanted_face = spread(wanted_face)
    rank_rows = jnp.broadcast_to(fine_rank.astype(F32), (8, elems))
    wanted_at = squeeze(
        lambda b: rank_rows[:, 128 * b : 128 * b + 128], wanted - elems * wanted_face[0:1]
    ).astype(jnp.int32)
    wanted_at = spread(wanted_at[0:1]) & 127

    wait_recv(first_pairs)

    def early_slot(k):
        k = k - 3 * blocks
        return in_reg[0, k // 2, k % 2] if k < 4 else in_dom[0, k - 4]

    outer = [
        pick_columns(early_slot, remote, code >> 7, code & 127, jnp.zeros((16, 128), F32))
        for code in fine_codes
    ]
    fine_midway = fine_base + lifted(lift, fine_factors, outer, outer)
    fine = integrate(series_of(fine_midway, fine_alpha), FIRST_HALF)
    fine_table = dot(traces[0:48], split_state(fine))

    block = jnp.zeros((16, 128), F32)
    for f in range(3):
        found = jnp.take_along_axis(fine_table[16 * f : 16 * f + 16], wanted_at, axis=1)
        block = jnp.where(wanted_face == f, found, block)
    lane8 = iota((8, 128), 1)
    block = jnp.where(lane8 < FINE_LANES, block[0:8], pltpu.roll(block[8:16], FINE_LANES, 1))
    out_fine[0] = block
    out_fine[1] = block
    fine_copies = []
    for i, (exists, device, _, at) in enumerate(sides):
        fine_copies.append(
            (
                exists,
                comes[2 * (i // 2) + at],
                pltpu.make_async_remote_copy(
                    src_ref=out_fine.at[at],
                    dst_ref=in_fine.at[i],
                    send_sem=ss_fine.at[i // 2],
                    recv_sem=rs_fine.at[i // 2],
                    device_id=device,
                    device_id_type=MESH,
                ),
            )
        )
    start(fine_copies)
    fine_pairs = [
        (
            sizes(out_fine, in_fine.at[pl.ds(2 * i, 2)], ss_fine.at[i], rs_fine.at[i]),
            sizes(out_fine.at[0], in_fine.at[2 * i], ss_fine.at[i], rs_fine.at[i]),
        )
        for i in range(2)
    ]
    pl.semaphore_wait(ready.at[1], 2)
    announce(2, 2)
    for t in range(n_dom):
        pl.when(within(t, 4))(land_copies[t].start)

    for b in range(blocks):
        columns = slice(128 * b, 128 * b + 128)
        index = jnp.broadcast_to(fine_rank[:, columns] & 127, (8, 128))
        mine = jnp.broadcast_to(cluster_ref[:, columns], (8, 128)) == 0
        for g in range(4):
            rows = slice(8 * g, 8 * g + 8)
            found = jnp.take_along_axis(fine[rows], index, axis=1)
            dense[rows, columns] = jnp.where(mine, found, later[rows, columns])
    second_split = split_state(dense[...])
    tab_c[...] = dot(traces, second_split)
    local_part(tab_c)
    wait_recv(late_pairs)

    lane16 = iota((16, 128), 1)
    both = []
    for k in range(6):
        first = early_slot(3 * blocks + k)
        if k < 4:
            coarse = in_reg[1, k // 2, k % 2]
            if k % 2 == 0:
                coarse = jnp.where(lane16 < REG_FINE, 0.0, coarse)
        else:
            coarse = jnp.where(lane16 < DOM_FINE, 0.0, in_dom[1, k - 4])
        both.append(first + coarse)
    columns = {}
    for f in range(3):
        for b in range(blocks):
            code = code_of(f, b)
            columns[f, b] = fine_column(code)
            beyond[f, b] = pick_columns(
                lambda k: both[k - 3 * blocks], remote, code >> 7, code & 127, beyond[f, b]
            )
    dense[...] = base[...] + increment(second_split, tab_c)

    quarters = range(padded // 128)
    at_of = [leaves[:, 128 * q : 128 * q + 128] for q in quarters]
    packed_base = {(g, q): squeeze(block_of(dense, g), at_of[q]) for q in quarters for g in range(4)}
    packed_facts = [squeeze(block_of(geometry, 0), at_of[q]) for q in quarters]
    packed_factors = flux_factors(
        *(jnp.concatenate([facts[i : i + 1] for facts in packed_facts], axis=1) for i in range(5))
    )
    packed_columns = {
        (f, q): fine_column(spread(packed_facts[q][5 + f : 6 + f].astype(jnp.int32)))
        for f in range(3)
        for q in quarters
    }
    pl.semaphore_wait(ready.at[2], 2)
    for t in range(n_dom):
        pl.when((t != d) & jnp.logical_not(within(t, 4)))(land_copies[t].start)
    wait_recv(fine_pairs)
    at = lane8 & (FINE_LANES - 1)

    def fine_block():
        return jnp.where(
            at < REG_FINE,
            in_fine[0],
            jnp.where(
                at < 2 * REG_FINE,
                in_fine[1],
                jnp.where(at < 2 * REG_FINE + DOM_FINE, in_fine[2], in_fine[3]),
            ),
        )

    def fine_outer(columns, count):
        fresh = fine_block()
        outer = []
        for f in range(3):
            late = []
            for b in range(count):
                column = columns[f, b][0:8] & (FINE_LANES - 1)
                low = jnp.take_along_axis(fresh, column, axis=1)
                high = jnp.take_along_axis(fresh, column + FINE_LANES, axis=1)
                found = jnp.concatenate([low, high], axis=0)
                late.append(jnp.where(columns[f, b] >= 0, found, 0.0))
            outer.append(jnp.concatenate(late, axis=1))
        return outer

    outer = fine_outer(packed_columns, len(quarters))
    share = lifted(lift, packed_factors, outer, outer)

    def cell(g, b):
        return dense[8 * g : 8 * g + 8, 128 * b : 128 * b + 128]

    group = iota((8, 128), 1) >> 5
    packed = {
        (g, q): packed_base[g, q] + share[8 * g : 8 * g + 8, 128 * q : 128 * q + 128]
        for q in quarters
        for g in range(4)
    }
    for t in range(n_dom):
        tile = jnp.zeros((8, 128), F32)
        for g in range(4):
            shift = (32 * (g - (t & 3))) % 128
            moved = packed[g, t // 4]
            if shift:
                moved = pltpu.roll(moved, shift, 1)
            tile = jnp.where(group == g, moved, tile)
        tile_out[t] = tile
        pl.when(t != d)(tile_copies[t].start)
    wait_send(first_pairs)
    wait_send(late_pairs)
    wait_send(fine_pairs)
    land_all.wait_send()
    tile_all.wait_send()
    outer = fine_outer(columns, blocks)
    dense[...] = dense[...] + lifted(lift, factors, outer, outer)
    land_all.wait_recv()
    kk = iota((1, 128), 1)
    stack = []
    for q in range(padded // 128):
        row_q = jnp.full((1, 128), -1, jnp.int32)
        for k in range(4 * q, min(4 * q + 4, n_dom)):
            row_q = jnp.where((kk >> 5) == (k & 3), land_in[k], row_q)
        stack.append(row_q)
    places = jnp.concatenate(stack, axis=1)
    comes_here = jnp.where(iota((elems, padded), 0) == places, 1.0, 0.0).astype(BF16)
    column = iota((8, padded), 1)
    row8 = iota((8, padded), 0)
    facts = jnp.where(row8 == 0, column >> 1, jnp.where(row8 == 1, column & 1, 1))
    found = dot_nt(facts.astype(F32).astype(BF16), comes_here).astype(jnp.int32)
    origin = jnp.where(found[2:3] > 0, found[0:1] * 2 + found[1:2], -1)

    result = {(g, b): cell(g, b) for g in range(4) for b in range(blocks)}
    for q in range(padded // 128):
        senders = range(4 * q, min(4 * q + 4, n_dom))
        if not senders:
            continue
        full, short = (
            sizes(tile_out.at[rows], tile_in.at[rows], ss_tile, rs_tile.at[q])
            for rows in (pl.ds(4 * q, len(senders)), pl.ds(4 * q, len(senders) - 1))
        )
        either(d // 4 == q, short.wait_recv, full.wait_recv)
        for g in range(4):
            rows = jnp.zeros((8, 128), F32)
            for t in senders:
                shift = (32 * ((t & 3) - g)) % 128
                moved = tile_in[t]
                if shift:
                    moved = pltpu.roll(moved, shift, 1)
                rows = jnp.where(group == (t & 3), moved, rows)
            for b in range(blocks):
                index = jnp.broadcast_to(origin[:, 128 * b : 128 * b + 128], (8, 128))
                found = jnp.take_along_axis(rows, index & 127, axis=1)
                result[g, b] = jnp.where((index >> 7) == q, found, result[g, b])
    for g in range(4):
        for b in range(blocks):
            dense[8 * g : 8 * g + 8, 128 * b : 128 * b + 128] = result[g, b]
    for v in range(3):
        out_ref[:, v, :] = dense[NODES * v : NODES * (v + 1), :]


def shards(n_region, n_dom, *args):
    (
        water_state,
        water_depth,
        metric,
        diff_ops,
        stiff_ops,
        trace_ops,
        lift_ops,
        cluster,
        face_code,
        send_region,
        send_dom,
        move_dom,
        move_slot,
    ) = args
    elems = water_state.shape[2]
    blocks = elems // 128
    vmem = pl.BlockSpec(memory_space=pltpu.VMEM)
    dma = pltpu.SemaphoreType.DMA

    def kernel(*refs):
        step_kernel(n_region, n_dom, elems, *refs)

    given = (
        jnp.transpose(water_state, (1, 0, 2)),
        water_depth.reshape(1, elems),
        metric,
        jnp.transpose(diff_ops, (1, 0, 2)),
        jnp.transpose(stiff_ops, (1, 0, 2)),
        trace_ops,
        jnp.transpose(lift_ops, (0, 2, 1)),
        cluster.reshape(1, elems),
        face_code,
        send_region,
        send_dom,
        move_dom.reshape(1, elems),
        move_slot.reshape(1, elems),
        *pattern(),
    )
    result = pl.pallas_call(
        kernel,
        out_shape=pltpu.VMEM((NODES, 3, elems), F32),
        in_specs=[pl.BlockSpec(memory_space=pl.ANY)] * len(given),
        out_specs=vmem,
        scratch_shapes=[pltpu.VMEM(x.shape, x.dtype) for x in given]
        + [
            dma((len(given),)),
            pltpu.SemaphoreType.REGULAR((3,)),
            pltpu.VMEM((32, 16), F32),
            pltpu.VMEM((32, 16), F32),
            pltpu.VMEM((16, 16), F32),
            pltpu.VMEM((32, elems), F32),
            pltpu.VMEM((32, elems), F32),
            pltpu.VMEM((8, elems), F32),
            pltpu.VMEM((96, elems), F32),
            pltpu.VMEM((48, elems), F32),
            pltpu.VMEM((96, elems), F32),
            pltpu.VMEM((3, blocks, 16, 128), F32),
            pltpu.VMEM((2, 2, 2, 16, 128), F32),
            pltpu.VMEM((2, 2, 16, 128), F32),
            pltpu.VMEM((2, 2, 2, 16, 128), F32),
            pltpu.VMEM((2, 2, 16, 128), F32),
            pltpu.VMEM((2, 8, 128), F32),
            pltpu.VMEM((4, 8, 128), F32),
            pltpu.VMEM((n_dom, 1, 128), jnp.int32),
            pltpu.VMEM((n_dom, 1, 128), jnp.int32),
            pltpu.VMEM((n_dom, 8, 128), F32),
            pltpu.VMEM((n_dom, 8, 128), F32),
            dma((2,)),
            dma((2,)),
            dma((2,)),
            dma((2,)),
            dma((2,)),
            dma((2,)),
            dma,
            dma,
            dma,
            dma((-(-n_dom // 4),)),
        ],
        compiler_params=pltpu.CompilerParams(collective_id=0, has_side_effects=True),
        name="wave_step",
    )(*given)
    return jnp.transpose(result, (1, 0, 2))


def solution(mesh):
    both = ("region", "dom")
    wide, flat = P(None, both), P(both)
    placed = (
        P(None, None, both),
        flat,
        wide,
        P(),
        P(),
        P(),
        P(),
        flat,
        wide,
        wide,
        wide,
        flat,
        flat,
    )
    n_region, n_dom = mesh.shape["region"], mesh.shape["dom"]

    def step(*args):
        return shards(n_region, n_dom, *args)

    return jax.shard_map(
        step,
        mesh=mesh,
        in_specs=placed,
        out_specs=P(None, None, both),
        check_vma=False,
    )
```

```python
import jax
import jax.numpy as jnp
import numpy as np
from jax import lax
from jax.experimental import pallas as pl
from jax.experimental.pallas import tpu as pltpu
from jax.sharding import PartitionSpec as P

MESH = pl.DeviceIdType.MESH
F32 = jnp.float32
BF16 = jnp.bfloat16
NODES = 10
FIRST_HALF = (0.5, 0.125, 1.0 / 48.0, 1.0 / 384.0)
SECOND_HALF = (0.5, 0.375, 7.0 / 48.0, 15.0 / 384.0)
MIGRANTS = 32
REG_FINE = 8
DOM_FINE = 4
FINE_LANES = 32
EARLY_LOADS = (3, 5, 13, 0, 1, 2, 9, 10)
LATE_LOADS = (4, 6, 7, 8, 11, 12, 14)


def iota(shape, dim):
    return lax.broadcasted_iota(jnp.int32, shape, dim)


def dot(a, b):
    return jnp.dot(a, b, preferred_element_type=F32)


def dot_nt(a, b):
    return lax.dot_general(a, b, (((1,), (1,)), ((), ())), preferred_element_type=F32)


def split_state(values):
    hi = values.astype(BF16)
    lo = (values - hi.astype(F32)).astype(BF16)
    return jnp.concatenate([hi, lo, hi], axis=0)


def pattern():
    pick = np.zeros((192, 32), np.float32)
    mask = np.zeros((192, 96), np.float32)
    columns = np.zeros((2, 16, 96), np.float32)
    for column in range(96):
        third, at = divmod(column, 32)
        if at < 3 * NODES:
            columns[third // 2, at % NODES, column] = 1.0

    def fill(row, source, var, sign):
        pick[row, source] = 1.0
        for third in range(3):
            first = 32 * third + NODES * var
            mask[row, first : first + NODES] = sign

    for which in range(2):
        for at in range(3 * NODES):
            node, part = at % NODES, at // NODES
            fill(32 * which + at, NODES * which + node, 1 if part == 0 else 0, -1.0)
        for node in range(NODES):
            fill(64 + 16 * which + node, NODES * which + node, 2, -1.0)
    for order in range(2):
        for face in range(3):
            for at in range(16):
                part, point = divmod(at, 4)
                source = 2 * NODES + 4 * face + (point if order else 3 - point)
                fill(96 + 48 * order + 16 * face + at, source, part % 3, 1.0)

    nodes = np.zeros((32, 16), np.float32)
    for row in range(3 * NODES):
        nodes[row, row % NODES] = 1.0
    places = np.zeros((2, 16, 288), np.float32)
    signs = np.zeros((32, 288), np.float32)
    for column in range(288):
        third, rest = divmod(column, 96)
        face, at = divmod(rest, 32)
        jump, at = divmod(at, 16)
        part, point = divmod(at, 4)
        places[third // 2, 4 * face + point, column] = 1.0
        for row in range(3 * NODES):
            var = row // NODES
            if jump:
                signs[row, column] = 1.0 if part == var else 0.0
            else:
                signs[row, column] = -1.0 if part in ((1, 2), (0,), (3,))[var] else 0.0
    first = np.zeros((416, 128), np.float32)
    first[0:192, 0:96] = mask
    first[192:384, 0:32] = pick
    first[384:416, 0:96] = columns.reshape(32, 96)
    second = np.zeros((96, 288), np.float32)
    second[0:32] = places.reshape(32, 288)
    second[32:64] = signs
    second[64:96, 0:16] = nodes
    return [jnp.asarray(x, BF16) for x in (first, second)]


def halves(values):
    hi = values.astype(BF16)
    return hi, (values - hi.astype(F32)).astype(BF16)


def spread_columns(values, first_ref):
    hi, lo = halves(values)
    return (
        dot(hi, first_ref[384:400, 0:96]) + dot(lo, first_ref[400:416, 0:96])
    ).astype(BF16)


def combine(slopes, alpha):
    a1, a2, a3, a4 = alpha
    both = a1 * slopes[0:32] + a2 * slopes[32:64]
    top = a3 * slopes[64:80] + a4 * slopes[80:96]
    return jnp.concatenate([both[0:16] + top, both[16:32]], axis=0)


def alpha_of(depth, m0, m1, m2, m3):
    row = iota((32, depth.shape[1]), 0)
    top = row[0:16] < NODES
    return (
        jnp.where(row < 10, m0, jnp.where(row < 20, depth * m0, depth * m2)),
        jnp.where(row < 10, m1, jnp.where(row < 20, depth * m1, depth * m3)),
        jnp.where(top, m2, 0.0),
        jnp.where(top, m3, 0.0),
    )


def flux_factors(depth, m0, m1, m2, m3):
    rows = iota((16, depth.shape[1]), 0)
    root = jnp.sqrt(depth)
    factors = []
    for hx, hy in ((-m1, -m3), (m0 + m1, m2 + m3), (-m0, -m2)):
        centre = jnp.where(
            rows < 4,
            depth * hx,
            jnp.where(rows < 8, hx, jnp.where(rows < 12, hy, depth * hy)),
        )
        factors.append((centre, root * jnp.sqrt(hx * hx + hy * hy)))
    return factors


def lifted(lift, factors, sums, differences):
    parts = []
    for (centre, jump), added, taken in zip(factors, sums, differences):
        parts.append(centre * added)
        parts.append(jump * taken)
    return dot(lift, split_state(jnp.concatenate(parts, axis=0)))


def pick_columns(load, sources, block, lane, start):
    out = start
    for k in sources:
        found = jnp.take_along_axis(load(k), lane, axis=1)
        out = jnp.where(block == k, found, out)
    return out


def step_kernel(
    n_region,
    n_dom,
    elems,
    state_ref,
    depth_ref,
    metric_ref,
    diff_ref,
    stiff_ref,
    trace_ref,
    lift_ref,
    cluster_ref,
    code_ref,
    send_reg_ref,
    send_dom_ref,
    move_dom_ref,
    move_slot_ref,
    first_ref,
    second_ref,
    out_ref,
    *scratch,
):
    hbm_refs = (
        state_ref,
        depth_ref,
        metric_ref,
        diff_ref,
        stiff_ref,
        trace_ref,
        lift_ref,
        cluster_ref,
        code_ref,
        send_reg_ref,
        send_dom_ref,
        move_dom_ref,
        move_slot_ref,
        first_ref,
        second_ref,
    )
    step_body(
        n_region, n_dom, elems, hbm_refs, out_ref, scratch[: len(hbm_refs)], *scratch[len(hbm_refs) :]
    )


def step_body(
    n_region,
    n_dom,
    elems,
    hbm_refs,
    out_ref,
    local_refs,
    in_sem,
    ready,
    first_ops,
    second_ops,
    lift_ops,
    dense,
    base,
    geometry,
    tab_a,
    tab_b,
    tab_c,
    beyond,
    out_reg,
    out_dom,
    in_reg,
    in_dom,
    out_fine,
    in_fine,
    land_out,
    land_in,
    tile_out,
    tile_in,
    ss_reg,
    rs_reg,
    ss_dom,
    rs_dom,
    ss_fine,
    rs_fine,
    ss_land,
    rs_land,
    ss_tile,
    rs_tile,
):
    r = lax.axis_index("region")
    d = lax.axis_index("dom")
    blocks = elems // 128
    has_low = r > 0
    has_high = r < n_region - 1
    dom_low = d > 0
    dom_high = d < n_dom - 1
    sides = (
        (has_high, {"region": r + 1}, 1, 0),
        (has_low, {"region": r - 1}, 0, 1),
        (dom_high, {"dom": d + 1}, 1, 0),
        (dom_low, {"dom": d - 1}, 0, 1),
    )
    comes = (has_low, has_high, dom_low, dom_high)

    loads = [
        pltpu.make_async_copy(src, dst, in_sem.at[i])
        for i, (src, dst) in enumerate(zip(hbm_refs, local_refs))
    ]
    barrier = pltpu.get_barrier_semaphore()

    def ring(k):
        return {"dom": lax.rem(d + k + n_dom, n_dom)}

    for i in EARLY_LOADS:
        loads[i].start()
    for exists, device, _, _ in sides[:2]:

        @pl.when(exists)
        def _():
            pl.semaphore_signal(barrier, inc=1, device_id=device, device_id_type=MESH)

    for k in (1, -1):
        pl.semaphore_signal(barrier, inc=1, device_id=ring(k), device_id_type=MESH)
    for i in LATE_LOADS:
        loads[i].start()

    def announce(stage, reach):
        for k in (reach, -reach):
            pl.semaphore_signal(
                ready.at[stage], inc=1, device_id=ring(k), device_id_type=MESH
            )

    (
        state_ref,
        depth_ref,
        metric_ref,
        diff_ref,
        stiff_ref,
        trace_ref,
        lift_ref,
        cluster_ref,
        code_ref,
        send_reg_ref,
        send_dom_ref,
        move_dom_ref,
        move_slot_ref,
        first_ref,
        second_ref,
    ) = local_refs
    first_ops[...] = jnp.zeros((32, 16), F32)
    second_ops[...] = jnp.zeros((32, 16), F32)
    lift_ops[...] = jnp.zeros((16, 16), F32)
    for i in EARLY_LOADS:
        loads[i].wait()

    for a in range(2):
        first_ops[NODES * a : NODES * (a + 1), 0:NODES] = diff_ref[:, a, :]
    for f in range(3):
        first_ops[2 * NODES + 4 * f : 2 * NODES + 4 * f + 4, 0:NODES] = trace_ref[f]
    wide = dot(first_ref[192:384, 0:32], spread_columns(first_ops[...], first_ref)).astype(BF16)
    wide = wide * first_ref[0:192, 0:96]
    slope, traces = wide[0:96], wide[96:192]

    dense[30:32, :] = jnp.zeros((2, elems), F32)
    for v in range(3):
        dense[NODES * v : NODES * (v + 1), :] = state_ref[:, v, :]
    state = dense[...]
    depth = depth_ref[...]
    m0, m1, m2, m3 = (metric_ref[i : i + 1, :] for i in range(4))

    alpha = alpha_of(depth, m0, m1, m2, m3)

    def series_of(values, alpha):
        series = [values]
        for _ in range(3):
            series.append(combine(dot(slope, split_state(series[-1])), alpha))
        return series

    def integrate(series, factors):
        summed = factors[0] * series[0]
        for factor, member in zip(factors[1:], series[1:]):
            summed = summed + factor * member
        return summed

    series = series_of(state, alpha)
    early = integrate(series, FIRST_HALF)
    early_split = split_state(early)
    tab_a[0:48] = dot(traces[0:48], early_split)

    def source(table):
        def load(k):
            f, b = divmod(k, blocks)
            return table[16 * f : 16 * f + 16, 128 * b : 128 * b + 128]

        return load

    def spread(vector):
        return jnp.broadcast_to(vector, (16, 128))

    own = range(3 * blocks)

    odd = lax.rem(r, 2)
    far_low, near_low = odd == 0, odd == 1

    def gather_sends(which, table, copies):
        def regional_list(lane_row):
            for b in range(2):
                columns = slice(128 * b, 128 * b + 128)
                index = jnp.where(lane_row == 1, send_reg_ref[1:2, columns], send_reg_ref[0:1, columns])
                index = spread(index)
                out_reg[which, lane_row, b] = pick_columns(
                    source(table), own, index >> 7, index & 127, jnp.zeros((16, 128), F32)
                )

        def leave(i, condition):
            exists, _, copy = copies[i]
            pl.when(exists & condition)(copy.start)

        regional_list(odd)
        leave(1, far_low)
        leave(0, near_low)
        for i in (2, 3):
            exists, _, copy = copies[i]
            lane_row = sides[i][2]
            index = spread(send_dom_ref[lane_row : lane_row + 1, :])
            out_dom[which, lane_row] = pick_columns(
                source(table), own, index >> 7, index & 127, jnp.zeros((16, 128), F32)
            )
            pl.when(exists)(copy.start)
        regional_list(1 - odd)
        leave(0, far_low)
        leave(1, near_low)

    def copies_a(which):
        copies = []
        for i, (exists, device, lane_row, at) in enumerate(sides):
            regional = i < 2
            copies.append(
                (
                    exists,
                    comes[2 * (i // 2) + at],
                    pltpu.make_async_remote_copy(
                        src_ref=(out_reg if regional else out_dom).at[which, lane_row],
                        dst_ref=(in_reg if regional else in_dom).at[which, at],
                        send_sem=(ss_reg if regional else ss_dom).at[which],
                        recv_sem=(rs_reg if regional else rs_dom).at[which],
                        device_id=device,
                        device_id_type=MESH,
                    ),
                )
            )
        return copies

    def start(copies):
        for exists, _, copy in copies:
            pl.when(exists)(copy.start)

    def sizes(src, dst, ss, rs):
        return pltpu.make_async_remote_copy(
            src_ref=src,
            dst_ref=dst,
            send_sem=ss,
            recv_sem=rs,
            device_id=ring(1),
            device_id_type=MESH,
        )

    def either(condition, yes, no):
        pl.when(condition)(yes)
        pl.when(jnp.logical_not(condition))(no)

    inner = (has_low & has_high, dom_low & dom_high)

    def pairs_a(which):
        return [
            (sizes(src.at[which], dst.at[which], *sems), sizes(src.at[which, 0], dst.at[which, 0], *sems))
            for src, dst, sems in (
                (out_reg, in_reg, (ss_reg.at[which], rs_reg.at[which])),
                (out_dom, in_dom, (ss_dom.at[which], rs_dom.at[which])),
            )
        ]

    def wait_recv(pairs):
        for condition, (two, one) in zip(inner, pairs):
            either(condition, two.wait_recv, one.wait_recv)

    def wait_send(pairs):
        for condition, (two, one) in zip(inner, pairs):
            either(condition, two.wait_send, one.wait_send)

    first_copies = copies_a(0)
    late_copies = copies_a(1)
    first_pairs, late_pairs = pairs_a(0), pairs_a(1)
    pl.semaphore_wait(barrier, 2 + has_low.astype(jnp.int32) + has_high.astype(jnp.int32))
    announce(0, 1)
    gather_sends(0, tab_a, first_copies)

    later = integrate(series, SECOND_HALF)
    tab_b[...] = dot(traces[0:48], split_state(later))
    gather_sends(1, tab_b, late_copies)

    tile_in[d] = jnp.zeros((8, 128), F32)
    land_in[d] = jnp.full((1, 128), -1, jnp.int32)
    for i in range(2):

        @pl.when(jnp.logical_not(comes[i]))
        def _():
            in_reg[:, i] = jnp.zeros(in_reg.shape[0:1] + in_reg.shape[2:], F32)

        @pl.when(jnp.logical_not(comes[2 + i]))
        def _():
            in_dom[:, i] = jnp.zeros(in_dom.shape[0:1] + in_dom.shape[2:], F32)

    for i in range(4):

        @pl.when(jnp.logical_not(comes[i]))
        def _():
            in_fine[i] = jnp.zeros((8, 128), F32)

    for i in LATE_LOADS:
        loads[i].wait()
    tab_a[48:96] = dot(traces[48:96], early_split)
    for a in range(2):
        second_ops[NODES * a : NODES * (a + 1), 0:NODES] = stiff_ref[:, a, :]
    stiff = dot(first_ref[192:288, 0:32], spread_columns(second_ops[...], first_ref)).astype(BF16)
    stiff = -(stiff * first_ref[0:96, 0:96])
    for f in range(3):
        lift_ops[4 * f : 4 * f + 4, 0:NODES] = lift_ref[f]
    hi, lo = halves(lift_ops[...])
    nodes = second_ref[64:96, 0:16]
    lift = dot(dot_nt(nodes, hi).astype(BF16), second_ref[0:16])
    lift = lift + dot(dot_nt(nodes, lo).astype(BF16), second_ref[16:32])
    lift = lift.astype(BF16) * second_ref[32:64]
    factors = flux_factors(depth, m0, m1, m2, m3)
    mirror = jnp.where((iota((16, 128), 0) >= 4) & (iota((16, 128), 0) < 12), -1.0, 1.0)
    first_code = 3 * elems
    regional = 2 * send_reg_ref.shape[1]
    wall_code = first_code + regional + 2 * send_dom_ref.shape[1]
    remote = range(3 * blocks, 3 * blocks + 6)

    def code_of(f, b):
        return spread(code_ref[f : f + 1, 128 * b : 128 * b + 128])

    def local_part(table):
        for f in range(3):
            for b in range(blocks):
                code = code_of(f, b)
                wall = mirror * table[48 + 16 * f : 64 + 16 * f, 128 * b : 128 * b + 128]
                wall = jnp.where(code == wall_code, wall, 0.0)
                beyond[f, b] = pick_columns(source(table), own, code >> 7, code & 127, wall)

    def increment(values_split, table):
        volume = combine(dot(stiff, values_split), alpha)
        outside = [jnp.concatenate([beyond[f, b] for b in range(blocks)], axis=1) for f in range(3)]
        inside = [table[48 + 16 * f : 64 + 16 * f, :] for f in range(3)]
        return volume + lifted(
            lift,
            factors,
            [x + y for x, y in zip(outside, inside)],
            [x - y for x, y in zip(outside, inside)],
        )

    def fine_column(code):
        slot = code - first_code
        reg = slot & 255
        from_reg = jnp.where(
            (slot >= 0) & (slot < regional) & (reg < REG_FINE), (slot >> 8) * REG_FINE + reg, -1
        )
        past = slot - regional
        dom = past & 127
        return jnp.where(
            (past >= 0) & (past < 256) & (dom < DOM_FINE),
            2 * REG_FINE + (past >> 7) * DOM_FINE + dom,
            from_reg,
        )

    local_part(tab_a)
    base[...] = state + increment(early_split, tab_a)
    pl.semaphore_wait(ready.at[0], 2)
    announce(1, 2)

    def to_peers(src, dst, ss, rs):
        return [
            pltpu.make_async_remote_copy(
                src_ref=src.at[t],
                dst_ref=dst.at[d],
                send_sem=ss,
                recv_sem=rs,
                device_id={"dom": t},
                device_id_type=MESH,
            )
            for t in range(n_dom)
        ]

    others = pl.ds(0, n_dom - 1)
    land_copies = to_peers(land_out, land_in, ss_land, rs_land)
    land_all = sizes(land_out.at[others], land_in.at[others], ss_land, rs_land)
    tile_copies = to_peers(tile_out, tile_in, ss_tile, rs_tile.at[d // 4])
    tile_all = sizes(tile_out.at[others], tile_in.at[others], ss_tile, rs_tile.at[0])

    def within(t, reach):
        apart = lax.rem(t - d + n_dom, n_dom)
        return (apart != 0) & ((apart <= reach) | (apart >= n_dom - reach))

    lanes = iota((1, elems), 1)
    target = move_dom_ref[...]
    target = jnp.where(target == d, -1, target)
    fine_row = 15
    is_fine = cluster_ref[...] == 0
    kind = iota((16, elems), 0)
    chosen = jnp.where(kind == target, 1.0, 0.0)
    chosen = jnp.where(kind == fine_row, jnp.where(is_fine, 1.0, 0.0), chosen)
    before = jnp.where(iota((elems, elems), 0) < iota((elems, elems), 1), 1.0, 0.0).astype(BF16)
    ranks = dot(chosen.astype(BF16), before)
    rank = jnp.sum(jnp.where(kind < fine_row, chosen * ranks, 0.0), axis=0, keepdims=True)
    fine_rank = ranks[fine_row:].astype(jnp.int32)
    fine_position = jnp.where(is_fine, fine_rank, -1)
    slots = n_dom * MIGRANTS
    padded = 384 if slots <= 384 else 128 * (-(-slots // 128))
    position = jnp.where(target < 0, -1, target * MIGRANTS + rank.astype(jnp.int32))
    inverse = jnp.concatenate(
        [
            jnp.where(iota((padded, elems), 0) == position, 1.0, 0.0),
            jnp.where(iota((128, elems), 0) == fine_position, 1.0, 0.0),
        ],
        axis=0,
    ).astype(BF16)
    place = move_slot_ref[...]
    which_row = iota((8, elems), 0)
    facts = jnp.where(
        which_row == 0,
        lanes >> 1,
        jnp.where(
            which_row == 1, lanes & 1, jnp.where(which_row == 2, place >> 1, place & 1)
        ),
    )
    facts = jnp.where(which_row < 4, facts, 0).astype(F32).astype(BF16)
    found = dot_nt(facts, inverse).astype(jnp.int32)
    leaves = found[0:1] * 2 + found[1:2]
    lands = found[2:3] * 2 + found[3:4]
    fine_at = leaves[:, padded : padded + 128]
    for t in range(n_dom):
        row = jnp.broadcast_to(lands[:, 128 * (t // 4) : 128 * (t // 4) + 128], (8, 128))
        row = jnp.take_along_axis(row, (iota((8, 128), 1) & 31) + 32 * (t & 3), axis=1)
        land_out[t] = row[0:1]

    geometry[0:1] = depth
    geometry[1:5] = metric_ref[...]
    geometry[5:8] = code_ref[...].astype(F32)

    def squeeze(load, index):
        index = jnp.broadcast_to(index, (8, 128))
        return pick_columns(load, range(blocks), index >> 7, index & 127, jnp.zeros((8, 128), F32))

    def block_of(ref, g):
        return lambda b: ref[8 * g : 8 * g + 8, 128 * b : 128 * b + 128]

    fine_base = jnp.concatenate([squeeze(block_of(base, g), fine_at) for g in range(4)], axis=0)
    facts = squeeze(block_of(geometry, 0), fine_at)
    fine_geometry = [facts[i : i + 1] for i in range(5)]
    fine_alpha = alpha_of(*fine_geometry)
    fine_factors = flux_factors(*fine_geometry)
    fine_codes = [spread(facts[5 + f : 6 + f].astype(jnp.int32)) for f in range(3)]

    lane = iota((1, 128), 1)
    wanted = jnp.where(
        lane < REG_FINE,
        send_reg_ref[1:2, 0:128],
        jnp.where(
            lane < 2 * REG_FINE,
            pltpu.roll(send_reg_ref[0:1, 0:128], REG_FINE, 1),
            jnp.where(
                lane < 2 * REG_FINE + DOM_FINE,
                pltpu.roll(send_dom_ref[1:2, :], 2 * REG_FINE, 1),
                pltpu.roll(send_dom_ref[0:1, :], 2 * REG_FINE + DOM_FINE, 1),
            ),
        ),
    )
    wanted_face = (wanted >= elems).astype(jnp.int32) + (wanted >= 2 * elems).astype(jnp.int32)
    wanted_face = spread(wanted_face)
    rank_rows = jnp.broadcast_to(fine_rank.astype(F32), (8, elems))
    wanted_at = squeeze(
        lambda b: rank_rows[:, 128 * b : 128 * b + 128], wanted - elems * wanted_face[0:1]
    ).astype(jnp.int32)
    wanted_at = spread(wanted_at[0:1]) & 127

    wait_recv(first_pairs)

    def early_slot(k):
        k = k - 3 * blocks
        return in_reg[0, k // 2, k % 2] if k < 4 else in_dom[0, k - 4]

    outer = [
        pick_columns(early_slot, remote, code >> 7, code & 127, jnp.zeros((16, 128), F32))
        for code in fine_codes
    ]
    fine_midway = fine_base + lifted(lift, fine_factors, outer, outer)
    fine = integrate(series_of(fine_midway, fine_alpha), FIRST_HALF)
    fine_table = dot(traces[0:48], split_state(fine))

    block = jnp.zeros((16, 128), F32)
    for f in range(3):
        found = jnp.take_along_axis(fine_table[16 * f : 16 * f + 16], wanted_at, axis=1)
        block = jnp.where(wanted_face == f, found, block)
    lane8 = iota((8, 128), 1)
    block = jnp.where(lane8 < FINE_LANES, block[0:8], pltpu.roll(block[8:16], FINE_LANES, 1))
    out_fine[0] = block
    out_fine[1] = block
    fine_copies = []
    for i, (exists, device, _, at) in enumerate(sides):
        fine_copies.append(
            (
                exists,
                comes[2 * (i // 2) + at],
                pltpu.make_async_remote_copy(
                    src_ref=out_fine.at[at],
                    dst_ref=in_fine.at[i],
                    send_sem=ss_fine.at[i // 2],
                    recv_sem=rs_fine.at[i // 2],
                    device_id=device,
                    device_id_type=MESH,
                ),
            )
        )
    start(fine_copies)
    fine_pairs = [
        (
            sizes(out_fine, in_fine.at[pl.ds(2 * i, 2)], ss_fine.at[i], rs_fine.at[i]),
            sizes(out_fine.at[0], in_fine.at[2 * i], ss_fine.at[i], rs_fine.at[i]),
        )
        for i in range(2)
    ]
    pl.semaphore_wait(ready.at[1], 2)
    announce(2, 2)
    for t in range(n_dom):
        pl.when(within(t, 4))(land_copies[t].start)

    for b in range(blocks):
        columns = slice(128 * b, 128 * b + 128)
        index = jnp.broadcast_to(fine_rank[:, columns] & 127, (8, 128))
        mine = jnp.broadcast_to(cluster_ref[:, columns], (8, 128)) == 0
        for g in range(4):
            rows = slice(8 * g, 8 * g + 8)
            found = jnp.take_along_axis(fine[rows], index, axis=1)
            dense[rows, columns] = jnp.where(mine, found, later[rows, columns])
    second_split = split_state(dense[...])
    tab_c[...] = dot(traces, second_split)
    local_part(tab_c)
    wait_recv(late_pairs)

    lane16 = iota((16, 128), 1)
    both = []
    for k in range(6):
        first = early_slot(3 * blocks + k)
        if k < 4:
            coarse = in_reg[1, k // 2, k % 2]
            if k % 2 == 0:
                coarse = jnp.where(lane16 < REG_FINE, 0.0, coarse)
        else:
            coarse = jnp.where(lane16 < DOM_FINE, 0.0, in_dom[1, k - 4])
        both.append(first + coarse)
    columns = {}
    for f in range(3):
        for b in range(blocks):
            code = code_of(f, b)
            columns[f, b] = fine_column(code)
            beyond[f, b] = pick_columns(
                lambda k: both[k - 3 * blocks], remote, code >> 7, code & 127, beyond[f, b]
            )
    dense[...] = base[...] + increment(second_split, tab_c)

    quarters = range(padded // 128)
    at_of = [leaves[:, 128 * q : 128 * q + 128] for q in quarters]
    packed_base = {(g, q): squeeze(block_of(dense, g), at_of[q]) for q in quarters for g in range(4)}
    packed_facts = [squeeze(block_of(geometry, 0), at_of[q]) for q in quarters]
    packed_factors = flux_factors(
        *(jnp.concatenate([facts[i : i + 1] for facts in packed_facts], axis=1) for i in range(5))
    )
    packed_columns = {
        (f, q): fine_column(spread(packed_facts[q][5 + f : 6 + f].astype(jnp.int32)))
        for f in range(3)
        for q in quarters
    }
    pl.semaphore_wait(ready.at[2], 2)
    for t in range(n_dom):
        pl.when((t != d) & jnp.logical_not(within(t, 4)))(land_copies[t].start)
    wait_recv(fine_pairs)
    at = lane8 & (FINE_LANES - 1)

    def fine_block():
        return jnp.where(
            at < REG_FINE,
            in_fine[0],
            jnp.where(
                at < 2 * REG_FINE,
                in_fine[1],
                jnp.where(at < 2 * REG_FINE + DOM_FINE, in_fine[2], in_fine[3]),
            ),
        )

    def fine_outer(columns, count):
        fresh = fine_block()
        outer = []
        for f in range(3):
            late = []
            for b in range(count):
                column = columns[f, b][0:8] & (FINE_LANES - 1)
                low = jnp.take_along_axis(fresh, column, axis=1)
                high = jnp.take_along_axis(fresh, column + FINE_LANES, axis=1)
                found = jnp.concatenate([low, high], axis=0)
                late.append(jnp.where(columns[f, b] >= 0, found, 0.0))
            outer.append(jnp.concatenate(late, axis=1))
        return outer

    outer = fine_outer(packed_columns, len(quarters))
    share = lifted(lift, packed_factors, outer, outer)

    def cell(g, b):
        return dense[8 * g : 8 * g + 8, 128 * b : 128 * b + 128]

    group = iota((8, 128), 1) >> 5
    packed = {
        (g, q): packed_base[g, q] + share[8 * g : 8 * g + 8, 128 * q : 128 * q + 128]
        for q in quarters
        for g in range(4)
    }
    for t in range(n_dom):
        tile = jnp.zeros((8, 128), F32)
        for g in range(4):
            shift = (32 * (g - (t & 3))) % 128
            moved = packed[g, t // 4]
            if shift:
                moved = pltpu.roll(moved, shift, 1)
            tile = jnp.where(group == g, moved, tile)
        tile_out[t] = tile
        pl.when(t != d)(tile_copies[t].start)
    wait_send(first_pairs)
    wait_send(late_pairs)
    wait_send(fine_pairs)
    land_all.wait_send()
    tile_all.wait_send()
    outer = fine_outer(columns, blocks)
    dense[...] = dense[...] + lifted(lift, factors, outer, outer)
    land_all.wait_recv()
    kk = iota((1, 128), 1)
    stack = []
    for q in range(padded // 128):
        row_q = jnp.full((1, 128), -1, jnp.int32)
        for k in range(4 * q, min(4 * q + 4, n_dom)):
            row_q = jnp.where((kk >> 5) == (k & 3), land_in[k], row_q)
        stack.append(row_q)
    places = jnp.concatenate(stack, axis=1)
    comes_here = jnp.where(iota((elems, padded), 0) == places, 1.0, 0.0).astype(BF16)
    column = iota((8, padded), 1)
    row8 = iota((8, padded), 0)
    facts = jnp.where(row8 == 0, column >> 1, jnp.where(row8 == 1, column & 1, 1))
    found = dot_nt(facts.astype(F32).astype(BF16), comes_here).astype(jnp.int32)
    origin = jnp.where(found[2:3] > 0, found[0:1] * 2 + found[1:2], -1)

    result = {(g, b): cell(g, b) for g in range(4) for b in range(blocks)}
    for q in range(padded // 128):
        senders = range(4 * q, min(4 * q + 4, n_dom))
        if not senders:
            continue
        full, short = (
            sizes(tile_out.at[rows], tile_in.at[rows], ss_tile, rs_tile.at[q])
            for rows in (pl.ds(4 * q, len(senders)), pl.ds(4 * q, len(senders) - 1))
        )
        either(d // 4 == q, short.wait_recv, full.wait_recv)
        for g in range(4):
            rows = jnp.zeros((8, 128), F32)
            for t in senders:
                shift = (32 * ((t & 3) - g)) % 128
                moved = tile_in[t]
                if shift:
                    moved = pltpu.roll(moved, shift, 1)
                rows = jnp.where(group == (t & 3), moved, rows)
            for b in range(blocks):
                index = jnp.broadcast_to(origin[:, 128 * b : 128 * b + 128], (8, 128))
                found = jnp.take_along_axis(rows, index & 127, axis=1)
                result[g, b] = jnp.where((index >> 7) == q, found, result[g, b])
    for g in range(4):
        for b in range(blocks):
            dense[8 * g : 8 * g + 8, 128 * b : 128 * b + 128] = result[g, b]
    for v in range(3):
        out_ref[:, v, :] = dense[NODES * v : NODES * (v + 1), :]


def shards(n_region, n_dom, *args):
    (
        water_state,
        water_depth,
        metric,
        diff_ops,
        stiff_ops,
        trace_ops,
        lift_ops,
        cluster,
        face_code,
        send_region,
        send_dom,
        move_dom,
        move_slot,
    ) = args
    elems = water_state.shape[2]
    blocks = elems // 128
    vmem = pl.BlockSpec(memory_space=pltpu.VMEM)
    dma = pltpu.SemaphoreType.DMA

    def kernel(*refs):
        step_kernel(n_region, n_dom, elems, *refs)

    given = (
        jnp.transpose(water_state, (1, 0, 2)),
        water_depth.reshape(1, elems),
        metric,
        jnp.transpose(diff_ops, (1, 0, 2)),
        jnp.transpose(stiff_ops, (1, 0, 2)),
        trace_ops,
        jnp.transpose(lift_ops, (0, 2, 1)),
        cluster.reshape(1, elems),
        face_code,
        send_region,
        send_dom,
        move_dom.reshape(1, elems),
        move_slot.reshape(1, elems),
        *pattern(),
    )
    result = pl.pallas_call(
        kernel,
        out_shape=pltpu.VMEM((NODES, 3, elems), F32),
        in_specs=[pl.BlockSpec(memory_space=pl.ANY)] * len(given),
        out_specs=vmem,
        scratch_shapes=[pltpu.VMEM(x.shape, x.dtype) for x in given]
        + [
            dma((len(given),)),
            pltpu.SemaphoreType.REGULAR((3,)),
            pltpu.VMEM((32, 16), F32),
            pltpu.VMEM((32, 16), F32),
            pltpu.VMEM((16, 16), F32),
            pltpu.VMEM((32, elems), F32),
            pltpu.VMEM((32, elems), F32),
            pltpu.VMEM((8, elems), F32),
            pltpu.VMEM((96, elems), F32),
            pltpu.VMEM((48, elems), F32),
            pltpu.VMEM((96, elems), F32),
            pltpu.VMEM((3, blocks, 16, 128), F32),
            pltpu.VMEM((2, 2, 2, 16, 128), F32),
            pltpu.VMEM((2, 2, 16, 128), F32),
            pltpu.VMEM((2, 2, 2, 16, 128), F32),
            pltpu.VMEM((2, 2, 16, 128), F32),
            pltpu.VMEM((2, 8, 128), F32),
            pltpu.VMEM((4, 8, 128), F32),
            pltpu.VMEM((n_dom, 1, 128), jnp.int32),
            pltpu.VMEM((n_dom, 1, 128), jnp.int32),
            pltpu.VMEM((n_dom, 8, 128), F32),
            pltpu.VMEM((n_dom, 8, 128), F32),
            dma((2,)),
            dma((2,)),
            dma((2,)),
            dma((2,)),
            dma((2,)),
            dma((2,)),
            dma,
            dma,
            dma,
            dma((-(-n_dom // 4),)),
        ],
        compiler_params=pltpu.CompilerParams(collective_id=0, has_side_effects=True),
        name="wave_step",
    )(*given)
    return jnp.transpose(result, (1, 0, 2))


def solution(mesh):
    both = ("region", "dom")
    wide, flat = P(None, both), P(both)
    placed = (
        P(None, None, both),
        flat,
        wide,
        P(),
        P(),
        P(),
        P(),
        flat,
        wide,
        wide,
        wide,
        flat,
        flat,
    )
    n_region, n_dom = mesh.shape["region"], mesh.shape["dom"]

    def step(*args):
        return shards(n_region, n_dom, *args)

    return jax.shard_map(
        step,
        mesh=mesh,
        in_specs=placed,
        out_specs=P(None, None, both),
        check_vma=False,
    )
```

```python
import jax
import jax.numpy as jnp
import numpy as np
from jax import lax
from jax.experimental import pallas as pl
from jax.experimental.pallas import tpu as pltpu
from jax.sharding import PartitionSpec as P

MESH = pl.DeviceIdType.MESH
F32 = jnp.float32
BF16 = jnp.bfloat16
NODES = 10
FIRST_HALF = (0.5, 0.125, 1.0 / 48.0, 1.0 / 384.0)
SECOND_HALF = (0.5, 0.375, 7.0 / 48.0, 15.0 / 384.0)
MIGRANTS = 32
REG_FINE = 8
DOM_FINE = 4
FINE_LANES = 32
EARLY_LOADS = (3, 5, 13, 0, 1, 2, 9, 10)
LATE_LOADS = (4, 6, 7, 8, 11, 12, 14)


def iota(shape, dim):
    return lax.broadcasted_iota(jnp.int32, shape, dim)


def dot(a, b):
    return jnp.dot(a, b, preferred_element_type=F32)


def dot_nt(a, b):
    return lax.dot_general(a, b, (((1,), (1,)), ((), ())), preferred_element_type=F32)


def split_state(values):
    hi = values.astype(BF16)
    lo = (values - hi.astype(F32)).astype(BF16)
    return jnp.concatenate([hi, lo, hi], axis=0)


def pattern():
    pick = np.zeros((192, 32), np.float32)
    mask = np.zeros((192, 96), np.float32)
    columns = np.zeros((2, 16, 96), np.float32)
    for column in range(96):
        third, at = divmod(column, 32)
        if at < 3 * NODES:
            columns[third // 2, at % NODES, column] = 1.0

    def fill(row, source, var, sign):
        pick[row, source] = 1.0
        for third in range(3):
            first = 32 * third + NODES * var
            mask[row, first : first + NODES] = sign

    for which in range(2):
        for at in range(3 * NODES):
            node, part = at % NODES, at // NODES
            fill(32 * which + at, NODES * which + node, 1 if part == 0 else 0, -1.0)
        for node in range(NODES):
            fill(64 + 16 * which + node, NODES * which + node, 2, -1.0)
    for order in range(2):
        for face in range(3):
            for at in range(16):
                part, point = divmod(at, 4)
                source = 2 * NODES + 4 * face + (point if order else 3 - point)
                fill(96 + 48 * order + 16 * face + at, source, part % 3, 1.0)

    nodes = np.zeros((32, 16), np.float32)
    for row in range(3 * NODES):
        nodes[row, row % NODES] = 1.0
    places = np.zeros((2, 16, 288), np.float32)
    signs = np.zeros((32, 288), np.float32)
    for column in range(288):
        third, rest = divmod(column, 96)
        face, at = divmod(rest, 32)
        jump, at = divmod(at, 16)
        part, point = divmod(at, 4)
        places[third // 2, 4 * face + point, column] = 1.0
        for row in range(3 * NODES):
            var = row // NODES
            if jump:
                signs[row, column] = 1.0 if part == var else 0.0
            else:
                signs[row, column] = -1.0 if part in ((1, 2), (0,), (3,))[var] else 0.0
    first = np.zeros((416, 128), np.float32)
    first[0:192, 0:96] = mask
    first[192:384, 0:32] = pick
    first[384:416, 0:96] = columns.reshape(32, 96)
    second = np.zeros((96, 288), np.float32)
    second[0:32] = places.reshape(32, 288)
    second[32:64] = signs
    second[64:96, 0:16] = nodes
    return [jnp.asarray(x, BF16) for x in (first, second)]


def halves(values):
    hi = values.astype(BF16)
    return hi, (values - hi.astype(F32)).astype(BF16)


def spread_columns(values, first_ref):
    hi, lo = halves(values)
    return (
        dot(hi, first_ref[384:400, 0:96]) + dot(lo, first_ref[400:416, 0:96])
    ).astype(BF16)


def combine(slopes, alpha):
    a1, a2, a3, a4 = alpha
    both = a1 * slopes[0:32] + a2 * slopes[32:64]
    top = a3 * slopes[64:80] + a4 * slopes[80:96]
    return jnp.concatenate([both[0:16] + top, both[16:32]], axis=0)


def alpha_of(depth, m0, m1, m2, m3):
    row = iota((32, depth.shape[1]), 0)
    top = row[0:16] < NODES
    return (
        jnp.where(row < 10, m0, jnp.where(row < 20, depth * m0, depth * m2)),
        jnp.where(row < 10, m1, jnp.where(row < 20, depth * m1, depth * m3)),
        jnp.where(top, m2, 0.0),
        jnp.where(top, m3, 0.0),
    )


def flux_factors(depth, m0, m1, m2, m3):
    rows = iota((16, depth.shape[1]), 0)
    root = jnp.sqrt(depth)
    factors = []
    for hx, hy in ((-m1, -m3), (m0 + m1, m2 + m3), (-m0, -m2)):
        centre = jnp.where(
            rows < 4,
            depth * hx,
            jnp.where(rows < 8, hx, jnp.where(rows < 12, hy, depth * hy)),
        )
        factors.append((centre, root * jnp.sqrt(hx * hx + hy * hy)))
    return factors


def lifted(lift, factors, sums, differences):
    parts = []
    for (centre, jump), added, taken in zip(factors, sums, differences):
        parts.append(centre * added)
        parts.append(jump * taken)
    return dot(lift, split_state(jnp.concatenate(parts, axis=0)))


def pick_columns(load, sources, block, lane, start):
    out = start
    for k in sources:
        found = jnp.take_along_axis(load(k), lane, axis=1)
        out = jnp.where(block == k, found, out)
    return out


def step_kernel(
    n_region,
    n_dom,
    elems,
    state_ref,
    depth_ref,
    metric_ref,
    diff_ref,
    stiff_ref,
    trace_ref,
    lift_ref,
    cluster_ref,
    code_ref,
    send_reg_ref,
    send_dom_ref,
    move_dom_ref,
    move_slot_ref,
    first_ref,
    second_ref,
    out_ref,
    *scratch,
):
    hbm_refs = (
        state_ref,
        depth_ref,
        metric_ref,
        diff_ref,
        stiff_ref,
        trace_ref,
        lift_ref,
        cluster_ref,
        code_ref,
        send_reg_ref,
        send_dom_ref,
        move_dom_ref,
        move_slot_ref,
        first_ref,
        second_ref,
    )
    step_body(
        n_region, n_dom, elems, hbm_refs, out_ref, scratch[: len(hbm_refs)], *scratch[len(hbm_refs) :]
    )


def step_body(
    n_region,
    n_dom,
    elems,
    hbm_refs,
    out_ref,
    local_refs,
    in_sem,
    ready,
    first_ops,
    second_ops,
    lift_ops,
    dense,
    base,
    geometry,
    tab_a,
    tab_b,
    tab_c,
    beyond,
    out_reg,
    out_dom,
    in_reg,
    in_dom,
    out_fine,
    in_fine,
    land_out,
    land_in,
    tile_out,
    tile_in,
    ss_reg,
    rs_reg,
    ss_dom,
    rs_dom,
    ss_fine,
    rs_fine,
    ss_land,
    rs_land,
    ss_tile,
    rs_tile,
):
    r = lax.axis_index("region")
    d = lax.axis_index("dom")
    blocks = elems // 128
    has_low = r > 0
    has_high = r < n_region - 1
    dom_low = d > 0
    dom_high = d < n_dom - 1
    sides = (
        (has_high, {"region": r + 1}, 1, 0),
        (has_low, {"region": r - 1}, 0, 1),
        (dom_high, {"dom": d + 1}, 1, 0),
        (dom_low, {"dom": d - 1}, 0, 1),
    )
    comes = (has_low, has_high, dom_low, dom_high)

    loads = [
        pltpu.make_async_copy(src, dst, in_sem.at[i])
        for i, (src, dst) in enumerate(zip(hbm_refs, local_refs))
    ]
    barrier = pltpu.get_barrier_semaphore()

    def ring(k):
        return {"dom": lax.rem(d + k + n_dom, n_dom)}

    for exists, device, _, _ in sides[:2]:

        @pl.when(exists)
        def _():
            pl.semaphore_signal(barrier, inc=1, device_id=device, device_id_type=MESH)

    for k in (1, -1):
        pl.semaphore_signal(barrier, inc=1, device_id=ring(k), device_id_type=MESH)
    for i in EARLY_LOADS:
        loads[i].start()
    for i in LATE_LOADS:
        loads[i].start()

    def announce(stage, reach):
        for k in (reach, -reach):
            pl.semaphore_signal(
                ready.at[stage], inc=1, device_id=ring(k), device_id_type=MESH
            )

    (
        state_ref,
        depth_ref,
        metric_ref,
        diff_ref,
        stiff_ref,
        trace_ref,
        lift_ref,
        cluster_ref,
        code_ref,
        send_reg_ref,
        send_dom_ref,
        move_dom_ref,
        move_slot_ref,
        first_ref,
        second_ref,
    ) = local_refs
    first_ops[...] = jnp.zeros((32, 16), F32)
    second_ops[...] = jnp.zeros((32, 16), F32)
    lift_ops[...] = jnp.zeros((16, 16), F32)
    for i in EARLY_LOADS:
        loads[i].wait()

    for a in range(2):
        first_ops[NODES * a : NODES * (a + 1), 0:NODES] = diff_ref[:, a, :]
    for f in range(3):
        first_ops[2 * NODES + 4 * f : 2 * NODES + 4 * f + 4, 0:NODES] = trace_ref[f]
    wide = dot(first_ref[192:384, 0:32], spread_columns(first_ops[...], first_ref)).astype(BF16)
    wide = wide * first_ref[0:192, 0:96]
    slope, traces = wide[0:96], wide[96:192]

    dense[30:32, :] = jnp.zeros((2, elems), F32)
    for v in range(3):
        dense[NODES * v : NODES * (v + 1), :] = state_ref[:, v, :]
    state = dense[...]
    depth = depth_ref[...]
    m0, m1, m2, m3 = (metric_ref[i : i + 1, :] for i in range(4))

    alpha = alpha_of(depth, m0, m1, m2, m3)

    def series_of(values, alpha):
        series = [values]
        for _ in range(3):
            series.append(combine(dot(slope, split_state(series[-1])), alpha))
        return series

    def integrate(series, factors):
        summed = factors[0] * series[0]
        for factor, member in zip(factors[1:], series[1:]):
            summed = summed + factor * member
        return summed

    series = series_of(state, alpha)
    early = integrate(series, FIRST_HALF)
    early_split = split_state(early)
    tab_a[0:48] = dot(traces[0:48], early_split)

    def source(table):
        def load(k):
            f, b = divmod(k, blocks)
            return table[16 * f : 16 * f + 16, 128 * b : 128 * b + 128]

        return load

    def spread(vector):
        return jnp.broadcast_to(vector, (16, 128))

    own = range(3 * blocks)

    odd = lax.rem(r, 2)
    far_low, near_low = odd == 0, odd == 1

    def gather_sends(which, table, copies):
        def regional_list(lane_row):
            for b in range(2):
                columns = slice(128 * b, 128 * b + 128)
                index = jnp.where(lane_row == 1, send_reg_ref[1:2, columns], send_reg_ref[0:1, columns])
                index = spread(index)
                out_reg[which, lane_row, b] = pick_columns(
                    source(table), own, index >> 7, index & 127, jnp.zeros((16, 128), F32)
                )

        def leave(i, condition):
            exists, _, copy = copies[i]
            pl.when(exists & condition)(copy.start)

        regional_list(odd)
        leave(1, far_low)
        leave(0, near_low)
        for i in (2, 3):
            exists, _, copy = copies[i]
            lane_row = sides[i][2]
            index = spread(send_dom_ref[lane_row : lane_row + 1, :])
            out_dom[which, lane_row] = pick_columns(
                source(table), own, index >> 7, index & 127, jnp.zeros((16, 128), F32)
            )
            pl.when(exists)(copy.start)
        regional_list(1 - odd)
        leave(0, far_low)
        leave(1, near_low)

    def copies_a(which):
        copies = []
        for i, (exists, device, lane_row, at) in enumerate(sides):
            regional = i < 2
            copies.append(
                (
                    exists,
                    comes[2 * (i // 2) + at],
                    pltpu.make_async_remote_copy(
                        src_ref=(out_reg if regional else out_dom).at[which, lane_row],
                        dst_ref=(in_reg if regional else in_dom).at[which, at],
                        send_sem=(ss_reg if regional else ss_dom).at[which],
                        recv_sem=(rs_reg if regional else rs_dom).at[which],
                        device_id=device,
                        device_id_type=MESH,
                    ),
                )
            )
        return copies

    def start(copies):
        for exists, _, copy in copies:
            pl.when(exists)(copy.start)

    def sizes(src, dst, ss, rs):
        return pltpu.make_async_remote_copy(
            src_ref=src,
            dst_ref=dst,
            send_sem=ss,
            recv_sem=rs,
            device_id=ring(1),
            device_id_type=MESH,
        )

    def either(condition, yes, no):
        pl.when(condition)(yes)
        pl.when(jnp.logical_not(condition))(no)

    inner = (has_low & has_high, dom_low & dom_high)

    def pairs_a(which):
        return [
            (sizes(src.at[which], dst.at[which], *sems), sizes(src.at[which, 0], dst.at[which, 0], *sems))
            for src, dst, sems in (
                (out_reg, in_reg, (ss_reg.at[which], rs_reg.at[which])),
                (out_dom, in_dom, (ss_dom.at[which], rs_dom.at[which])),
            )
        ]

    def wait_recv(pairs):
        for condition, (two, one) in zip(inner, pairs):
            either(condition, two.wait_recv, one.wait_recv)

    def wait_send(pairs):
        for condition, (two, one) in zip(inner, pairs):
            either(condition, two.wait_send, one.wait_send)

    first_copies = copies_a(0)
    late_copies = copies_a(1)
    first_pairs, late_pairs = pairs_a(0), pairs_a(1)
    pl.semaphore_wait(barrier, 2 + has_low.astype(jnp.int32) + has_high.astype(jnp.int32))
    announce(0, 1)
    gather_sends(0, tab_a, first_copies)

    later = integrate(series, SECOND_HALF)
    tab_b[...] = dot(traces[0:48], split_state(later))
    gather_sends(1, tab_b, late_copies)

    tile_in[d] = jnp.zeros((8, 128), F32)
    land_in[d] = jnp.full((1, 128), -1, jnp.int32)
    for i in range(2):

        @pl.when(jnp.logical_not(comes[i]))
        def _():
            in_reg[:, i] = jnp.zeros(in_reg.shape[0:1] + in_reg.shape[2:], F32)

        @pl.when(jnp.logical_not(comes[2 + i]))
        def _():
            in_dom[:, i] = jnp.zeros(in_dom.shape[0:1] + in_dom.shape[2:], F32)

    for i in range(4):

        @pl.when(jnp.logical_not(comes[i]))
        def _():
            in_fine[i] = jnp.zeros((8, 128), F32)

    for i in LATE_LOADS:
        loads[i].wait()
    tab_a[48:96] = dot(traces[48:96], early_split)
    for a in range(2):
        second_ops[NODES * a : NODES * (a + 1), 0:NODES] = stiff_ref[:, a, :]
    stiff = dot(first_ref[192:288, 0:32], spread_columns(second_ops[...], first_ref)).astype(BF16)
    stiff = -(stiff * first_ref[0:96, 0:96])
    for f in range(3):
        lift_ops[4 * f : 4 * f + 4, 0:NODES] = lift_ref[f]
    hi, lo = halves(lift_ops[...])
    nodes = second_ref[64:96, 0:16]
    lift = dot(dot_nt(nodes, hi).astype(BF16), second_ref[0:16])
    lift = lift + dot(dot_nt(nodes, lo).astype(BF16), second_ref[16:32])
    lift = lift.astype(BF16) * second_ref[32:64]
    factors = flux_factors(depth, m0, m1, m2, m3)
    mirror = jnp.where((iota((16, 128), 0) >= 4) & (iota((16, 128), 0) < 12), -1.0, 1.0)
    first_code = 3 * elems
    regional = 2 * send_reg_ref.shape[1]
    wall_code = first_code + regional + 2 * send_dom_ref.shape[1]
    remote = range(3 * blocks, 3 * blocks + 6)

    def code_of(f, b):
        return spread(code_ref[f : f + 1, 128 * b : 128 * b + 128])

    def local_part(table):
        for f in range(3):
            for b in range(blocks):
                code = code_of(f, b)
                wall = mirror * table[48 + 16 * f : 64 + 16 * f, 128 * b : 128 * b + 128]
                wall = jnp.where(code == wall_code, wall, 0.0)
                beyond[f, b] = pick_columns(source(table), own, code >> 7, code & 127, wall)

    def increment(values_split, table):
        volume = combine(dot(stiff, values_split), alpha)
        outside = [jnp.concatenate([beyond[f, b] for b in range(blocks)], axis=1) for f in range(3)]
        inside = [table[48 + 16 * f : 64 + 16 * f, :] for f in range(3)]
        return volume + lifted(
            lift,
            factors,
            [x + y for x, y in zip(outside, inside)],
            [x - y for x, y in zip(outside, inside)],
        )

    def fine_column(code):
        slot = code - first_code
        reg = slot & 255
        from_reg = jnp.where(
            (slot >= 0) & (slot < regional) & (reg < REG_FINE), (slot >> 8) * REG_FINE + reg, -1
        )
        past = slot - regional
        dom = past & 127
        return jnp.where(
            (past >= 0) & (past < 256) & (dom < DOM_FINE),
            2 * REG_FINE + (past >> 7) * DOM_FINE + dom,
            from_reg,
        )

    local_part(tab_a)
    base[...] = state + increment(early_split, tab_a)
    pl.semaphore_wait(ready.at[0], 2)
    announce(1, 2)

    def to_peers(src, dst, ss, rs):
        return [
            pltpu.make_async_remote_copy(
                src_ref=src.at[t],
                dst_ref=dst.at[d],
                send_sem=ss,
                recv_sem=rs,
                device_id={"dom": t},
                device_id_type=MESH,
            )
            for t in range(n_dom)
        ]

    others = pl.ds(0, n_dom - 1)
    land_copies = to_peers(land_out, land_in, ss_land, rs_land)
    land_all = sizes(land_out.at[others], land_in.at[others], ss_land, rs_land)
    tile_copies = to_peers(tile_out, tile_in, ss_tile, rs_tile.at[d // 4])
    tile_all = sizes(tile_out.at[others], tile_in.at[others], ss_tile, rs_tile.at[0])

    def within(t, reach):
        apart = lax.rem(t - d + n_dom, n_dom)
        return (apart != 0) & ((apart <= reach) | (apart >= n_dom - reach))

    lanes = iota((1, elems), 1)
    target = move_dom_ref[...]
    target = jnp.where(target == d, -1, target)
    fine_row = 15
    is_fine = cluster_ref[...] == 0
    kind = iota((16, elems), 0)
    chosen = jnp.where(kind == target, 1.0, 0.0)
    chosen = jnp.where(kind == fine_row, jnp.where(is_fine, 1.0, 0.0), chosen)
    before = jnp.where(iota((elems, elems), 0) < iota((elems, elems), 1), 1.0, 0.0).astype(BF16)
    ranks = dot(chosen.astype(BF16), before)
    rank = jnp.sum(jnp.where(kind < fine_row, chosen * ranks, 0.0), axis=0, keepdims=True)
    fine_rank = ranks[fine_row:].astype(jnp.int32)
    fine_position = jnp.where(is_fine, fine_rank, -1)
    slots = n_dom * MIGRANTS
    padded = 384 if slots <= 384 else 128 * (-(-slots // 128))
    position = jnp.where(target < 0, -1, target * MIGRANTS + rank.astype(jnp.int32))
    inverse = jnp.concatenate(
        [
            jnp.where(iota((padded, elems), 0) == position, 1.0, 0.0),
            jnp.where(iota((128, elems), 0) == fine_position, 1.0, 0.0),
        ],
        axis=0,
    ).astype(BF16)
    place = move_slot_ref[...]
    which_row = iota((8, elems), 0)
    facts = jnp.where(
        which_row == 0,
        lanes >> 1,
        jnp.where(
            which_row == 1, lanes & 1, jnp.where(which_row == 2, place >> 1, place & 1)
        ),
    )
    facts = jnp.where(which_row < 4, facts, 0).astype(F32).astype(BF16)
    found = dot_nt(facts, inverse).astype(jnp.int32)
    leaves = found[0:1] * 2 + found[1:2]
    lands = found[2:3] * 2 + found[3:4]
    fine_at = leaves[:, padded : padded + 128]
    for t in range(n_dom):
        row = jnp.broadcast_to(lands[:, 128 * (t // 4) : 128 * (t // 4) + 128], (8, 128))
        row = jnp.take_along_axis(row, (iota((8, 128), 1) & 31) + 32 * (t & 3), axis=1)
        land_out[t] = row[0:1]

    geometry[0:1] = depth
    geometry[1:5] = metric_ref[...]
    geometry[5:8] = code_ref[...].astype(F32)

    def squeeze(load, index):
        index = jnp.broadcast_to(index, (8, 128))
        return pick_columns(load, range(blocks), index >> 7, index & 127, jnp.zeros((8, 128), F32))

    def block_of(ref, g):
        return lambda b: ref[8 * g : 8 * g + 8, 128 * b : 128 * b + 128]

    fine_base = jnp.concatenate([squeeze(block_of(base, g), fine_at) for g in range(4)], axis=0)
    facts = squeeze(block_of(geometry, 0), fine_at)
    fine_geometry = [facts[i : i + 1] for i in range(5)]
    fine_alpha = alpha_of(*fine_geometry)
    fine_factors = flux_factors(*fine_geometry)
    fine_codes = [spread(facts[5 + f : 6 + f].astype(jnp.int32)) for f in range(3)]

    lane = iota((1, 128), 1)
    wanted = jnp.where(
        lane < REG_FINE,
        send_reg_ref[1:2, 0:128],
        jnp.where(
            lane < 2 * REG_FINE,
            pltpu.roll(send_reg_ref[0:1, 0:128], REG_FINE, 1),
            jnp.where(
                lane < 2 * REG_FINE + DOM_FINE,
                pltpu.roll(send_dom_ref[1:2, :], 2 * REG_FINE, 1),
                pltpu.roll(send_dom_ref[0:1, :], 2 * REG_FINE + DOM_FINE, 1),
            ),
        ),
    )
    wanted_face = (wanted >= elems).astype(jnp.int32) + (wanted >= 2 * elems).astype(jnp.int32)
    wanted_face = spread(wanted_face)
    rank_rows = jnp.broadcast_to(fine_rank.astype(F32), (8, elems))
    wanted_at = squeeze(
        lambda b: rank_rows[:, 128 * b : 128 * b + 128], wanted - elems * wanted_face[0:1]
    ).astype(jnp.int32)
    wanted_at = spread(wanted_at[0:1]) & 127

    wait_recv(first_pairs)

    def early_slot(k):
        k = k - 3 * blocks
        return in_reg[0, k // 2, k % 2] if k < 4 else in_dom[0, k - 4]

    outer = [
        pick_columns(early_slot, remote, code >> 7, code & 127, jnp.zeros((16, 128), F32))
        for code in fine_codes
    ]
    fine_midway = fine_base + lifted(lift, fine_factors, outer, outer)
    fine = integrate(series_of(fine_midway, fine_alpha), FIRST_HALF)
    fine_table = dot(traces[0:48], split_state(fine))

    block = jnp.zeros((16, 128), F32)
    for f in range(3):
        found = jnp.take_along_axis(fine_table[16 * f : 16 * f + 16], wanted_at, axis=1)
        block = jnp.where(wanted_face == f, found, block)
    lane8 = iota((8, 128), 1)
    block = jnp.where(lane8 < FINE_LANES, block[0:8], pltpu.roll(block[8:16], FINE_LANES, 1))
    out_fine[0] = block
    out_fine[1] = block
    fine_copies = []
    for i, (exists, device, _, at) in enumerate(sides):
        fine_copies.append(
            (
                exists,
                comes[2 * (i // 2) + at],
                pltpu.make_async_remote_copy(
                    src_ref=out_fine.at[at],
                    dst_ref=in_fine.at[i],
                    send_sem=ss_fine.at[i // 2],
                    recv_sem=rs_fine.at[i // 2],
                    device_id=device,
                    device_id_type=MESH,
                ),
            )
        )
    start(fine_copies)
    fine_pairs = [
        (
            sizes(out_fine, in_fine.at[pl.ds(2 * i, 2)], ss_fine.at[i], rs_fine.at[i]),
            sizes(out_fine.at[0], in_fine.at[2 * i], ss_fine.at[i], rs_fine.at[i]),
        )
        for i in range(2)
    ]
    pl.semaphore_wait(ready.at[1], 2)
    announce(2, 2)
    for t in range(n_dom):
        pl.when(within(t, 4))(land_copies[t].start)

    for b in range(blocks):
        columns = slice(128 * b, 128 * b + 128)
        index = jnp.broadcast_to(fine_rank[:, columns] & 127, (8, 128))
        mine = jnp.broadcast_to(cluster_ref[:, columns], (8, 128)) == 0
        for g in range(4):
            rows = slice(8 * g, 8 * g + 8)
            found = jnp.take_along_axis(fine[rows], index, axis=1)
            dense[rows, columns] = jnp.where(mine, found, later[rows, columns])
    second_split = split_state(dense[...])
    tab_c[...] = dot(traces, second_split)
    local_part(tab_c)
    wait_recv(late_pairs)

    lane16 = iota((16, 128), 1)
    both = []
    for k in range(6):
        first = early_slot(3 * blocks + k)
        if k < 4:
            coarse = in_reg[1, k // 2, k % 2]
            if k % 2 == 0:
                coarse = jnp.where(lane16 < REG_FINE, 0.0, coarse)
        else:
            coarse = jnp.where(lane16 < DOM_FINE, 0.0, in_dom[1, k - 4])
        both.append(first + coarse)
    columns = {}
    for f in range(3):
        for b in range(blocks):
            code = code_of(f, b)
            columns[f, b] = fine_column(code)
            beyond[f, b] = pick_columns(
                lambda k: both[k - 3 * blocks], remote, code >> 7, code & 127, beyond[f, b]
            )
    dense[...] = base[...] + increment(second_split, tab_c)

    quarters = range(padded // 128)
    at_of = [leaves[:, 128 * q : 128 * q + 128] for q in quarters]
    packed_base = {(g, q): squeeze(block_of(dense, g), at_of[q]) for q in quarters for g in range(4)}
    packed_facts = [squeeze(block_of(geometry, 0), at_of[q]) for q in quarters]
    packed_factors = flux_factors(
        *(jnp.concatenate([facts[i : i + 1] for facts in packed_facts], axis=1) for i in range(5))
    )
    packed_columns = {
        (f, q): fine_column(spread(packed_facts[q][5 + f : 6 + f].astype(jnp.int32)))
        for f in range(3)
        for q in quarters
    }
    pl.semaphore_wait(ready.at[2], 2)
    for t in range(n_dom):
        pl.when((t != d) & jnp.logical_not(within(t, 4)))(land_copies[t].start)
    wait_recv(fine_pairs)
    at = lane8 & (FINE_LANES - 1)

    def fine_block():
        return jnp.where(
            at < REG_FINE,
            in_fine[0],
            jnp.where(
                at < 2 * REG_FINE,
                in_fine[1],
                jnp.where(at < 2 * REG_FINE + DOM_FINE, in_fine[2], in_fine[3]),
            ),
        )

    def fine_outer(columns, count):
        fresh = fine_block()
        outer = []
        for f in range(3):
            late = []
            for b in range(count):
                column = columns[f, b][0:8] & (FINE_LANES - 1)
                low = jnp.take_along_axis(fresh, column, axis=1)
                high = jnp.take_along_axis(fresh, column + FINE_LANES, axis=1)
                found = jnp.concatenate([low, high], axis=0)
                late.append(jnp.where(columns[f, b] >= 0, found, 0.0))
            outer.append(jnp.concatenate(late, axis=1))
        return outer

    outer = fine_outer(packed_columns, len(quarters))
    share = lifted(lift, packed_factors, outer, outer)

    def cell(g, b):
        return dense[8 * g : 8 * g + 8, 128 * b : 128 * b + 128]

    group = iota((8, 128), 1) >> 5
    packed = {
        (g, q): packed_base[g, q] + share[8 * g : 8 * g + 8, 128 * q : 128 * q + 128]
        for q in quarters
        for g in range(4)
    }
    for t in range(n_dom):
        tile = jnp.zeros((8, 128), F32)
        for g in range(4):
            shift = (32 * (g - (t & 3))) % 128
            moved = packed[g, t // 4]
            if shift:
                moved = pltpu.roll(moved, shift, 1)
            tile = jnp.where(group == g, moved, tile)
        tile_out[t] = tile
        pl.when(t != d)(tile_copies[t].start)
    wait_send(first_pairs)
    wait_send(late_pairs)
    wait_send(fine_pairs)
    land_all.wait_send()
    tile_all.wait_send()
    outer = fine_outer(columns, blocks)
    dense[...] = dense[...] + lifted(lift, factors, outer, outer)
    land_all.wait_recv()
    kk = iota((1, 128), 1)
    stack = []
    for q in range(padded // 128):
        row_q = jnp.full((1, 128), -1, jnp.int32)
        for k in range(4 * q, min(4 * q + 4, n_dom)):
            row_q = jnp.where((kk >> 5) == (k & 3), land_in[k], row_q)
        stack.append(row_q)
    places = jnp.concatenate(stack, axis=1)
    comes_here = jnp.where(iota((elems, padded), 0) == places, 1.0, 0.0).astype(BF16)
    column = iota((8, padded), 1)
    row8 = iota((8, padded), 0)
    facts = jnp.where(row8 == 0, column >> 1, jnp.where(row8 == 1, column & 1, 1))
    found = dot_nt(facts.astype(F32).astype(BF16), comes_here).astype(jnp.int32)
    origin = jnp.where(found[2:3] > 0, found[0:1] * 2 + found[1:2], -1)

    result = {(g, b): cell(g, b) for g in range(4) for b in range(blocks)}
    for q in range(padded // 128):
        senders = range(4 * q, min(4 * q + 4, n_dom))
        if not senders:
            continue
        full, short = (
            sizes(tile_out.at[rows], tile_in.at[rows], ss_tile, rs_tile.at[q])
            for rows in (pl.ds(4 * q, len(senders)), pl.ds(4 * q, len(senders) - 1))
        )
        either(d // 4 == q, short.wait_recv, full.wait_recv)
        for g in range(4):
            rows = jnp.zeros((8, 128), F32)
            for t in senders:
                shift = (32 * ((t & 3) - g)) % 128
                moved = tile_in[t]
                if shift:
                    moved = pltpu.roll(moved, shift, 1)
                rows = jnp.where(group == (t & 3), moved, rows)
            for b in range(blocks):
                index = jnp.broadcast_to(origin[:, 128 * b : 128 * b + 128], (8, 128))
                found = jnp.take_along_axis(rows, index & 127, axis=1)
                result[g, b] = jnp.where((index >> 7) == q, found, result[g, b])
    for g in range(4):
        for b in range(blocks):
            dense[8 * g : 8 * g + 8, 128 * b : 128 * b + 128] = result[g, b]
    for v in range(3):
        out_ref[:, v, :] = dense[NODES * v : NODES * (v + 1), :]


def shards(n_region, n_dom, *args):
    (
        water_state,
        water_depth,
        metric,
        diff_ops,
        stiff_ops,
        trace_ops,
        lift_ops,
        cluster,
        face_code,
        send_region,
        send_dom,
        move_dom,
        move_slot,
    ) = args
    elems = water_state.shape[2]
    blocks = elems // 128
    vmem = pl.BlockSpec(memory_space=pltpu.VMEM)
    dma = pltpu.SemaphoreType.DMA

    def kernel(*refs):
        step_kernel(n_region, n_dom, elems, *refs)

    given = (
        jnp.transpose(water_state, (1, 0, 2)),
        water_depth.reshape(1, elems),
        metric,
        jnp.transpose(diff_ops, (1, 0, 2)),
        jnp.transpose(stiff_ops, (1, 0, 2)),
        trace_ops,
        jnp.transpose(lift_ops, (0, 2, 1)),
        cluster.reshape(1, elems),
        face_code,
        send_region,
        send_dom,
        move_dom.reshape(1, elems),
        move_slot.reshape(1, elems),
        *pattern(),
    )
    result = pl.pallas_call(
        kernel,
        out_shape=pltpu.VMEM((NODES, 3, elems), F32),
        in_specs=[pl.BlockSpec(memory_space=pl.ANY)] * len(given),
        out_specs=vmem,
        scratch_shapes=[pltpu.VMEM(x.shape, x.dtype) for x in given]
        + [
            dma((len(given),)),
            pltpu.SemaphoreType.REGULAR((3,)),
            pltpu.VMEM((32, 16), F32),
            pltpu.VMEM((32, 16), F32),
            pltpu.VMEM((16, 16), F32),
            pltpu.VMEM((32, elems), F32),
            pltpu.VMEM((32, elems), F32),
            pltpu.VMEM((8, elems), F32),
            pltpu.VMEM((96, elems), F32),
            pltpu.VMEM((48, elems), F32),
            pltpu.VMEM((96, elems), F32),
            pltpu.VMEM((3, blocks, 16, 128), F32),
            pltpu.VMEM((2, 2, 2, 16, 128), F32),
            pltpu.VMEM((2, 2, 16, 128), F32),
            pltpu.VMEM((2, 2, 2, 16, 128), F32),
            pltpu.VMEM((2, 2, 16, 128), F32),
            pltpu.VMEM((2, 8, 128), F32),
            pltpu.VMEM((4, 8, 128), F32),
            pltpu.VMEM((n_dom, 1, 128), jnp.int32),
            pltpu.VMEM((n_dom, 1, 128), jnp.int32),
            pltpu.VMEM((n_dom, 8, 128), F32),
            pltpu.VMEM((n_dom, 8, 128), F32),
            dma((2,)),
            dma((2,)),
            dma((2,)),
            dma((2,)),
            dma((2,)),
            dma((2,)),
            dma,
            dma,
            dma,
            dma((-(-n_dom // 4),)),
        ],
        compiler_params=pltpu.CompilerParams(collective_id=0, has_side_effects=True),
        name="wave_step",
    )(*given)
    return jnp.transpose(result, (1, 0, 2))


def solution(mesh):
    both = ("region", "dom")
    wide, flat = P(None, both), P(both)
    placed = (
        P(None, None, both),
        flat,
        wide,
        P(),
        P(),
        P(),
        P(),
        flat,
        wide,
        wide,
        wide,
        flat,
        flat,
    )
    n_region, n_dom = mesh.shape["region"], mesh.shape["dom"]

    def step(*args):
        return shards(n_region, n_dom, *args)

    return jax.shard_map(
        step,
        mesh=mesh,
        in_specs=placed,
        out_specs=P(None, None, both),
        check_vma=False,
    )
```
